32 devices in a mesh: dp: 16 (over z, y, core), mp: 2 (over x).
Axes of the slice: x: 2, y: 2, z: 4, core: 2. Of those that a mesh axis runs over, the one named last changes fastest.
Arguments:
- inputs: bfloat16 [8192, 2048], P('dp', 'mp'), may hold values from -6 to 6
- grad_moved: bfloat16 [8192, 2048], P('dp', 'mp'), may hold values from -6 to 6
- moved: int32 [16, 4], P('dp'), may hold values from 0 to 1, as said below
- segments: int32 [8192], P('dp'), may hold values from 0 to 511, as said below
- input_norm_gain: float32 [2048], replicated, may hold values from 0.5 to 1.5
- proj_in: bfloat16 [2048, 3072], P(None, 'mp'), may hold values from -0.125 to 0.125
- proj_out: bfloat16 [1024, 2048], P('mp'), may hold values from -0.1875 to 0.1875
Outputs:
- input_gradient: bfloat16 [8192, 2048], P('dp', 'mp')
- grad_proj_in: float32 [2048, 3072], P('dp', 'mp')
- grad_proj_out: float32 [1024, 2048], P('mp', 'dp')
The draws below stay inside these ranges and needn't reach their ends.
Inputs may be any that keep to these rules, and one draw needn't show every extreme that they name: moved[g] equals moved[g XOR (8)] for every group g: blocks are swapped between partner groups slot for slot. `segments`: within each group of 512 rows the history numbers start at 0 on its first row, never fall and rise by at most one from row to row; histories never cross groups; in some group every event is a history of its own.
All inputs are finite; a program needn't handle non-finite values.
Results may differ from the reference program's by a relative error of at most 0.011.
Values may be sent and summed in bfloat16 or wider, within the bound.
A program may use at most 128 MiB of HBM per device.

```python
import jax
import jax.numpy as jnp
from jax import lax

D = 2048
HEADS = 8
DV = 128
DQK = 64
BLOCK = 128
ROWS_DEV = 512
TOKENS = 8192
NBLK = 4
HPD = 4
N_DP = 16
N_MP = 2


def draw_moved(key, part):
    half = TOKENS // ROWS_DEV // 2
    flags = jax.random.randint(jax.random.fold_in(key, 11), (half, NBLK), 0, 2).astype(jnp.int32)
    return jnp.concatenate([flags, flags], axis=0)


def draw_segments(key, part):
    groups = TOKENS // ROWS_DEV
    level = jax.random.randint(jax.random.fold_in(key, 21), (groups, 1), 0, 6)
    picks = jax.random.randint(jax.random.fold_in(key, 22), (groups, ROWS_DEV), 0, 1024)
    special = jax.random.randint(jax.random.fold_in(key, 23), (), 0, groups)
    starts = picks < jnp.right_shift(256, level)
    order = jnp.arange(ROWS_DEV, dtype=jnp.int32)[None, :]
    which = jnp.arange(groups, dtype=jnp.int32)[:, None]
    starts = jnp.where(order == 0, True, starts)
    starts = jnp.where(which == special, True, starts).astype(jnp.int32)
    ident = jnp.cumsum(starts, axis=1) - 1
    return ident.reshape(TOKENS).astype(jnp.int32)


def strengthened(drawn, own_key, source, target, shards_of, factor):
    owner, partner = [(jnp.arange(drawn.shape[dim]) // (drawn.shape[dim] // shards_of)).reshape([-1 if axis == dim else 1 for axis in range(drawn.ndim)]) for dim in (source, target)]
    chosen = jax.random.permutation(own_key, shards_of)[partner]
    strong = (owner == chosen) | (owner == (partner + shards_of // 2) % shards_of)
    return jnp.where(strong, factor * drawn, drawn)


def block_scale(own_key, shape, shards, low, top_value):
    factor_of, own = 1.0, jax.random.fold_in(own_key, 6)
    for dim, shards_of in shards:
        steps = jnp.exp(jax.random.uniform(jax.random.fold_in(own, dim), (shards_of,), jnp.float32, low / len(shards), top_value / len(shards)))
        factor_of = factor_of * jnp.repeat(steps, shape[dim] // shards_of).reshape([-1 if axis == dim else 1 for axis in range(len(shape))])
    return factor_of


def noise(stream_key, dims, deviation, bound, pieces=(), held_as=jnp.bfloat16):
    array = deviation * jax.random.normal(stream_key, dims, jnp.float32)
    if pieces:
        array = array * block_scale(stream_key, dims, pieces, -0.22, 0.18)
    return jnp.clip(array, -bound, bound).astype(held_as)


def gaussian_with(stream_key, shape, spread, bound, shards, heavy, kind=jnp.bfloat16):
    values = spread * jax.random.normal(stream_key, shape, jnp.float32)
    if shards:
        values = values * block_scale(stream_key, shape, shards, -0.22, 0.18)
    return jnp.clip(strengthened(values, jax.random.fold_in(stream_key, 3), *heavy), -bound, bound).astype(kind)


def setup_inputs(seed: int = 0) -> dict:
    splits = jax.random.split(jax.random.key(seed), 8)
    return {
        "inputs": gaussian_with(splits[0], (TOKENS, D), 1.0, 6.0, ((0, 16), (1, 2)), (0, 1, 16, 2.0)),
        "grad_moved": gaussian_with(splits[1], (TOKENS, D), 1.0, 6.0, ((0, 16), (1, 2)), (0, 1, 16, 2.0)),
        "moved": draw_moved(jax.random.fold_in(splits[7], 71), 0),
        "segments": draw_segments(jax.random.fold_in(splits[7], 71), 0),
        "input_norm_gain": jnp.clip(1.0 + 0.1 * jax.random.normal(splits[4], (D,), jnp.float32), 0.5, 1.5),
        "proj_in": noise(splits[5], (D, HEADS * (2 * DV + 2 * DQK)), D ** -0.5, 0.125, ((1, 2),)),
        "proj_out": noise(splits[6], (HEADS * DV, D), (HEADS * DV) ** -0.5, 0.1875, ((0, 2),)),
    }


epsilon = 1e-05
head_floor = 1.0

def head_pass(act_dev, seg_dev, mix_dev):
    span = 2 * DV + 2 * DQK
    rows = act_dev.shape[0]
    parts = act_dev.reshape(rows, HEADS, span).astype(jnp.float32)
    u_vals = parts[:, :, :DV]
    v_vals = parts[:, :, DV:2 * DV]
    q_vals = parts[:, :, 2 * DV:2 * DV + DQK]
    k_vals = parts[:, :, 2 * DV + DQK:]
    order = jnp.arange(rows, dtype=jnp.int32)
    visible = ((seg_dev[:, None] == seg_dev[None, :]) & (order[None, :] <= order[:, None])).astype(jnp.float32)
    scores = jnp.einsum('qhd,khd->hqk', q_vals, k_vals)
    sig_s = jax.nn.sigmoid(scores)
    attend = (scores * sig_s * visible).astype(jnp.bfloat16).astype(jnp.float32)
    slope = sig_s * (1.0 + scores * (1.0 - sig_s))
    outvals = jnp.einsum('hqk,khd->qhd', attend, v_vals)
    mean_shifted = outvals - lax.optimization_barrier(jnp.mean(outvals, axis=-1, keepdims=True))
    head_inv = lax.rsqrt(lax.optimization_barrier(jnp.mean(mean_shifted * mean_shifted, axis=-1, keepdims=True)) + head_floor)
    onorm = mean_shifted * head_inv
    mixed = (onorm * u_vals).astype(jnp.bfloat16)
    grad_mix = mix_dev.reshape(rows, HEADS, DV)
    grad_u = grad_mix * onorm
    gon = grad_mix * u_vals
    grad_o = (head_inv * (gon - lax.optimization_barrier(jnp.mean(gon, axis=-1, keepdims=True)) - onorm * lax.optimization_barrier(jnp.mean(gon * onorm, axis=-1, keepdims=True)))).astype(jnp.bfloat16).astype(jnp.float32)
    grad_att = jnp.einsum('qhd,khd->hqk', grad_o, v_vals)
    grad_v = jnp.einsum('hqk,qhd->khd', attend, grad_o)
    grad_scores = (grad_att * visible * slope).astype(jnp.bfloat16).astype(jnp.float32)
    grad_q = jnp.einsum('hqk,khd->qhd', grad_scores, k_vals)
    grad_k = jnp.einsum('hqk,qhd->khd', grad_scores, q_vals)
    grad_act = jnp.concatenate([grad_u, grad_v, grad_q, grad_k], axis=-1).reshape(rows, HEADS * span)
    return (mixed.reshape(rows, HEADS * DV), grad_act)

def reference(inputs, grad_moved, moved, segments, input_norm_gain, proj_in, proj_out):
    groups = N_DP
    span = 2 * DV + 2 * DQK
    blocks = grad_moved.reshape(groups, NBLK, BLOCK, D)
    partner = jnp.concatenate([blocks[groups // 2:], blocks[:groups // 2]], axis=0)
    output_gradient = jnp.where(moved[:, :, None, None] == 1, partner, blocks).reshape(TOKENS, D)
    xfull = inputs.astype(jnp.float32)
    mean_shifted = xfull - lax.optimization_barrier(jnp.mean(xfull, axis=1, keepdims=True))
    inverse_deviation = lax.rsqrt(lax.optimization_barrier(jnp.mean(mean_shifted * mean_shifted, axis=1, keepdims=True)) + epsilon)
    standardized_input = mean_shifted * inverse_deviation
    normalized_rows = (standardized_input * input_norm_gain[None, :]).astype(jnp.bfloat16)
    pre = jnp.dot(normalized_rows, proj_in, preferred_element_type=jnp.float32)
    sig_p = jax.nn.sigmoid(pre)
    act = (pre * sig_p).astype(jnp.bfloat16)
    grad_mix = lax.dot_general(output_gradient, proj_out, (((1,), (1,)), ((), ())), preferred_element_type=jnp.float32)
    mixed, grad_act = lax.map(lambda item: head_pass(item[0], item[1], item[2]), (act.reshape(groups, ROWS_DEV, HEADS * span), segments.reshape(groups, ROWS_DEV), grad_mix.reshape(groups, ROWS_DEV, HEADS * DV)))
    mixed = mixed.reshape(TOKENS, HEADS * DV)
    grad_act = grad_act.reshape(TOKENS, HEADS * span)
    grad_pre = (grad_act * sig_p * (1.0 + pre * (1.0 - sig_p))).astype(jnp.bfloat16)
    grad_proj_out = lax.dot_general(mixed, output_gradient, (((0,), (0,)), ((), ())), preferred_element_type=jnp.float32)
    grad_proj_in = lax.dot_general(normalized_rows, grad_pre, (((0,), (0,)), ((), ())), preferred_element_type=jnp.float32)
    width = HPD * span
    grad_normed = jnp.zeros((TOKENS, D), jnp.float32)
    for group in range(N_MP):
        term = lax.dot_general(grad_pre[:, group * width:(group + 1) * width], proj_in[:, group * width:(group + 1) * width], (((1,), (1,)), ((), ())), preferred_element_type=jnp.float32)
        rounded = lax.optimization_barrier(term.astype(jnp.bfloat16))
        grad_normed = grad_normed + rounded.astype(jnp.float32)
    gain_scaled = grad_normed * input_norm_gain[None, :]
    input_gradient = output_gradient.astype(jnp.float32) + inverse_deviation * (gain_scaled - lax.optimization_barrier(jnp.mean(gain_scaled, axis=1, keepdims=True)) - standardized_input * lax.optimization_barrier(jnp.mean(gain_scaled * standardized_input, axis=1, keepdims=True)))
    return (input_gradient.astype(jnp.bfloat16), grad_proj_in, grad_proj_out)
```

```python
import jax
import jax.numpy as jnp
from jax import lax
from jax.experimental import pallas as pl
from jax.experimental.pallas import tpu as pltpu
from jax.sharding import PartitionSpec as P

DV = 128
DQK = 64
BLOCK = 128


epsilon = 1e-05
head_floor = 1.0


def swapped(block, axis, apart):
    count = lax.axis_size(axis)
    route = []
    for low in range(count):
        high = low | 1 << apart
        if high != low and high < count:
            route += [(low, high), (high, low)]
    return lax.ppermute(block, axis, route)


def gathered(block):
    return lax.all_gather(block, "mp", axis=1, tiled=True)


def forward_heads(acts, visible, heads_here):
    span = 2 * DV + 2 * DQK
    rows = acts.shape[0]
    parts = acts.reshape(rows, heads_here, span)
    u_vals = parts[:, :, :DV]
    v_vals = parts[:, :, DV : 2 * DV]
    q_vals = parts[:, :, 2 * DV : 2 * DV + DQK]
    k_vals = parts[:, :, 2 * DV + DQK :]
    scores = jnp.einsum("qhd,khd->hqk", q_vals, k_vals, preferred_element_type=jnp.float32)
    sig_s = jax.nn.sigmoid(scores)
    attend = (scores * sig_s * visible[None]).astype(jnp.bfloat16)
    slope = sig_s * (1.0 + scores * (1.0 - sig_s))
    outvals = jnp.einsum("hqk,khd->qhd", attend, v_vals, preferred_element_type=jnp.float32)
    mean_shifted = outvals - jnp.mean(outvals, axis=-1, keepdims=True)
    head_inv = lax.rsqrt(jnp.mean(mean_shifted * mean_shifted, axis=-1, keepdims=True) + head_floor)
    onorm = mean_shifted * head_inv
    mixed = (onorm * u_vals).astype(jnp.bfloat16).reshape(rows, heads_here * DV)
    saved = (u_vals, v_vals, q_vals, k_vals, attend, slope, onorm, head_inv)
    return (mixed, saved)


def backward_heads(saved, grad_mix, visible, heads_here):
    u_vals, v_vals, q_vals, k_vals, attend, slope, onorm, head_inv = saved
    rows = grad_mix.shape[0]
    grad_mixr = grad_mix.reshape(rows, heads_here, DV)
    grad_u = grad_mixr * onorm
    gon = grad_mixr * u_vals
    grad_o = (
        head_inv
        * (
            gon
            - jnp.mean(gon, axis=-1, keepdims=True)
            - onorm * jnp.mean(gon * onorm, axis=-1, keepdims=True)
        )
    ).astype(jnp.bfloat16)
    grad_att = jnp.einsum("qhd,khd->hqk", grad_o, v_vals, preferred_element_type=jnp.float32)
    grad_v = jnp.einsum("hqk,qhd->khd", attend, grad_o, preferred_element_type=jnp.float32)
    grad_scores = (grad_att * visible[None] * slope).astype(jnp.bfloat16)
    grad_q = jnp.einsum("hqk,khd->qhd", grad_scores, k_vals, preferred_element_type=jnp.float32)
    grad_k = jnp.einsum("hqk,qhd->khd", grad_scores, q_vals, preferred_element_type=jnp.float32)
    grad_act = jnp.concatenate([grad_u, grad_v, grad_q, grad_k], axis=-1)
    return grad_act.reshape(rows, heads_here * (2 * DV + 2 * DQK))


MESH = pl.DeviceIdType.MESH
SPAN = 2 * DV + 2 * DQK
PIECE = 512
LOW, FULL = jnp.bfloat16, jnp.float32


def dot(a, b, i, j):
    return lax.dot_general(a, b, (((i,), (j,)), ((), ())), preferred_element_type=FULL)


def fused_kernel(
    x_hbm, g_hbm, moved_ref, seg_ref, gain_ref, win_hbm, wout_hbm,
    gin_ref, gout_ref, grad_ref,
    x2, own_g, land_z, dy2, w_in, w_out, lhs_t, rhs, slope_p, u_all, v_all, q_all, k_all,
    att0, att1, att2, att3, slo0, slo1, slo2, slo3, onorm_ref, hinv_ref, gm_ref, gv_acc, gk_acc,
    mean_ref, inv_ref, land_t, send_t, own_t, land_s, send_s,
    send_c, recv_c, send_y, keep_y, recv_y, send_z, from_low, from_high,
    sem_local, sem_zs, sem_zr, sem_xs, sem_xr, sem_ds, sem_dr, sem_ts, sem_tr,
    sem_cs, sem_cr, sem_ys, sem_yr, sem_fs, sem_low, sem_high,
):
    heads = u_all.shape[0]
    half = x_hbm.shape[1]
    wide = heads * SPAN
    attends = (att0, att1, att2, att3)
    slopes = (slo0, slo1, slo2, slo3)
    d = lax.axis_index("dp")
    x = lax.axis_index("mp")
    z = d // 4
    y = (d // 2) % 2
    c = d % 2
    upper = z // 2
    inner = (z + upper) % 2
    core_peer = d + 1 - 2 * c
    y_peer = d + 2 - 4 * y
    partner = (d + 8) % 16

    barrier = pltpu.get_barrier_semaphore()

    def greet(where):
        pl.semaphore_signal(barrier, inc=1, device_id=where, device_id_type=MESH)

    greet({"dp": partner})
    greet({"mp": 1 - x})
    greet({"dp": core_peer})
    greet({"dp": y_peer})

    @pl.when(z > 0)
    def _():
        greet({"dp": d - 4})

    @pl.when(z < 3)
    def _():
        greet({"dp": d + 4})

    def local(i, src, dst):
        return pltpu.make_async_copy(src, dst, sem_local.at[i])

    local_x = local(0, x_hbm, x2.at[x])
    local_win = local(1, win_hbm, w_in)
    local_g = local(2, g_hbm, own_g)
    local_wout = local(3, wout_hbm, w_out)
    local_x.start()
    local_win.start()
    local_g.start()
    local_wout.start()

    pl.semaphore_wait(barrier, 4 + (z + 3) // 4 + (6 - z) // 4)

    def remote(src, dst, send_sem, recv_sem, where):
        return pltpu.make_async_remote_copy(
            src_ref=src, dst_ref=dst, send_sem=send_sem, recv_sem=recv_sem,
            device_id=where, device_id_type=MESH,
        )

    def rows_of(j):
        return pl.ds(pl.multiple_of(j * BLOCK, BLOCK), BLOCK)

    def short(i):
        return pl.ds(pl.multiple_of(i * 64, 64), 64)

    def swap(i):
        return remote(
            g_hbm.at[short(i)], land_z.at[short(i)], sem_zs.at[i], sem_zr.at[i], {"dp": partner}
        )

    def share_x(j):
        return remote(
            x_hbm.at[rows_of(j)], x2.at[x, rows_of(j)], sem_xs.at[j], sem_xr.at[j], {"mp": 1 - x}
        )

    def share_dy(i):
        return remote(
            dy2.at[x, short(i)], dy2.at[x, short(i)], sem_ds.at[i], sem_dr.at[i], {"mp": 1 - x}
        )

    def cross_t(j):
        return remote(
            send_t.at[rows_of(j)], land_t.at[rows_of(j)], sem_ts.at[j], sem_tr.at[j], {"mp": 1 - x}
        )

    cross_s = remote(send_s, land_s, sem_ts.at[4], sem_tr.at[4], {"mp": 1 - x})

    def begin_swap(i, carry):
        swap(7 - i).start()
        return carry

    def begin_share(j, carry):
        share_x(j).start()
        return carry

    lax.fori_loop(0, 8, begin_swap, 0)
    lax.fori_loop(0, 4, begin_share, 0)

    def arrive(j):
        rows = rows_of(j)
        share_x(j).wait_recv()
        first = x2[0, rows, :].astype(FULL)
        second = x2[1, rows, :].astype(FULL)
        total = jnp.sum(first, axis=1, keepdims=True) + jnp.sum(second, axis=1, keepdims=True)
        mean = total * (1.0 / (2 * half))
        first = first - mean
        second = second - mean
        square = jnp.sum(first * first, axis=1, keepdims=True) + jnp.sum(
            second * second, axis=1, keepdims=True
        )
        inverse = lax.rsqrt(square * (1.0 / (2 * half)) + epsilon)
        mean_ref[rows, :] = mean
        inv_ref[rows, :] = inverse
        n0 = (first * inverse * gain_ref[:, :half]).astype(LOW)
        n1 = (second * inverse * gain_ref[:, half:]).astype(LOW)
        lhs_t[0, :half, rows] = n0.T
        lhs_t[0, half:, rows] = n1.T
        for h in range(heads):
            cols = slice(h * SPAN, (h + 1) * SPAN)
            pre = dot(n0, w_in[:half, cols], 1, 0) + dot(n1, w_in[half:, cols], 1, 0)
            sig = jax.nn.sigmoid(pre)
            act = (pre * sig).astype(LOW)
            slope_p[rows, cols] = sig * (1.0 + pre * (1.0 - sig))
            u_all[h, rows, :] = act[:, :DV]
            v_all[h, rows, :] = act[:, DV : 2 * DV]
            q_all[h, rows, :] = act[:, 2 * DV : 2 * DV + DQK]
            k_all[h, rows, :] = act[:, 2 * DV + DQK :]

    def forward(j):
        rows = slice(j * BLOCK, (j + 1) * BLOCK)
        w = (j + 1) * BLOCK
        seg = seg_ref[:, :w].astype(FULL)
        mine = jnp.broadcast_to(seg[:, j * BLOCK :], (BLOCK, BLOCK)).T
        row = lax.broadcasted_iota(jnp.int32, (BLOCK, w), 0) + j * BLOCK
        col = lax.broadcasted_iota(jnp.int32, (BLOCK, w), 1)
        same = jnp.concatenate([mine] * (j + 1), axis=1) == seg
        visible = jnp.where(same & (col <= row), 1.0, 0.0)

        def head(h, carry):
            scores = dot(q_all[h, rows, :], k_all[h, :w, :], 1, 1)
            sig = jax.nn.sigmoid(scores)
            attend = (scores * sig * visible).astype(LOW)
            attends[j][h] = attend
            slopes[j][h] = sig * (1.0 + scores * (1.0 - sig)) * visible
            outvals = dot(attend, v_all[h, :w, :], 1, 0)
            shifted = outvals - jnp.mean(outvals, axis=1, keepdims=True)
            inverse = lax.rsqrt(jnp.mean(shifted * shifted, axis=1, keepdims=True) + head_floor)
            onorm = shifted * inverse
            hinv_ref[h, rows, :] = inverse
            cols = pl.ds(pl.multiple_of(h * DV, DV), DV)
            onorm_ref[rows, cols] = onorm
            mixed_at = pl.ds(pl.multiple_of(wide + h * DV, DV), DV)
            rhs[rows, mixed_at] = (onorm * u_all[h, rows, :].astype(FULL)).astype(LOW)
            return carry

        lax.fori_loop(0, heads, head, 0)

    def relay(j):
        for i in (2 * j + 1, 2 * j):
            rows = slice(i * 64, (i + 1) * 64)
            swap(i).wait_recv()
            flags = jnp.full((64, half), moved_ref[0, j], jnp.int32)
            dy2[x, rows, :] = jnp.where(
                flags == 1, land_z[rows, :].astype(FULL), own_g[rows, :].astype(FULL)
            ).astype(LOW)
            share_dy(i).start()

    def backward(j):
        rows = slice(j * BLOCK, (j + 1) * BLOCK)
        w = (j + 1) * BLOCK
        share_dy(2 * j + 1).wait_recv()
        share_dy(2 * j).wait_recv()
        d0, d1 = dy2[0, rows, :], dy2[1, rows, :]
        gm_ref[...] = dot(d0, w_out[:, :half], 1, 1) + dot(d1, w_out[:, half:], 1, 1)

        def head(h, carry):
            mix_at = pl.ds(pl.multiple_of(h * DV, DV), DV)
            base = pl.multiple_of(h * SPAN, DV)
            u_at = pl.ds(base, DV)
            v_at = pl.ds(pl.multiple_of(base + DV, DV), DV)
            qk_at = pl.ds(pl.multiple_of(base + 2 * DV, DV), DV)
            onorm = onorm_ref[rows, mix_at]
            mix = gm_ref[:, mix_at]
            gon = mix * u_all[h, rows, :].astype(FULL)
            grad_o = (
                hinv_ref[h, rows, :]
                * (
                    gon
                    - jnp.mean(gon, axis=1, keepdims=True)
                    - onorm * jnp.mean(gon * onorm, axis=1, keepdims=True)
                )
            ).astype(LOW)
            rhs[rows, u_at] = (mix * onorm * slope_p[rows, u_at]).astype(LOW)
            grad_s = (dot(grad_o, v_all[h, :w, :], 1, 1) * slopes[j][h]).astype(LOW)
            grad_v = dot(attends[j][h], grad_o, 0, 0)
            grad_k = dot(grad_s, q_all[h, rows, :], 0, 0)
            if j < 3:
                grad_v = grad_v + gv_acc[h, :w, :]
                grad_k = grad_k + gk_acc[h, :w, :]
            if j > 0:
                gv_acc[h, : j * BLOCK, :] = grad_v[: j * BLOCK]
                gk_acc[h, : j * BLOCK, :] = grad_k[: j * BLOCK]
            rhs[rows, v_at] = (grad_v[j * BLOCK :] * slope_p[rows, v_at]).astype(LOW)
            grad_qk = jnp.concatenate(
                [dot(grad_s, k_all[h, :w, :], 1, 0), grad_k[j * BLOCK :]], axis=1
            )
            rhs[rows, qk_at] = (grad_qk * slope_p[rows, qk_at]).astype(LOW)
            return carry

        lax.fori_loop(0, heads, head, 0)

    def turn(j):
        rows = slice(j * BLOCK, (j + 1) * BLOCK)
        lhs_t[1, :half, rows] = dy2[0, rows, :].T
        lhs_t[1, half:, rows] = dy2[1, rows, :].T

    def side_of(side):
        return pl.ds(pl.multiple_of(side * half, half), half)

    def standard(rows, side):
        return (x2[side, rows, :].astype(FULL) - mean_ref[rows, :]) * inv_ref[rows, :]

    def terms(j, carry):
        rows = rows_of(j)

        def half_term(side):
            term = dot(rhs[rows, :wide], w_in[side_of(side), :], 1, 1).astype(LOW)
            scaled = term.astype(FULL) * gain_ref[:, side_of(side)]
            first = jnp.sum(scaled, axis=1, keepdims=True)
            second = jnp.sum(scaled * standard(rows, side), axis=1, keepdims=True)
            return term, first, second

        away, first_a, second_a = half_term(1 - x)
        send_t[rows, :] = away
        cross_t(j).start()
        kept, first_k, second_k = half_term(x)
        own_t[rows, :] = kept
        lane = lax.broadcasted_iota(jnp.int32, (BLOCK, BLOCK), 1)
        send_s[rows, :] = jnp.where(lane == 0, first_a + first_k, second_a + second_k)
        return carry

    def gradient(j, carry):
        rows = rows_of(j)
        cross_t(j).wait_recv()
        means = (send_s[rows, :] + land_s[rows, :]) * (1.0 / (2 * half))
        normed_grad = own_t[rows, :].astype(FULL) + land_t[rows, :].astype(FULL)
        grad_ref[rows, :] = (
            dy2[x, rows, :].astype(FULL)
            + inv_ref[rows, :]
            * (
                normed_grad * gain_ref[:, side_of(x)]
                - means[:, 0:1]
                - standard(rows, x) * means[:, 1:2]
            )
        ).astype(LOW)
        cross_t(j).wait_send()
        return carry

    def target(k):
        v = (3 - k) + (k // 2) * inner * (2 * k - 5)
        return (1 - upper) * v + upper * (3 - v)

    def product(k, side, core, p):
        chunk = target(k) * 4 + side * 2 + core
        left = lhs_t[p // 3, rows_of(chunk), :]
        return dot(left, rhs[:, pl.ds(pl.multiple_of(p * PIECE, PIECE), PIECE)], 1, 0)

    def to_core(slot, p):
        return remote(
            send_c.at[slot, p], recv_c.at[slot, p], sem_cs.at[slot, p], sem_cr.at[slot, p],
            {"dp": core_peer},
        )

    def to_y(k, p):
        return remote(
            send_y.at[k, p], recv_y.at[k, p], sem_ys.at[k, p], sem_yr.at[k, p], {"dp": y_peer}
        )

    def up(k, t, p):
        return remote(
            send_z.at[k, p], from_low.at[t, p], sem_fs.at[k, p], sem_low.at[t, p], {"dp": d + 4}
        )

    def down(k, t, p):
        return remote(
            send_z.at[k, p], from_high.at[t, p], sem_fs.at[k, p], sem_high.at[t, p], {"dp": d - 4}
        )

    def away(k, low, high):
        def issue(p, carry):
            send_c[k, p] = product(k, 1 - y, 1 - c, p).astype(LOW)
            to_core(k, p).start()
            return carry

        def finish(p, carry):
            mine = product(k, 1 - y, c, p)
            to_core(k, p).wait_recv()
            send_y[k, p] = (mine + recv_c[k, p].astype(FULL)).astype(LOW)
            to_y(k, p).start()
            return carry

        lax.fori_loop(low, high, issue, 0)
        lax.fori_loop(low, high, finish, 0)

    def keep(k):
        def issue(p, carry):
            send_c[k + 4, p] = product(k, y, 1 - c, p).astype(LOW)
            to_core(k + 4, p).start()
            return carry

        def finish(p, carry):
            mine = product(k, y, c, p)
            to_core(k + 4, p).wait_recv()
            keep_y[k, p] = (mine + recv_c[k + 4, p].astype(FULL)).astype(LOW)
            return carry

        lax.fori_loop(0, 4, issue, 0)
        lax.fori_loop(0, 4, finish, 0)

    def along(k):
        t = target(k)

        def piece(p, carry):
            to_y(k, p).wait_recv()

            def forward_piece(arrived, sem, present, copy):
                @pl.when(present)
                def _():
                    pltpu.make_async_copy(arrived.at[t, p], arrived.at[t, p], sem.at[t, p]).wait()
                    send_z[k, p] = (
                        keep_y[k, p].astype(FULL)
                        + recv_y[k, p].astype(FULL)
                        + arrived[t, p].astype(FULL)
                    ).astype(LOW)

                @pl.when(jnp.logical_not(present))
                def _():
                    send_z[k, p] = (
                        keep_y[k, p].astype(FULL) + recv_y[k, p].astype(FULL)
                    ).astype(LOW)

                copy.start()

            @pl.when(t > z)
            def _():
                forward_piece(from_low, sem_low, z > 0, up(k, t, p))

            @pl.when(t < z)
            def _():
                forward_piece(from_high, sem_high, z < 3, down(k, t, p))

            return carry

        lax.fori_loop(0, 4, piece, 0)

    local_x.wait()
    local_win.wait()
    arrive(0)
    forward(0)
    arrive(1)
    forward(1)
    local_g.wait()
    relay(3)
    arrive(2)
    forward(2)
    arrive(3)
    forward(3)
    relay(2)
    local_wout.wait()
    backward(3)
    turn(3)
    relay(1)
    backward(2)
    turn(2)
    backward(1)
    turn(1)
    relay(0)
    lax.fori_loop(0, 3, lambda i, carry: terms(3 - i, carry), 0)
    backward(0)

    away(0, 0, 3)
    turn(0)
    away(0, 3, 4)
    keep(0)
    away(1, 0, 4)
    terms(0, 0)
    cross_s.start()
    keep(1)
    away(2, 0, 4)
    along(0)
    keep(2)
    away(3, 0, 4)
    keep(3)
    along(1)
    cross_s.wait()
    lax.fori_loop(0, 4, gradient, 0)
    along(2)

    total = gm_ref

    def gather_total(p):
        to_y(3, p).wait_recv()
        total[...] = keep_y[3, p].astype(FULL) + recv_y[3, p].astype(FULL)

        @pl.when(z > 0)
        def _():
            pltpu.make_async_copy(from_low.at[z, p], from_low.at[z, p], sem_low.at[z, p]).wait()
            total[...] += from_low[z, p].astype(FULL)

        @pl.when(z < 3)
        def _():
            pltpu.make_async_copy(from_high.at[z, p], from_high.at[z, p], sem_high.at[z, p]).wait()
            total[...] += from_high[z, p].astype(FULL)

    def store_in(p, carry):
        gather_total(p)
        gin_ref[:, pl.ds(pl.multiple_of(p * PIECE, PIECE), PIECE)] = total[...]
        return carry

    lax.fori_loop(0, 3, store_in, 0)
    gather_total(3)
    gout_ref[...] = total[...].T

    def drain_swap(i, carry):
        swap(i).wait_send()
        share_dy(i).wait_send()
        return carry

    lax.fori_loop(0, 8, drain_swap, 0)

    def drain_share(j, carry):
        share_x(j).wait_send()
        return carry

    lax.fori_loop(0, 4, drain_share, 0)

    def drain_core(i, carry):
        to_core(i // 4, i % 4).wait_send()
        return carry

    lax.fori_loop(0, 32, drain_core, 0)

    def drain_far(i, carry):
        k, p = i // 4, i % 4
        to_y(k, p).wait_send()
        t = target(k)

        @pl.when(t > z)
        def _():
            up(k, t, p).wait_send()

        @pl.when(t < z)
        def _():
            down(k, t, p).wait_send()

        return carry

    lax.fori_loop(0, 16, drain_far, 0)


def fused(inputs, grad_moved, moved, segments, gain, proj_in, proj_out):
    rows, half = inputs.shape
    wide, narrow = proj_in.shape[1], proj_out.shape[0]
    heads = wide // SPAN
    vmem, dma = pltpu.VMEM, pltpu.SemaphoreType.DMA
    anywhere = pl.BlockSpec(memory_space=pl.ANY)
    inside = pl.BlockSpec(memory_space=pltpu.VMEM)
    pieces = vmem((4, 4, 128, PIECE), LOW)
    widths = [(j + 1) * BLOCK for j in range(rows // BLOCK)]
    gin, gout, grad = pl.pallas_call(
        fused_kernel,
        out_shape=(
            jax.ShapeDtypeStruct((128, wide), FULL),
            jax.ShapeDtypeStruct((narrow, 128), FULL),
            jax.ShapeDtypeStruct((rows, half), LOW),
        ),
        in_specs=[
            anywhere, anywhere, pl.BlockSpec(memory_space=pltpu.SMEM), inside, inside,
            anywhere, anywhere,
        ],
        out_specs=[inside] * 3,
        scratch_shapes=[
            vmem((2, rows, half), LOW),
            vmem((rows, half), LOW),
            vmem((rows, half), LOW),
            vmem((2, rows, half), LOW),
            vmem(proj_in.shape, LOW),
            vmem(proj_out.shape, LOW),
            vmem((2, 2 * half, rows), LOW),
            vmem((rows, wide + narrow), LOW),
            vmem((rows, wide), FULL),
            vmem((heads, rows, DV), LOW),
            vmem((heads, rows, DV), LOW),
            vmem((heads, rows, DQK), LOW),
            vmem((heads, rows, DQK), LOW),
        ]
        + [vmem((heads, BLOCK, w), LOW) for w in widths]
        + [vmem((heads, BLOCK, w), FULL) for w in widths]
        + [
            vmem((rows, narrow), FULL),
            vmem((heads, rows, 1), FULL),
            vmem((BLOCK, narrow), FULL),
            vmem((heads, rows - BLOCK, DV), FULL),
            vmem((heads, rows - BLOCK, DQK), FULL),
            vmem((rows, 1), FULL),
            vmem((rows, 1), FULL),
            vmem((rows, half), LOW),
            vmem((rows, half), LOW),
            vmem((rows, half), LOW),
            vmem((rows, 128), FULL),
            vmem((rows, 128), FULL),
            vmem((8, 4, 128, PIECE), LOW),
            vmem((8, 4, 128, PIECE), LOW),
        ]
        + [pieces] * 6
        + [
            dma((4,)), dma((8,)), dma((8,)), dma((4,)), dma((4,)), dma((8,)), dma((8,)),
            dma((5,)), dma((5,)), dma((8, 4)), dma((8, 4)), dma((4, 4)), dma((4, 4)),
            dma((4, 4)), dma((4, 4)), dma((4, 4)),
        ],
        compiler_params=pltpu.CompilerParams(
            collective_id=0, has_side_effects=True, vmem_limit_bytes=62 * 1024 * 1024
        ),
    )(inputs, grad_moved, moved, segments[None, :], gain[None, :], proj_in, proj_out)
    return (grad, gin, gout)


def on_device(inputs, grad_moved, moved, segments, input_norm_gain, proj_in, proj_out):
    rows = inputs.shape[0]
    span = 2 * DV + 2 * DQK
    heads_here = proj_in.shape[1] // span
    if lax.axis_size("mp") == 2 and lax.axis_size("dp") == 16:
        return fused(inputs, grad_moved, moved, segments, input_norm_gain, proj_in, proj_out)
    top_bit = lax.axis_size("dp").bit_length() - 2
    blocks = rows // BLOCK
    mine = [grad_moved[j * BLOCK : (j + 1) * BLOCK] for j in range(blocks)]
    theirs = [swapped(block, "dp", top_bit) for block in mine]
    full_x = gathered(inputs)
    full_dy = jnp.concatenate(
        [gathered(jnp.where(moved[0, j] == 1, theirs[j], mine[j])) for j in range(blocks)], axis=0
    )
    xfull = full_x.astype(jnp.float32)
    mean_shifted = xfull - jnp.mean(xfull, axis=1, keepdims=True)
    inverse_deviation = lax.rsqrt(
        jnp.mean(mean_shifted * mean_shifted, axis=1, keepdims=True) + epsilon
    )
    standardized_input = mean_shifted * inverse_deviation
    normalized_rows = (standardized_input * input_norm_gain[None, :]).astype(jnp.bfloat16)
    pre = jnp.dot(normalized_rows, proj_in, preferred_element_type=jnp.float32)
    sig_p = jax.nn.sigmoid(pre)
    acts = (pre * sig_p).astype(jnp.bfloat16)
    grad_mix = lax.dot_general(
        full_dy, proj_out, (((1,), (1,)), ((), ())), preferred_element_type=jnp.float32
    )
    order = jnp.arange(rows, dtype=jnp.int32)
    visible = (
        (segments[:, None] == segments[None, :]) & (order[None, :] <= order[:, None])
    ).astype(jnp.float32)
    mixed, saved = forward_heads(acts, visible, heads_here)
    grad_act = backward_heads(saved, grad_mix, visible, heads_here)
    grad_pre = (grad_act * sig_p * (1.0 + pre * (1.0 - sig_p))).astype(jnp.bfloat16)
    local = inputs.shape[1]
    offset = lax.axis_index("mp") * local
    normed_term = lax.dot_general(
        grad_pre, proj_in, (((1,), (1,)), ((), ())), preferred_element_type=jnp.float32
    ).astype(jnp.bfloat16)
    term_scaled = normed_term.astype(jnp.float32) * input_norm_gain[None, :]
    sums = jnp.stack([jnp.sum(term_scaled, axis=1), jnp.sum(term_scaled * standardized_input, axis=1)])
    partial_out = lax.dot_general(
        mixed, full_dy, (((0,), (0,)), ((), ())), preferred_element_type=jnp.float32
    )
    grad_proj_out = lax.psum_scatter(
        partial_out.astype(jnp.bfloat16), "dp", scatter_dimension=1, tiled=True
    ).astype(jnp.float32)
    partial_in = lax.dot_general(
        normalized_rows, grad_pre, (((0,), (0,)), ((), ())), preferred_element_type=jnp.float32
    )
    grad_proj_in = lax.psum_scatter(
        partial_in.astype(jnp.bfloat16), "dp", scatter_dimension=0, tiled=True
    ).astype(jnp.float32)
    sums = lax.psum(sums, "mp")
    grad_normed = lax.psum_scatter(
        normed_term, "mp", scatter_dimension=1, tiled=True
    ).astype(jnp.float32)
    means = sums / standardized_input.shape[1]
    here = lambda array: lax.dynamic_slice_in_dim(array, offset, local, 1)
    grad_here = here(full_dy).astype(jnp.float32) + inverse_deviation * (
        grad_normed * here(input_norm_gain[None, :])
        - means[0][:, None]
        - here(standardized_input) * means[1][:, None]
    )
    input_gradient = grad_here.astype(jnp.bfloat16)
    return (input_gradient, grad_proj_in, grad_proj_out)


def solution(mesh):
    return jax.shard_map(
        on_device,
        mesh=mesh,
        in_specs=(
            P("dp", "mp"),
            P("dp", "mp"),
            P("dp", None),
            P("dp"),
            P(),
            P(None, "mp"),
            P("mp", None),
        ),
        out_specs=(P("dp", "mp"), P("dp", "mp"), P("mp", "dp")),
        check_vma=False,
    )
```

```python
import jax
import jax.numpy as jnp
from jax import lax
from jax.experimental import pallas as pl
from jax.experimental.pallas import tpu as pltpu
from jax.sharding import PartitionSpec as P

DV = 128
DQK = 64
BLOCK = 128


epsilon = 1e-05
head_floor = 1.0


def swapped(block, axis, apart):
    count = lax.axis_size(axis)
    route = []
    for low in range(count):
        high = low | 1 << apart
        if high != low and high < count:
            route += [(low, high), (high, low)]
    return lax.ppermute(block, axis, route)


def gathered(block):
    return lax.all_gather(block, "mp", axis=1, tiled=True)


def forward_heads(acts, visible, heads_here):
    span = 2 * DV + 2 * DQK
    rows = acts.shape[0]
    parts = acts.reshape(rows, heads_here, span)
    u_vals = parts[:, :, :DV]
    v_vals = parts[:, :, DV : 2 * DV]
    q_vals = parts[:, :, 2 * DV : 2 * DV + DQK]
    k_vals = parts[:, :, 2 * DV + DQK :]
    scores = jnp.einsum("qhd,khd->hqk", q_vals, k_vals, preferred_element_type=jnp.float32)
    sig_s = jax.nn.sigmoid(scores)
    attend = (scores * sig_s * visible[None]).astype(jnp.bfloat16)
    slope = sig_s * (1.0 + scores * (1.0 - sig_s))
    outvals = jnp.einsum("hqk,khd->qhd", attend, v_vals, preferred_element_type=jnp.float32)
    mean_shifted = outvals - jnp.mean(outvals, axis=-1, keepdims=True)
    head_inv = lax.rsqrt(jnp.mean(mean_shifted * mean_shifted, axis=-1, keepdims=True) + head_floor)
    onorm = mean_shifted * head_inv
    mixed = (onorm * u_vals).astype(jnp.bfloat16).reshape(rows, heads_here * DV)
    saved = (u_vals, v_vals, q_vals, k_vals, attend, slope, onorm, head_inv)
    return (mixed, saved)


def backward_heads(saved, grad_mix, visible, heads_here):
    u_vals, v_vals, q_vals, k_vals, attend, slope, onorm, head_inv = saved
    rows = grad_mix.shape[0]
    grad_mixr = grad_mix.reshape(rows, heads_here, DV)
    grad_u = grad_mixr * onorm
    gon = grad_mixr * u_vals
    grad_o = (
        head_inv
        * (
            gon
            - jnp.mean(gon, axis=-1, keepdims=True)
            - onorm * jnp.mean(gon * onorm, axis=-1, keepdims=True)
        )
    ).astype(jnp.bfloat16)
    grad_att = jnp.einsum("qhd,khd->hqk", grad_o, v_vals, preferred_element_type=jnp.float32)
    grad_v = jnp.einsum("hqk,qhd->khd", attend, grad_o, preferred_element_type=jnp.float32)
    grad_scores = (grad_att * visible[None] * slope).astype(jnp.bfloat16)
    grad_q = jnp.einsum("hqk,khd->qhd", grad_scores, k_vals, preferred_element_type=jnp.float32)
    grad_k = jnp.einsum("hqk,qhd->khd", grad_scores, q_vals, preferred_element_type=jnp.float32)
    grad_act = jnp.concatenate([grad_u, grad_v, grad_q, grad_k], axis=-1)
    return grad_act.reshape(rows, heads_here * (2 * DV + 2 * DQK))


MESH = pl.DeviceIdType.MESH
SPAN = 2 * DV + 2 * DQK
PIECE = 512
STRIP = 32
LOW, FULL = jnp.bfloat16, jnp.float32


def dot(a, b, i, j):
    return lax.dot_general(a, b, (((i,), (j,)), ((), ())), preferred_element_type=FULL)


def fused_kernel(
    x_hbm, g_hbm, moved_hbm, seg_hbm, gain_hbm, win_hbm, wout_hbm,
    gin_hbm, gout_hbm, grad_hbm,
    x2, own_g, land_z, dy2, w_in, w_out, lhs_t, rhs, slope_p, u_all, v_all, q_all, k_all,
    att0, att1, att2, att3, slo0, slo1, slo2, slo3, onorm_ref, hinv_ref, gm_ref, gv_acc, gk_acc,
    mean_ref, inv_ref, land_t, send_t, own_t, land_s, send_s, side_t, mixed_y,
    send_c, recv_c, send_g, recv_g, send_y, keep_y, recv_y, send_z, from_low, from_high,
    moved_ref, seg_ref, gain_ref, gin_ref, gout_ref, grad_ref,
    sem_local, sem_zs, sem_zr, sem_xs, sem_xr, sem_ds, sem_dr, sem_ts, sem_tr, sem_ms, sem_mr,
    sem_os, sem_or, sem_cs, sem_cr, sem_gs, sem_gr, sem_ys, sem_yr, sem_fs, sem_low, sem_high,
    sem_out,
):
    heads = u_all.shape[0]
    half = x_hbm.shape[1]
    wide = heads * SPAN
    attends = (att0, att1, att2, att3)
    slopes = (slo0, slo1, slo2, slo3)
    d = lax.axis_index("dp")
    x = lax.axis_index("mp")
    z = d // 4
    y = (d // 2) % 2
    c = d % 2
    upper = z // 2
    inner = (z + upper) % 2
    core_peer = d + 1 - 2 * c
    y_peer = d + 2 - 4 * y
    partner = (d + 8) % 16

    barrier = pltpu.get_barrier_semaphore()

    def greet(where):
        pl.semaphore_signal(barrier, inc=1, device_id=where, device_id_type=MESH)

    greet({"dp": partner})
    greet({"mp": 1 - x})
    greet({"dp": core_peer})
    greet({"dp": y_peer})

    @pl.when(z > 0)
    def _():
        greet({"dp": d - 4})

    @pl.when(z < 3)
    def _():
        greet({"dp": d + 4})

    def local(i, src, dst):
        return pltpu.make_async_copy(src, dst, sem_local.at[i])

    local_x = local(0, x_hbm, x2.at[x])
    local_win = local(1, win_hbm, w_in)
    local_g = local(2, g_hbm, own_g)
    local_wout = local(3, wout_hbm, w_out)
    local_gain = local(4, gain_hbm, gain_ref)
    local_seg = local(5, seg_hbm, seg_ref)
    local_moved = local(6, moved_hbm, moved_ref)
    local_x.start()
    local_gain.start()
    local_win.start()
    local_seg.start()
    local_moved.start()
    local_g.start()
    local_wout.start()

    pl.semaphore_wait(barrier, 4 + (z + 3) // 4 + (6 - z) // 4)

    def remote(src, dst, send_sem, recv_sem, where):
        return pltpu.make_async_remote_copy(
            src_ref=src, dst_ref=dst, send_sem=send_sem, recv_sem=recv_sem,
            device_id=where, device_id_type=MESH,
        )

    def rows_of(j):
        return pl.ds(pl.multiple_of(j * BLOCK, BLOCK), BLOCK)

    def short(i):
        return pl.ds(pl.multiple_of(i * STRIP, STRIP), STRIP)

    def swap(i):
        return remote(
            g_hbm.at[short(i)], land_z.at[short(i)], sem_zs.at[i], sem_zr.at[i], {"dp": partner}
        )

    def share_x(j):
        return remote(
            x_hbm.at[rows_of(j)], x2.at[x, rows_of(j)], sem_xs.at[j], sem_xr.at[j], {"mp": 1 - x}
        )

    def share_dy(i):
        return remote(
            dy2.at[x, short(i)], dy2.at[x, short(i)], sem_ds.at[i], sem_dr.at[i], {"mp": 1 - x}
        )

    def cross_t(i):
        return remote(send_t.at[i], land_t.at[i], sem_ts.at[i], sem_tr.at[i], {"mp": 1 - x})

    share_mixed = remote(
        rhs.at[:, pl.ds(wide, heads * DV)], mixed_y, sem_ms, sem_mr, {"dp": y_peer}
    )

    def share_turned(q, j):
        there = pl.ds(pl.multiple_of((2 * q + 1 - y) * 256, 256), 256)
        landing = pl.ds(pl.multiple_of(q * 256, 256), 256)
        return remote(
            lhs_t.at[1, there, rows_of(j)], side_t.at[landing, rows_of(j)],
            sem_os.at[q, j], sem_or.at[q, j], {"dp": y_peer},
        )

    cross_s = remote(send_s, land_s, sem_ts.at[4], sem_tr.at[4], {"mp": 1 - x})

    def begin_swap(i, carry):
        swap(15 - i).start()
        return carry

    def begin_share(j, carry):
        share_x(j).start()
        return carry

    lax.fori_loop(0, 16, begin_swap, 0)
    lax.fori_loop(0, 4, begin_share, 0)

    def arrive(j):
        rows = rows_of(j)
        share_x(j).wait_recv()
        first = x2[0, rows, :].astype(FULL)
        second = x2[1, rows, :].astype(FULL)
        total = jnp.sum(first, axis=1, keepdims=True) + jnp.sum(second, axis=1, keepdims=True)
        mean = total * (1.0 / (2 * half))
        first = first - mean
        second = second - mean
        square = jnp.sum(first * first, axis=1, keepdims=True) + jnp.sum(
            second * second, axis=1, keepdims=True
        )
        inverse = lax.rsqrt(square * (1.0 / (2 * half)) + epsilon)
        mean_ref[rows, :] = mean
        inv_ref[rows, :] = inverse
        n0 = (first * inverse * gain_ref[:, :half]).astype(LOW)
        n1 = (second * inverse * gain_ref[:, half:]).astype(LOW)
        lhs_t[0, :half, rows] = n0.T
        lhs_t[0, half:, rows] = n1.T
        for h in range(heads):
            cols = slice(h * SPAN, (h + 1) * SPAN)
            pre = dot(n0, w_in[:half, cols], 1, 0) + dot(n1, w_in[half:, cols], 1, 0)
            sig = jax.nn.sigmoid(pre)
            act = (pre * sig).astype(LOW)
            slope_p[rows, cols] = sig * (1.0 + pre * (1.0 - sig))
            u_all[h, rows, :] = act[:, :DV]
            v_all[h, rows, :] = act[:, DV : 2 * DV]
            q_all[h, rows, :] = act[:, 2 * DV : 2 * DV + DQK]
            k_all[h, rows, :] = act[:, 2 * DV + DQK :]

    def forward(j):
        rows = slice(j * BLOCK, (j + 1) * BLOCK)
        w = (j + 1) * BLOCK
        seg = seg_ref[:, :w].astype(FULL)
        mine = jnp.broadcast_to(seg[:, j * BLOCK :], (BLOCK, BLOCK)).T
        row = lax.broadcasted_iota(jnp.int32, (BLOCK, w), 0) + j * BLOCK
        col = lax.broadcasted_iota(jnp.int32, (BLOCK, w), 1)
        same = jnp.concatenate([mine] * (j + 1), axis=1) == seg
        visible = jnp.where(same & (col <= row), 1.0, 0.0)

        def head(h, carry):
            scores = dot(q_all[h, rows, :], k_all[h, :w, :], 1, 1)
            sig = jax.nn.sigmoid(scores)
            attend = (scores * sig * visible).astype(LOW)
            attends[j][h] = attend
            slopes[j][h] = sig * (1.0 + scores * (1.0 - sig)) * visible
            outvals = dot(attend, v_all[h, :w, :], 1, 0)
            shifted = outvals - jnp.mean(outvals, axis=1, keepdims=True)
            inverse = lax.rsqrt(jnp.mean(shifted * shifted, axis=1, keepdims=True) + head_floor)
            onorm = shifted * inverse
            hinv_ref[h, rows, :] = inverse
            onorm_ref[rows, h * DV : (h + 1) * DV] = onorm
            mixed_at = slice(wide + h * DV, wide + (h + 1) * DV)
            rhs[rows, mixed_at] = (onorm * u_all[h, rows, :].astype(FULL)).astype(LOW)
            return carry

        for h in range(heads):
            head(h, 0)

    def relay(i):
        rows = slice(i * STRIP, (i + 1) * STRIP)
        swap(i).wait_recv()
        flags = jnp.full((STRIP, half), moved_ref[0, i // 4], jnp.int32)
        dy2[x, rows, :] = jnp.where(
            flags == 1, land_z[rows, :].astype(FULL), own_g[rows, :].astype(FULL)
        ).astype(LOW)
        share_dy(i).start()

    def backward(j):
        rows = slice(j * BLOCK, (j + 1) * BLOCK)
        w = (j + 1) * BLOCK
        for i in range(4):
            share_dy(4 * j + i).wait_recv()
        d0, d1 = dy2[0, rows, :], dy2[1, rows, :]
        gm_ref[...] = dot(d0, w_out[:, :half], 1, 1) + dot(d1, w_out[:, half:], 1, 1)

        def head(h, carry):
            mix_at = slice(h * DV, (h + 1) * DV)
            u_at = slice(h * SPAN, h * SPAN + DV)
            v_at = slice(h * SPAN + DV, h * SPAN + 2 * DV)
            qk_at = slice(h * SPAN + 2 * DV, (h + 1) * SPAN)
            onorm = onorm_ref[rows, mix_at]
            mix = gm_ref[:, mix_at]
            gon = mix * u_all[h, rows, :].astype(FULL)
            grad_o = (
                hinv_ref[h, rows, :]
                * (
                    gon
                    - jnp.mean(gon, axis=1, keepdims=True)
                    - onorm * jnp.mean(gon * onorm, axis=1, keepdims=True)
                )
            ).astype(LOW)
            rhs[rows, u_at] = (mix * onorm * slope_p[rows, u_at]).astype(LOW)
            grad_s = (dot(grad_o, v_all[h, :w, :], 1, 1) * slopes[j][h]).astype(LOW)
            grad_v = dot(attends[j][h], grad_o, 0, 0)
            grad_k = dot(grad_s, q_all[h, rows, :], 0, 0)
            if j < 3:
                grad_v = grad_v + gv_acc[h, :w, :]
                grad_k = grad_k + gk_acc[h, :w, :]
            if j > 0:
                gv_acc[h, : j * BLOCK, :] = grad_v[: j * BLOCK]
                gk_acc[h, : j * BLOCK, :] = grad_k[: j * BLOCK]
            rhs[rows, v_at] = (grad_v[j * BLOCK :] * slope_p[rows, v_at]).astype(LOW)
            grad_qk = jnp.concatenate(
                [dot(grad_s, k_all[h, :w, :], 1, 0), grad_k[j * BLOCK :]], axis=1
            )
            rhs[rows, qk_at] = (grad_qk * slope_p[rows, qk_at]).astype(LOW)
            return carry

        for h in range(heads):
            head(h, 0)

    def turn(j, side):
        rows = slice(j * BLOCK, (j + 1) * BLOCK)
        lhs_t[1, side_of(side), rows] = dy2[side, rows, :].T
        share_turned(2 * side, j).start()
        share_turned(2 * side + 1, j).start()

    def side_of(side):
        return pl.ds(pl.multiple_of(side * half, half), half)

    tile = 256

    def tile_of(side, i):
        return pl.ds(pl.multiple_of(side * half + i * tile, tile), tile)

    def inside(i):
        return pl.ds(pl.multiple_of(i * tile, tile), tile)

    def standard(side, i):
        return (x2[side, :, inside(i)].astype(FULL) - mean_ref[...]) * inv_ref[...]

    def term(side, i):
        part = dot(rhs[:, :wide], w_in[tile_of(side, i), :], 1, 1).astype(LOW)
        scaled = part.astype(FULL) * gain_ref[:, tile_of(side, i)]
        first = jnp.sum(scaled, axis=1, keepdims=True)
        second = jnp.sum(scaled * standard(side, i), axis=1, keepdims=True)
        lane = lax.broadcasted_iota(jnp.int32, send_s.shape, 1)
        return part, jnp.where(lane == 0, first, second)

    def term_away(i, carry):
        part, sums = term(1 - x, i)
        send_t[i] = part
        cross_t(i).start()
        send_s[...] = sums + send_s[...]
        return carry

    def term_kept(i, carry):
        part, sums = term(x, i)
        own_t[i] = part
        send_s[...] = sums + send_s[...]
        return carry

    def store_grad(i):
        return pltpu.make_async_copy(
            grad_ref.at[i], grad_hbm.at[:, inside(i)], sem_out.at[i]
        )

    def gradient(i, carry):
        cross_t(i).wait_recv()
        means = (send_s[...] + land_s[...]) * (1.0 / (2 * half))
        normed_grad = own_t[i].astype(FULL) + land_t[i].astype(FULL)
        grad_ref[i] = (
            dy2[x, :, inside(i)].astype(FULL)
            + inv_ref[...]
            * (
                normed_grad * gain_ref[:, tile_of(x, i)]
                - means[:, 0:1]
                - standard(x, i) * means[:, 1:2]
            )
        ).astype(LOW)
        store_grad(i).start()
        cross_t(i).wait_send()
        return carry

    def target(k):
        v = (3 - k) + (k // 2) * inner * (2 * k - 5)
        return (1 - upper) * v + upper * (3 - v)

    def product(k, side, core, p):
        chunk = target(k) * 4 + side * 2 + core
        left = lhs_t[0, rows_of(chunk), :]
        return dot(left, rhs[:, pl.ds(pl.multiple_of(p * PIECE, PIECE), PIECE)], 1, 0)

    def to_core(slot, p):
        return remote(
            send_c.at[slot, p], recv_c.at[slot, p], sem_cs.at[slot, p], sem_cr.at[slot, p],
            {"dp": core_peer},
        )

    def to_y(k, p):
        return remote(
            send_y.at[k, p], recv_y.at[k, p], sem_ys.at[k, p], sem_yr.at[k, p], {"dp": y_peer}
        )

    def up(k, t, p):
        return remote(
            send_z.at[k, p], from_low.at[t, p], sem_fs.at[k, p], sem_low.at[t, p], {"dp": d + 4}
        )

    def down(k, t, p):
        return remote(
            send_z.at[k, p], from_high.at[t, p], sem_fs.at[k, p], sem_high.at[t, p], {"dp": d - 4}
        )

    def away(k):
        def issue(p, carry):
            send_c[k, p] = product(k, 1 - y, 1 - c, p).astype(LOW)
            to_core(k, p).start()
            return carry

        def finish(p, carry):
            mine = product(k, 1 - y, c, p)
            to_core(k, p).wait_recv()
            send_y[k, p] = (mine + recv_c[k, p].astype(FULL)).astype(LOW)
            to_y(k, p).start()
            return carry

        lax.fori_loop(0, 3, issue, 0)
        lax.fori_loop(0, 3, finish, 0)

    def keep(k):
        def issue(p, carry):
            send_c[k + 4, p] = product(k, y, 1 - c, p).astype(LOW)
            to_core(k + 4, p).start()
            return carry

        def finish(p, carry):
            mine = product(k, y, c, p)
            to_core(k + 4, p).wait_recv()
            keep_y[k, p] = (mine + recv_c[k + 4, p].astype(FULL)).astype(LOW)
            return carry

        lax.fori_loop(0, 3, issue, 0)
        lax.fori_loop(0, 3, finish, 0)

    def out_product(k, core):
        chunk = target(k) * 4 + y * 2 + core
        other = target(k) * 2 + core
        mixed = rhs[:, wide:]
        return dot(lhs_t[1, rows_of(chunk), :], mixed, 1, 0) + dot(
            side_t[rows_of(other), :], mixed_y[...], 1, 0
        )

    def out_core(k):
        return remote(
            send_g.at[k], recv_g.at[k], sem_gs.at[k], sem_gr.at[k], {"dp": core_peer}
        )

    def out_issue(k, carry):
        send_g[k] = out_product(k, 1 - c).astype(LOW)
        out_core(k).start()
        return carry

    def out_finish(k, carry):
        mine = out_product(k, c)
        out_core(k).wait_recv()
        keep_y[k, 3] = (mine + recv_g[k].astype(FULL)).astype(LOW)
        return carry

    def along_piece(k, p, with_y):
        t = target(k)
        if with_y:
            to_y(k, p).wait_recv()

        def here():
            if with_y:
                return keep_y[k, p].astype(FULL) + recv_y[k, p].astype(FULL)
            return keep_y[k, p].astype(FULL)

        def forward_piece(arrived, sem, present, copy):
            @pl.when(present)
            def _():
                pltpu.make_async_copy(arrived.at[t, p], arrived.at[t, p], sem.at[t, p]).wait()
                send_z[k, p] = (here() + arrived[t, p].astype(FULL)).astype(LOW)

            @pl.when(jnp.logical_not(present))
            def _():
                send_z[k, p] = here().astype(LOW)

            copy.start()

        @pl.when(t > z)
        def _():
            forward_piece(from_low, sem_low, z > 0, up(k, t, p))

        @pl.when(t < z)
        def _():
            forward_piece(from_high, sem_high, z < 3, down(k, t, p))

    def along(k, low, high):
        def piece(p, carry):
            along_piece(k, p, True)
            return carry

        lax.fori_loop(low, high, piece, 0)

    def along_out(k, carry):
        along_piece(k, 3, False)
        return carry

    send_s[...] = jnp.zeros_like(send_s)
    local_x.wait()
    local_gain.wait()
    local_win.wait()
    arrive(0)
    local_g.wait()
    local_moved.wait()
    local_seg.wait()
    relay(15)
    forward(0)
    relay(14)
    arrive(1)
    relay(13)
    forward(1)
    relay(12)
    arrive(2)
    relay(11)
    forward(2)
    relay(10)
    arrive(3)
    relay(9)
    forward(3)
    share_mixed.start()
    relay(8)
    local_wout.wait()
    backward(3)
    relay(7)
    turn(3, 0)
    turn(3, 1)
    backward(2)
    relay(6)
    turn(2, 0)
    turn(2, 1)
    relay(5)
    relay(4)
    relay(3)
    backward(1)
    relay(2)
    turn(1, 0)
    turn(1, 1)
    relay(1)
    relay(0)
    turn(0, x)
    backward(0)

    away(0)
    turn(0, 1 - x)
    keep(0)
    lax.fori_loop(0, 2, term_away, 0)
    along(0, 0, 1)
    lax.fori_loop(2, 4, term_away, 0)
    away(1)
    along(0, 1, 2)
    keep(1)
    away(2)
    along(0, 2, 3)
    keep(2)
    share_mixed.wait_recv()

    def turned_here(i, carry):
        share_turned(i // 4, i % 4).wait_recv()
        return carry

    lax.fori_loop(0, 16, turned_here, 0)
    lax.fori_loop(0, 4, out_issue, 0)
    lax.fori_loop(0, 4, out_finish, 0)
    along_out(0, 0)
    along(1, 0, 1)
    away(3)
    along_out(1, 0)
    along(1, 1, 2)
    lax.fori_loop(0, 4, term_kept, 0)
    cross_s.start()
    along_out(2, 0)
    along(1, 2, 3)
    keep(3)
    along(2, 0, 1)
    cross_s.wait()
    lax.fori_loop(0, 4, gradient, 0)
    along(2, 1, 3)

    total = gm_ref

    def gather_total(p, with_y):
        if with_y:
            to_y(3, p).wait_recv()
            total[...] = keep_y[3, p].astype(FULL) + recv_y[3, p].astype(FULL)
        else:
            total[...] = keep_y[3, p].astype(FULL)

        @pl.when(z > 0)
        def _():
            pltpu.make_async_copy(from_low.at[z, p], from_low.at[z, p], sem_low.at[z, p]).wait()
            total[...] += from_low[z, p].astype(FULL)

        @pl.when(z < 3)
        def _():
            pltpu.make_async_copy(from_high.at[z, p], from_high.at[z, p], sem_high.at[z, p]).wait()
            total[...] += from_high[z, p].astype(FULL)

    def store_in(p):
        cols = pl.ds(p * PIECE, PIECE)
        return pltpu.make_async_copy(gin_ref.at[:, cols], gin_hbm.at[:, cols], sem_out.at[4 + p])

    store_out = pltpu.make_async_copy(gout_ref, gout_hbm, sem_out.at[7])

    gather_total(3, False)
    gout_ref[...] = total[...].T
    store_out.start()
    for p in range(3):
        gather_total(p, True)
        gin_ref[:, p * PIECE : (p + 1) * PIECE] = total[...]
        store_in(p).start()

    def drain_swap(i, carry):
        swap(i).wait_send()
        share_dy(i).wait_send()
        return carry

    lax.fori_loop(0, 16, drain_swap, 0)

    def drain_share(j, carry):
        share_x(j).wait_send()
        out_core(j).wait_send()
        store_grad(j).wait()
        for q in range(4):
            share_turned(q, j).wait_send()
        return carry

    lax.fori_loop(0, 4, drain_share, 0)

    def drain_core(i, carry):
        to_core(i // 3, i % 3).wait_send()
        return carry

    lax.fori_loop(0, 24, drain_core, 0)
    share_mixed.wait_send()

    def drain_far(i, carry):
        k, p = i // 4, i % 4
        t = target(k)

        @pl.when(p < 3)
        def _():
            to_y(k, p).wait_send()

        @pl.when(t > z)
        def _():
            up(k, t, p).wait_send()

        @pl.when(t < z)
        def _():
            down(k, t, p).wait_send()

        return carry

    lax.fori_loop(0, 16, drain_far, 0)
    for p in range(3):
        store_in(p).wait()
    store_out.wait()


def finish_kernel(*refs):
    count = len(refs) // 2
    sems = refs[-1]
    copies = [
        pltpu.make_async_copy(refs[i], refs[count + i], sems.at[i]) for i in range(count)
    ]
    for copy in copies:
        copy.start()
    for copy in copies:
        copy.wait()


def finished(*arrays):
    anywhere = pl.BlockSpec(memory_space=pl.ANY)
    return pl.pallas_call(
        finish_kernel,
        out_shape=tuple(jax.ShapeDtypeStruct(a.shape, a.dtype) for a in arrays),
        in_specs=[anywhere] * len(arrays),
        out_specs=[anywhere] * len(arrays),
        scratch_shapes=[pltpu.SemaphoreType.DMA((len(arrays),))],
    )(*arrays)


def fused(inputs, grad_moved, moved, segments, gain, proj_in, proj_out):
    rows, half = inputs.shape
    wide, narrow = proj_in.shape[1], proj_out.shape[0]
    heads = wide // SPAN
    vmem, dma = pltpu.VMEM, pltpu.SemaphoreType.DMA
    anywhere = pl.BlockSpec(memory_space=pl.ANY)
    pieces = vmem((4, 4, 128, PIECE), LOW)
    thirds = vmem((4, 3, 128, PIECE), LOW)
    widths = [(j + 1) * BLOCK for j in range(rows // BLOCK)]
    gin, gout, grad = pl.pallas_call(
        fused_kernel,
        out_shape=(
            jax.ShapeDtypeStruct((128, wide), FULL),
            jax.ShapeDtypeStruct((narrow, 128), FULL),
            jax.ShapeDtypeStruct((rows, half), LOW),
        ),
        in_specs=[anywhere] * 7,
        out_specs=[anywhere] * 3,
        scratch_shapes=[
            vmem((2, rows, half), LOW),
            vmem((rows, half), LOW),
            vmem((rows, half), LOW),
            vmem((2, rows, half), LOW),
            vmem(proj_in.shape, LOW),
            vmem(proj_out.shape, LOW),
            vmem((2, 2 * half, rows), LOW),
            vmem((rows, wide + narrow), LOW),
            vmem((rows, wide), FULL),
            vmem((heads, rows, DV), LOW),
            vmem((heads, rows, DV), LOW),
            vmem((heads, rows, DQK), LOW),
            vmem((heads, rows, DQK), LOW),
        ]
        + [vmem((heads, BLOCK, w), LOW) for w in widths]
        + [vmem((heads, BLOCK, w), FULL) for w in widths]
        + [
            vmem((rows, narrow), FULL),
            vmem((heads, rows, 1), FULL),
            vmem((BLOCK, narrow), FULL),
            vmem((heads, rows - BLOCK, DV), FULL),
            vmem((heads, rows - BLOCK, DQK), FULL),
            vmem((rows, 1), FULL),
            vmem((rows, 1), FULL),
            vmem((4, rows, half // 4), LOW),
            vmem((4, rows, half // 4), LOW),
            vmem((4, rows, half // 4), LOW),
            vmem((rows, 128), FULL),
            vmem((rows, 128), FULL),
            vmem((half, rows), LOW),
            vmem((rows, narrow), LOW),
            vmem((8, 3, 128, PIECE), LOW),
            vmem((8, 3, 128, PIECE), LOW),
            vmem((4, 128, PIECE), LOW),
            vmem((4, 128, PIECE), LOW),
            thirds, pieces, thirds, pieces, pieces, pieces,
            pltpu.SMEM(moved.shape, jnp.int32),
            vmem((1, rows), jnp.int32),
            vmem((1, 2 * half), FULL),
            vmem((128, wide), FULL),
            vmem((narrow, 128), FULL),
            vmem((4, rows, half // 4), LOW),
            dma((7,)), dma((16,)), dma((16,)), dma((4,)), dma((4,)), dma((16,)), dma((16,)),
            dma((5,)), dma((5,)), dma, dma, dma((4, 4)), dma((4, 4)), dma((8, 3)), dma((8, 3)),
            dma((4,)), dma((4,)), dma((4, 3)), dma((4, 3)), dma((4, 4)), dma((4, 4)), dma((4, 4)),
            dma((8,)),
        ],
        compiler_params=pltpu.CompilerParams(
            collective_id=0, has_side_effects=True, vmem_limit_bytes=62 * 1024 * 1024
        ),
    )(inputs, grad_moved, moved, segments[None, :], gain[None, :], proj_in, proj_out)
    return finished(grad, gin, gout)


def on_device(inputs, grad_moved, moved, segments, input_norm_gain, proj_in, proj_out):
    rows = inputs.shape[0]
    span = 2 * DV + 2 * DQK
    heads_here = proj_in.shape[1] // span
    if lax.axis_size("mp") == 2 and lax.axis_size("dp") == 16:
        return fused(inputs, grad_moved, moved, segments, input_norm_gain, proj_in, proj_out)
    top_bit = lax.axis_size("dp").bit_length() - 2
    blocks = rows // BLOCK
    mine = [grad_moved[j * BLOCK : (j + 1) * BLOCK] for j in range(blocks)]
    theirs = [swapped(block, "dp", top_bit) for block in mine]
    full_x = gathered(inputs)
    full_dy = jnp.concatenate(
        [gathered(jnp.where(moved[0, j] == 1, theirs[j], mine[j])) for j in range(blocks)], axis=0
    )
    xfull = full_x.astype(jnp.float32)
    mean_shifted = xfull - jnp.mean(xfull, axis=1, keepdims=True)
    inverse_deviation = lax.rsqrt(
        jnp.mean(mean_shifted * mean_shifted, axis=1, keepdims=True) + epsilon
    )
    standardized_input = mean_shifted * inverse_deviation
    normalized_rows = (standardized_input * input_norm_gain[None, :]).astype(jnp.bfloat16)
    pre = jnp.dot(normalized_rows, proj_in, preferred_element_type=jnp.float32)
    sig_p = jax.nn.sigmoid(pre)
    acts = (pre * sig_p).astype(jnp.bfloat16)
    grad_mix = lax.dot_general(
        full_dy, proj_out, (((1,), (1,)), ((), ())), preferred_element_type=jnp.float32
    )
    order = jnp.arange(rows, dtype=jnp.int32)
    visible = (
        (segments[:, None] == segments[None, :]) & (order[None, :] <= order[:, None])
    ).astype(jnp.float32)
    mixed, saved = forward_heads(acts, visible, heads_here)
    grad_act = backward_heads(saved, grad_mix, visible, heads_here)
    grad_pre = (grad_act * sig_p * (1.0 + pre * (1.0 - sig_p))).astype(jnp.bfloat16)
    local = inputs.shape[1]
    offset = lax.axis_index("mp") * local
    normed_term = lax.dot_general(
        grad_pre, proj_in, (((1,), (1,)), ((), ())), preferred_element_type=jnp.float32
    ).astype(jnp.bfloat16)
    term_scaled = normed_term.astype(jnp.float32) * input_norm_gain[None, :]
    sums = jnp.stack([jnp.sum(term_scaled, axis=1), jnp.sum(term_scaled * standardized_input, axis=1)])
    partial_out = lax.dot_general(
        mixed, full_dy, (((0,), (0,)), ((), ())), preferred_element_type=jnp.float32
    )
    grad_proj_out = lax.psum_scatter(
        partial_out.astype(jnp.bfloat16), "dp", scatter_dimension=1, tiled=True
    ).astype(jnp.float32)
    partial_in = lax.dot_general(
        normalized_rows, grad_pre, (((0,), (0,)), ((), ())), preferred_element_type=jnp.float32
    )
    grad_proj_in = lax.psum_scatter(
        partial_in.astype(jnp.bfloat16), "dp", scatter_dimension=0, tiled=True
    ).astype(jnp.float32)
    sums = lax.psum(sums, "mp")
    grad_normed = lax.psum_scatter(
        normed_term, "mp", scatter_dimension=1, tiled=True
    ).astype(jnp.float32)
    means = sums / standardized_input.shape[1]
    here = lambda array: lax.dynamic_slice_in_dim(array, offset, local, 1)
    grad_here = here(full_dy).astype(jnp.float32) + inverse_deviation * (
        grad_normed * here(input_norm_gain[None, :])
        - means[0][:, None]
        - here(standardized_input) * means[1][:, None]
    )
    input_gradient = grad_here.astype(jnp.bfloat16)
    return (input_gradient, grad_proj_in, grad_proj_out)


def solution(mesh):
    return jax.shard_map(
        on_device,
        mesh=mesh,
        in_specs=(
            P("dp", "mp"),
            P("dp", "mp"),
            P("dp", None),
            P("dp"),
            P(),
            P(None, "mp"),
            P("mp", None),
        ),
        out_specs=(P("dp", "mp"), P("dp", "mp"), P("mp", "dp")),
        check_vma=False,
    )
```

```python
import jax
import jax.numpy as jnp
from jax import lax
from jax.experimental import pallas as pl
from jax.experimental.pallas import tpu as pltpu
from jax.sharding import PartitionSpec as P

DV = 128
DQK = 64
BLOCK = 128


epsilon = 1e-05
head_floor = 1.0


def swapped(block, axis, apart):
    count = lax.axis_size(axis)
    route = []
    for low in range(count):
        high = low | 1 << apart
        if high != low and high < count:
            route += [(low, high), (high, low)]
    return lax.ppermute(block, axis, route)


def gathered(block):
    return lax.all_gather(block, "mp", axis=1, tiled=True)


def forward_heads(acts, visible, heads_here):
    span = 2 * DV + 2 * DQK
    rows = acts.shape[0]
    parts = acts.reshape(rows, heads_here, span)
    u_vals = parts[:, :, :DV]
    v_vals = parts[:, :, DV : 2 * DV]
    q_vals = parts[:, :, 2 * DV : 2 * DV + DQK]
    k_vals = parts[:, :, 2 * DV + DQK :]
    scores = jnp.einsum("qhd,khd->hqk", q_vals, k_vals, preferred_element_type=jnp.float32)
    sig_s = jax.nn.sigmoid(scores)
    attend = (scores * sig_s * visible[None]).astype(jnp.bfloat16)
    slope = sig_s * (1.0 + scores * (1.0 - sig_s))
    outvals = jnp.einsum("hqk,khd->qhd", attend, v_vals, preferred_element_type=jnp.float32)
    mean_shifted = outvals - jnp.mean(outvals, axis=-1, keepdims=True)
    head_inv = lax.rsqrt(jnp.mean(mean_shifted * mean_shifted, axis=-1, keepdims=True) + head_floor)
    onorm = mean_shifted * head_inv
    mixed = (onorm * u_vals).astype(jnp.bfloat16).reshape(rows, heads_here * DV)
    saved = (u_vals, v_vals, q_vals, k_vals, attend, slope, onorm, head_inv)
    return (mixed, saved)


def backward_heads(saved, grad_mix, visible, heads_here):
    u_vals, v_vals, q_vals, k_vals, attend, slope, onorm, head_inv = saved
    rows = grad_mix.shape[0]
    grad_mixr = grad_mix.reshape(rows, heads_here, DV)
    grad_u = grad_mixr * onorm
    gon = grad_mixr * u_vals
    grad_o = (
        head_inv
        * (
            gon
            - jnp.mean(gon, axis=-1, keepdims=True)
            - onorm * jnp.mean(gon * onorm, axis=-1, keepdims=True)
        )
    ).astype(jnp.bfloat16)
    grad_att = jnp.einsum("qhd,khd->hqk", grad_o, v_vals, preferred_element_type=jnp.float32)
    grad_v = jnp.einsum("hqk,qhd->khd", attend, grad_o, preferred_element_type=jnp.float32)
    grad_scores = (grad_att * visible[None] * slope).astype(jnp.bfloat16)
    grad_q = jnp.einsum("hqk,khd->qhd", grad_scores, k_vals, preferred_element_type=jnp.float32)
    grad_k = jnp.einsum("hqk,qhd->khd", grad_scores, q_vals, preferred_element_type=jnp.float32)
    grad_act = jnp.concatenate([grad_u, grad_v, grad_q, grad_k], axis=-1)
    return grad_act.reshape(rows, heads_here * (2 * DV + 2 * DQK))


MESH = pl.DeviceIdType.MESH
SPAN = 2 * DV + 2 * DQK
PIECE = 512
STRIP = 32
LOW, FULL = jnp.bfloat16, jnp.float32


def dot(a, b, i, j):
    return lax.dot_general(a, b, (((i,), (j,)), ((), ())), preferred_element_type=FULL)


def fused_kernel(
    x_hbm, g_hbm, moved_hbm, seg_hbm, gain_hbm, win_hbm, wout_hbm,
    gin_hbm, gout_hbm, grad_hbm,
    x2, own_g, land_z, dy2, w_in, w_out, norm_t, dy_t, rhs, mixed, slope_p, u_all, v_all, q_all, k_all,
    att0, att1, att2, att3, slo0, slo1, slo2, slo3, onorm_ref, hinv_ref, gm_ref, gv_acc, gk_acc,
    mean_ref, inv_ref, land_t, send_t, own_t, land_s, send_s, side_t, mixed_y,
    send_c, recv_c, send_g, recv_g, send_y, keep_y, recv_y, send_z, from_low, from_high,
    moved_ref, seg_ref, gain_ref, gin_ref, gout_ref, grad_ref,
    sem_local, sem_zs, sem_zr, sem_xs, sem_xr, sem_ds, sem_dr, sem_ts, sem_tr, sem_ms, sem_mr,
    sem_os, sem_or, sem_cs, sem_cr, sem_gs, sem_gr, sem_ys, sem_yr, sem_fs, sem_low, sem_high,
    sem_out,
):
    heads = u_all.shape[0]
    half = x_hbm.shape[1]
    wide = heads * SPAN
    attends = (att0, att1, att2, att3)
    slopes = (slo0, slo1, slo2, slo3)
    d = lax.axis_index("dp")
    x = lax.axis_index("mp")
    z = d // 4
    y = (d // 2) % 2
    c = d % 2
    upper = z // 2
    inner = (z + upper) % 2
    core_peer = d + 1 - 2 * c
    y_peer = d + 2 - 4 * y
    partner = (d + 8) % 16

    barrier = pltpu.get_barrier_semaphore()

    def greet(where):
        pl.semaphore_signal(barrier, inc=1, device_id=where, device_id_type=MESH)

    greet({"dp": partner})
    greet({"mp": 1 - x})
    greet({"dp": core_peer})
    greet({"dp": y_peer})

    @pl.when(z > 0)
    def _():
        greet({"dp": d - 4})

    @pl.when(z < 3)
    def _():
        greet({"dp": d + 4})

    def local(i, src, dst):
        return pltpu.make_async_copy(src, dst, sem_local.at[i])

    local_x = local(0, x_hbm, x2.at[x])
    local_win = local(1, win_hbm, w_in)
    local_g = local(2, g_hbm, own_g)
    local_wout = local(3, wout_hbm, w_out)
    local_gain = local(4, gain_hbm, gain_ref)
    local_seg = local(5, seg_hbm, seg_ref)
    local_moved = local(6, moved_hbm, moved_ref)
    local_x.start()
    local_gain.start()
    local_win.start()
    local_seg.start()
    local_moved.start()
    local_g.start()
    local_wout.start()

    pl.semaphore_wait(barrier, 4 + (z + 3) // 4 + (6 - z) // 4)

    def remote(src, dst, send_sem, recv_sem, where):
        return pltpu.make_async_remote_copy(
            src_ref=src, dst_ref=dst, send_sem=send_sem, recv_sem=recv_sem,
            device_id=where, device_id_type=MESH,
        )

    def rows_of(j):
        return pl.ds(pl.multiple_of(j * BLOCK, BLOCK), BLOCK)

    def short(i):
        return pl.ds(pl.multiple_of(i * STRIP, STRIP), STRIP)

    def swap(i):
        return remote(
            g_hbm.at[short(i)], land_z.at[short(i)], sem_zs.at[i], sem_zr.at[i], {"dp": partner}
        )

    def share_x(j):
        return remote(
            x_hbm.at[rows_of(j)], x2.at[x, rows_of(j)], sem_xs.at[j], sem_xr.at[j], {"mp": 1 - x}
        )

    def share_dy(i):
        return remote(
            dy2.at[x, short(i)], dy2.at[x, short(i)], sem_ds.at[i], sem_dr.at[i], {"mp": 1 - x}
        )

    def cross_t(i):
        return remote(send_t.at[i], land_t.at[i], sem_ts.at[i], sem_tr.at[i], {"mp": 1 - x})

    def share_mixed(j):
        return remote(
            mixed.at[rows_of(j)], mixed_y.at[rows_of(j)], sem_ms.at[j], sem_mr.at[j],
            {"dp": y_peer},
        )

    def share_turned(q, j):
        there = pl.ds(pl.multiple_of((2 * q + 1 - y) * 256, 256), 256)
        landing = pl.ds(pl.multiple_of(q * 256, 256), 256)
        return remote(
            dy_t.at[j, there], side_t.at[j, landing],
            sem_os.at[q, j], sem_or.at[q, j], {"dp": y_peer},
        )

    cross_s = remote(send_s, land_s, sem_ts.at[4], sem_tr.at[4], {"mp": 1 - x})

    def begin_swap(i, carry):
        swap(15 - i).start()
        return carry

    def begin_share(j, carry):
        share_x(j).start()
        return carry

    lax.fori_loop(0, 16, begin_swap, 0)
    lax.fori_loop(0, 4, begin_share, 0)

    def arrive(j):
        rows = rows_of(j)
        share_x(j).wait_recv()
        first = x2[0, rows, :].astype(FULL)
        second = x2[1, rows, :].astype(FULL)
        total = jnp.sum(first, axis=1, keepdims=True) + jnp.sum(second, axis=1, keepdims=True)
        mean = total * (1.0 / (2 * half))
        first = first - mean
        second = second - mean
        square = jnp.sum(first * first, axis=1, keepdims=True) + jnp.sum(
            second * second, axis=1, keepdims=True
        )
        inverse = lax.rsqrt(square * (1.0 / (2 * half)) + epsilon)
        mean_ref[rows, :] = mean
        inv_ref[rows, :] = inverse
        n0 = (first * inverse * gain_ref[:, :half]).astype(LOW)
        n1 = (second * inverse * gain_ref[:, half:]).astype(LOW)
        norm_t[:half, rows] = n0.T
        norm_t[half:, rows] = n1.T
        for h in range(heads):
            cols = slice(h * SPAN, (h + 1) * SPAN)
            pre = dot(n0, w_in[:half, cols], 1, 0) + dot(n1, w_in[half:, cols], 1, 0)
            sig = jax.nn.sigmoid(pre)
            act = (pre * sig).astype(LOW)
            slope_p[rows, cols] = sig * (1.0 + pre * (1.0 - sig))
            u_all[h, rows, :] = act[:, :DV]
            v_all[h, rows, :] = act[:, DV : 2 * DV]
            q_all[h, rows, :] = act[:, 2 * DV : 2 * DV + DQK]
            k_all[h, rows, :] = act[:, 2 * DV + DQK :]

    def forward(j):
        rows = slice(j * BLOCK, (j + 1) * BLOCK)
        w = (j + 1) * BLOCK
        seg = seg_ref[:, :w].astype(FULL)
        mine = jnp.broadcast_to(seg[:, j * BLOCK :], (BLOCK, BLOCK)).T
        row = lax.broadcasted_iota(jnp.int32, (BLOCK, w), 0) + j * BLOCK
        col = lax.broadcasted_iota(jnp.int32, (BLOCK, w), 1)
        same = jnp.concatenate([mine] * (j + 1), axis=1) == seg
        visible = jnp.where(same & (col <= row), 1.0, 0.0)

        def head(h, carry):
            scores = dot(q_all[h, rows, :], k_all[h, :w, :], 1, 1)
            sig = jax.nn.sigmoid(scores)
            attend = (scores * sig * visible).astype(LOW)
            attends[j][h] = attend
            slopes[j][h] = sig * (1.0 + scores * (1.0 - sig)) * visible
            outvals = dot(attend, v_all[h, :w, :], 1, 0)
            shifted = outvals - jnp.mean(outvals, axis=1, keepdims=True)
            inverse = lax.rsqrt(jnp.mean(shifted * shifted, axis=1, keepdims=True) + head_floor)
            onorm = shifted * inverse
            hinv_ref[h, rows, :] = inverse
            onorm_ref[rows, h * DV : (h + 1) * DV] = onorm
            mixed[rows, h * DV : (h + 1) * DV] = (onorm * u_all[h, rows, :].astype(FULL)).astype(LOW)
            return carry

        for h in range(heads):
            head(h, 0)
        share_mixed(j).start()

    def relay(i):
        rows = slice(i * STRIP, (i + 1) * STRIP)
        swap(i).wait_recv()
        flags = jnp.full((STRIP, half), moved_ref[0, i // 4], jnp.int32)
        dy2[x, rows, :] = jnp.where(
            flags == 1, land_z[rows, :].astype(FULL), own_g[rows, :].astype(FULL)
        ).astype(LOW)
        share_dy(i).start()

    def side_of(side):
        return pl.ds(pl.multiple_of(side * half, half), half)

    def turn(j, side):
        rows = slice(j * BLOCK, (j + 1) * BLOCK)
        dy_t[j, side_of(side), :] = dy2[side, rows, :].T
        share_turned(2 * side, j).start()
        share_turned(2 * side + 1, j).start()

    def backward(j):
        rows = slice(j * BLOCK, (j + 1) * BLOCK)
        w = (j + 1) * BLOCK
        for i in range(4):
            share_dy(4 * j + i).wait_recv()
        if j > 0:
            turn(j, 0)
            turn(j, 1)
        d0, d1 = dy2[0, rows, :], dy2[1, rows, :]
        gm_ref[...] = dot(d0, w_out[:, :half], 1, 1) + dot(d1, w_out[:, half:], 1, 1)

        def head(h, carry):
            mix_at = slice(h * DV, (h + 1) * DV)
            u_at = slice(h * SPAN, h * SPAN + DV)
            v_at = slice(h * SPAN + DV, h * SPAN + 2 * DV)
            qk_at = slice(h * SPAN + 2 * DV, (h + 1) * SPAN)
            onorm = onorm_ref[rows, mix_at]
            mix = gm_ref[:, mix_at]
            gon = mix * u_all[h, rows, :].astype(FULL)
            grad_o = (
                hinv_ref[h, rows, :]
                * (
                    gon
                    - jnp.mean(gon, axis=1, keepdims=True)
                    - onorm * jnp.mean(gon * onorm, axis=1, keepdims=True)
                )
            ).astype(LOW)
            rhs[rows, u_at] = (mix * onorm * slope_p[rows, u_at]).astype(LOW)
            grad_s = (dot(grad_o, v_all[h, :w, :], 1, 1) * slopes[j][h]).astype(LOW)
            grad_v = dot(attends[j][h], grad_o, 0, 0)
            grad_k = dot(grad_s, q_all[h, rows, :], 0, 0)
            if j < 3:
                grad_v = grad_v + gv_acc[h, :w, :]
                grad_k = grad_k + gk_acc[h, :w, :]
            if j > 0:
                gv_acc[h, : j * BLOCK, :] = grad_v[: j * BLOCK]
                gk_acc[h, : j * BLOCK, :] = grad_k[: j * BLOCK]
            rhs[rows, v_at] = (grad_v[j * BLOCK :] * slope_p[rows, v_at]).astype(LOW)
            grad_qk = jnp.concatenate(
                [dot(grad_s, k_all[h, :w, :], 1, 0), grad_k[j * BLOCK :]], axis=1
            )
            rhs[rows, qk_at] = (grad_qk * slope_p[rows, qk_at]).astype(LOW)
            return carry

        for h in range(heads):
            head(h, 0)

    tile = 256

    def tile_of(side, i):
        return pl.ds(pl.multiple_of(side * half + i * tile, tile), tile)

    def inside(i):
        return pl.ds(pl.multiple_of(i * tile, tile), tile)

    def standard(side, i):
        return (x2[side, :, inside(i)].astype(FULL) - mean_ref[...]) * inv_ref[...]

    def term(side, i):
        part = dot(rhs[...], w_in[tile_of(side, i), :], 1, 1).astype(LOW)
        scaled = part.astype(FULL) * gain_ref[:, tile_of(side, i)]
        first = jnp.sum(scaled, axis=1, keepdims=True)
        second = jnp.sum(scaled * standard(side, i), axis=1, keepdims=True)
        lane = lax.broadcasted_iota(jnp.int32, send_s.shape, 1)
        return part, jnp.where(lane == 0, first, second)

    def term_away(i, carry):
        part, sums = term(1 - x, i)
        send_t[i] = part
        cross_t(i).start()
        send_s[...] = sums + send_s[...]
        return carry

    def term_kept(i, carry):
        part, sums = term(x, i)
        own_t[i] = part
        send_s[...] = sums + send_s[...]
        return carry

    def store_grad(i):
        return pltpu.make_async_copy(
            grad_ref.at[i], grad_hbm.at[:, inside(i)], sem_out.at[i]
        )

    def gradient(i, carry):
        cross_t(i).wait_recv()
        means = (send_s[...] + land_s[...]) * (1.0 / (2 * half))
        normed_grad = own_t[i].astype(FULL) + land_t[i].astype(FULL)
        grad_ref[i] = (
            dy2[x, :, inside(i)].astype(FULL)
            + inv_ref[...]
            * (
                normed_grad * gain_ref[:, tile_of(x, i)]
                - means[:, 0:1]
                - standard(x, i) * means[:, 1:2]
            )
        ).astype(LOW)
        store_grad(i).start()
        cross_t(i).wait_send()
        return carry

    def target(k):
        v = (3 - k) + (k // 2) * inner * (2 * k - 5)
        return (1 - upper) * v + upper * (3 - v)

    def product(k, side, core, p):
        chunk = target(k) * 4 + side * 2 + core
        left = norm_t[rows_of(chunk), :]
        return dot(left, rhs[:, pl.ds(pl.multiple_of(p * PIECE, PIECE), PIECE)], 1, 0)

    def to_core(slot, p):
        return remote(
            send_c.at[slot, p], recv_c.at[slot, p], sem_cs.at[slot, p], sem_cr.at[slot, p],
            {"dp": core_peer},
        )

    def to_y(k, p):
        return remote(
            send_y.at[k, p], recv_y.at[k, p], sem_ys.at[k, p], sem_yr.at[k, p], {"dp": y_peer}
        )

    def up(k, t, p):
        return remote(
            send_z.at[k, p], from_low.at[t, p], sem_fs.at[k, p], sem_low.at[t, p], {"dp": d + 4}
        )

    def down(k, t, p):
        return remote(
            send_z.at[k, p], from_high.at[t, p], sem_fs.at[k, p], sem_high.at[t, p], {"dp": d - 4}
        )

    def away(k):
        def issue(p, carry):
            send_c[k, p] = product(k, 1 - y, 1 - c, p).astype(LOW)
            to_core(k, p).start()
            return carry

        def finish(p, carry):
            mine = product(k, 1 - y, c, p)
            to_core(k, p).wait_recv()
            send_y[k, p] = (mine + recv_c[k, p].astype(FULL)).astype(LOW)
            to_y(k, p).start()
            return carry

        lax.fori_loop(0, 3, issue, 0)
        lax.fori_loop(0, 3, finish, 0)

    def keep(k):
        def issue(p, carry):
            send_c[k + 4, p] = product(k, y, 1 - c, p).astype(LOW)
            to_core(k + 4, p).start()
            return carry

        def finish(p, carry):
            mine = product(k, y, c, p)
            to_core(k + 4, p).wait_recv()
            keep_y[k, p] = (mine + recv_c[k + 4, p].astype(FULL)).astype(LOW)
            return carry

        lax.fori_loop(0, 3, issue, 0)
        lax.fori_loop(0, 3, finish, 0)

    def out_product(k, core):
        chunk = target(k) * 4 + y * 2 + core
        other = target(k) * 2 + core
        mine = jnp.concatenate([dy_t[j, rows_of(chunk), :] for j in range(4)], axis=1)
        theirs = jnp.concatenate([side_t[j, rows_of(other), :] for j in range(4)], axis=1)
        return dot(mine, mixed[...], 1, 0) + dot(theirs, mixed_y[...], 1, 0)

    def out_core(k):
        return remote(
            send_g.at[k], recv_g.at[k], sem_gs.at[k], sem_gr.at[k], {"dp": core_peer}
        )

    def out_issue(k, carry):
        send_g[k] = out_product(k, 1 - c).astype(LOW)
        out_core(k).start()
        return carry

    def out_finish(k, carry):
        mine = out_product(k, c)
        out_core(k).wait_recv()
        keep_y[k, 3] = (mine + recv_g[k].astype(FULL)).astype(LOW)
        return carry

    def along_piece(k, p, with_y):
        t = target(k)
        if with_y:
            to_y(k, p).wait_recv()

        def here():
            if with_y:
                return keep_y[k, p].astype(FULL) + recv_y[k, p].astype(FULL)
            return keep_y[k, p].astype(FULL)

        def forward_piece(arrived, sem, present, copy):
            @pl.when(present)
            def _():
                pltpu.make_async_copy(arrived.at[t, p], arrived.at[t, p], sem.at[t, p]).wait()
                send_z[k, p] = (here() + arrived[t, p].astype(FULL)).astype(LOW)

            @pl.when(jnp.logical_not(present))
            def _():
                send_z[k, p] = here().astype(LOW)

            copy.start()

        @pl.when(t > z)
        def _():
            forward_piece(from_low, sem_low, z > 0, up(k, t, p))

        @pl.when(t < z)
        def _():
            forward_piece(from_high, sem_high, z < 3, down(k, t, p))

    def along(k, low, high):
        def piece(p, carry):
            along_piece(k, p, True)
            return carry

        lax.fori_loop(low, high, piece, 0)

    def along_out(k, carry):
        along_piece(k, 3, False)
        return carry

    send_s[...] = jnp.zeros_like(send_s)
    local_x.wait()
    local_gain.wait()
    local_win.wait()
    arrive(0)
    local_g.wait()
    local_moved.wait()
    local_seg.wait()
    relay(15)
    forward(0)
    relay(14)
    arrive(1)
    relay(13)
    forward(1)
    relay(12)
    arrive(2)
    relay(11)
    forward(2)
    relay(10)
    arrive(3)
    relay(9)
    forward(3)
    relay(8)
    local_wout.wait()
    backward(3)
    relay(7)
    backward(2)
    relay(6)
    relay(5)
    relay(4)
    relay(3)
    backward(1)
    relay(2)
    relay(1)
    relay(0)
    turn(0, x)
    backward(0)

    away(0)
    turn(0, 1 - x)
    keep(0)
    lax.fori_loop(0, 2, term_away, 0)
    along(0, 0, 1)
    lax.fori_loop(2, 4, term_away, 0)
    away(1)
    along(0, 1, 2)
    keep(1)
    away(2)
    along(0, 2, 3)
    keep(2)

    def mixed_here(j, carry):
        share_mixed(j).wait_recv()
        return carry

    lax.fori_loop(0, 4, mixed_here, 0)

    def turned_here(i, carry):
        share_turned(i // 4, i % 4).wait_recv()
        return carry

    lax.fori_loop(0, 16, turned_here, 0)
    lax.fori_loop(0, 4, out_issue, 0)
    lax.fori_loop(0, 4, out_finish, 0)
    along_out(0, 0)
    along(1, 0, 1)
    away(3)
    along_out(1, 0)
    along(1, 1, 2)
    lax.fori_loop(0, 4, term_kept, 0)
    cross_s.start()
    along_out(2, 0)
    along(1, 2, 3)
    keep(3)
    along(2, 0, 1)
    cross_s.wait()
    lax.fori_loop(0, 4, gradient, 0)
    along(2, 1, 3)

    total = gm_ref

    def gather_total(p, with_y):
        if with_y:
            to_y(3, p).wait_recv()
            total[...] = keep_y[3, p].astype(FULL) + recv_y[3, p].astype(FULL)
        else:
            total[...] = keep_y[3, p].astype(FULL)

        @pl.when(z > 0)
        def _():
            pltpu.make_async_copy(from_low.at[z, p], from_low.at[z, p], sem_low.at[z, p]).wait()
            total[...] += from_low[z, p].astype(FULL)

        @pl.when(z < 3)
        def _():
            pltpu.make_async_copy(from_high.at[z, p], from_high.at[z, p], sem_high.at[z, p]).wait()
            total[...] += from_high[z, p].astype(FULL)

    def store_in(p):
        cols = pl.ds(p * PIECE, PIECE)
        return pltpu.make_async_copy(gin_ref.at[:, cols], gin_hbm.at[:, cols], sem_out.at[4 + p])

    store_out = pltpu.make_async_copy(gout_ref, gout_hbm, sem_out.at[7])

    gather_total(3, False)
    gout_ref[...] = total[...].T
    store_out.start()
    for p in range(3):
        gather_total(p, True)
        gin_ref[:, p * PIECE : (p + 1) * PIECE] = total[...]
        store_in(p).start()

    def drain_swap(i, carry):
        swap(i).wait_send()
        share_dy(i).wait_send()
        return carry

    lax.fori_loop(0, 16, drain_swap, 0)

    def drain_share(j, carry):
        share_x(j).wait_send()
        out_core(j).wait_send()
        share_mixed(j).wait_send()
        store_grad(j).wait()
        for q in range(4):
            share_turned(q, j).wait_send()
        return carry

    lax.fori_loop(0, 4, drain_share, 0)

    def drain_core(i, carry):
        to_core(i // 3, i % 3).wait_send()
        return carry

    lax.fori_loop(0, 24, drain_core, 0)

    def drain_far(i, carry):
        k, p = i // 4, i % 4
        t = target(k)

        @pl.when(p < 3)
        def _():
            to_y(k, p).wait_send()

        @pl.when(t > z)
        def _():
            up(k, t, p).wait_send()

        @pl.when(t < z)
        def _():
            down(k, t, p).wait_send()

        return carry

    lax.fori_loop(0, 16, drain_far, 0)
    for p in range(3):
        store_in(p).wait()
    store_out.wait()


def finish_kernel(grad, gin, gout, grad_out, gin_out, gout_out, b_grad, b_gin, b_gout, sems):
    steps = []
    for source, staged, result, parts in (
        (grad, b_grad, grad_out, 4), (gin, b_gin, gin_out, 2), (gout, b_gout, gout_out, 1),
    ):
        size = source.shape[0] // parts
        for i in range(parts):
            at = pl.ds(i * size, size)
            n = len(steps)
            steps.append((
                pltpu.make_async_copy(source.at[at], staged.at[at], sems.at[0, n]),
                pltpu.make_async_copy(staged.at[at], result.at[at], sems.at[1, n]),
            ))
    for fetch, _ in steps:
        fetch.start()
    for fetch, store in steps:
        fetch.wait()
        store.start()
    for _, store in steps:
        store.wait()


def finished(*arrays):
    anywhere = pl.BlockSpec(memory_space=pl.ANY)
    return pl.pallas_call(
        finish_kernel,
        out_shape=tuple(jax.ShapeDtypeStruct(a.shape, a.dtype) for a in arrays),
        in_specs=[anywhere] * len(arrays),
        out_specs=[anywhere] * len(arrays),
        scratch_shapes=[pltpu.VMEM(a.shape, a.dtype) for a in arrays]
        + [pltpu.SemaphoreType.DMA((2, 7))],
    )(*arrays)


def fused(inputs, grad_moved, moved, segments, gain, proj_in, proj_out):
    rows, half = inputs.shape
    wide, narrow = proj_in.shape[1], proj_out.shape[0]
    heads = wide // SPAN
    vmem, dma = pltpu.VMEM, pltpu.SemaphoreType.DMA
    anywhere = pl.BlockSpec(memory_space=pl.ANY)
    pieces = vmem((4, 4, 128, PIECE), LOW)
    thirds = vmem((4, 3, 128, PIECE), LOW)
    widths = [(j + 1) * BLOCK for j in range(rows // BLOCK)]
    gin, gout, grad = pl.pallas_call(
        fused_kernel,
        out_shape=(
            jax.ShapeDtypeStruct((128, wide), FULL),
            jax.ShapeDtypeStruct((narrow, 128), FULL),
            jax.ShapeDtypeStruct((rows, half), LOW),
        ),
        in_specs=[anywhere] * 7,
        out_specs=[anywhere] * 3,
        scratch_shapes=[
            vmem((2, rows, half), LOW),
            vmem((rows, half), LOW),
            vmem((rows, half), LOW),
            vmem((2, rows, half), LOW),
            vmem(proj_in.shape, LOW),
            vmem(proj_out.shape, LOW),
            vmem((2 * half, rows), LOW),
            vmem((4, 2 * half, BLOCK), LOW),
            vmem((rows, wide), LOW),
            vmem((rows, narrow), LOW),
            vmem((rows, wide), FULL),
            vmem((heads, rows, DV), LOW),
            vmem((heads, rows, DV), LOW),
            vmem((heads, rows, DQK), LOW),
            vmem((heads, rows, DQK), LOW),
        ]
        + [vmem((heads, BLOCK, w), LOW) for w in widths]
        + [vmem((heads, BLOCK, w), FULL) for w in widths]
        + [
            vmem((rows, narrow), FULL),
            vmem((heads, rows, 1), FULL),
            vmem((BLOCK, narrow), FULL),
            vmem((heads, rows - BLOCK, DV), FULL),
            vmem((heads, rows - BLOCK, DQK), FULL),
            vmem((rows, 1), FULL),
            vmem((rows, 1), FULL),
            vmem((4, rows, half // 4), LOW),
            vmem((4, rows, half // 4), LOW),
            vmem((4, rows, half // 4), LOW),
            vmem((rows, 128), FULL),
            vmem((rows, 128), FULL),
            vmem((4, half, BLOCK), LOW),
            vmem((rows, narrow), LOW),
            vmem((8, 3, 128, PIECE), LOW),
            vmem((8, 3, 128, PIECE), LOW),
            vmem((4, 128, PIECE), LOW),
            vmem((4, 128, PIECE), LOW),
            thirds, pieces, thirds, pieces, pieces, pieces,
            pltpu.SMEM(moved.shape, jnp.int32),
            vmem((1, rows), jnp.int32),
            vmem((1, 2 * half), FULL),
            vmem((128, wide), FULL),
            vmem((narrow, 128), FULL),
            vmem((4, rows, half // 4), LOW),
            dma((7,)), dma((16,)), dma((16,)), dma((4,)), dma((4,)), dma((16,)), dma((16,)),
            dma((5,)), dma((5,)), dma((4,)), dma((4,)), dma((4, 4)), dma((4, 4)), dma((8, 3)), dma((8, 3)),
            dma((4,)), dma((4,)), dma((4, 3)), dma((4, 3)), dma((4, 4)), dma((4, 4)), dma((4, 4)),
            dma((8,)),
        ],
        compiler_params=pltpu.CompilerParams(
            collective_id=0, has_side_effects=True, vmem_limit_bytes=62 * 1024 * 1024
        ),
    )(inputs, grad_moved, moved, segments[None, :], gain[None, :], proj_in, proj_out)
    return finished(grad, gin, gout)


def on_device(inputs, grad_moved, moved, segments, input_norm_gain, proj_in, proj_out):
    rows = inputs.shape[0]
    span = 2 * DV + 2 * DQK
    heads_here = proj_in.shape[1] // span
    if lax.axis_size("mp") == 2 and lax.axis_size("dp") == 16:
        return fused(inputs, grad_moved, moved, segments, input_norm_gain, proj_in, proj_out)
    top_bit = lax.axis_size("dp").bit_length() - 2
    blocks = rows // BLOCK
    mine = [grad_moved[j * BLOCK : (j + 1) * BLOCK] for j in range(blocks)]
    theirs = [swapped(block, "dp", top_bit) for block in mine]
    full_x = gathered(inputs)
    full_dy = jnp.concatenate(
        [gathered(jnp.where(moved[0, j] == 1, theirs[j], mine[j])) for j in range(blocks)], axis=0
    )
    xfull = full_x.astype(jnp.float32)
    mean_shifted = xfull - jnp.mean(xfull, axis=1, keepdims=True)
    inverse_deviation = lax.rsqrt(
        jnp.mean(mean_shifted * mean_shifted, axis=1, keepdims=True) + epsilon
    )
    standardized_input = mean_shifted * inverse_deviation
    normalized_rows = (standardized_input * input_norm_gain[None, :]).astype(jnp.bfloat16)
    pre = jnp.dot(normalized_rows, proj_in, preferred_element_type=jnp.float32)
    sig_p = jax.nn.sigmoid(pre)
    acts = (pre * sig_p).astype(jnp.bfloat16)
    grad_mix = lax.dot_general(
        full_dy, proj_out, (((1,), (1,)), ((), ())), preferred_element_type=jnp.float32
    )
    order = jnp.arange(rows, dtype=jnp.int32)
    visible = (
        (segments[:, None] == segments[None, :]) & (order[None, :] <= order[:, None])
    ).astype(jnp.float32)
    mixed, saved = forward_heads(acts, visible, heads_here)
    grad_act = backward_heads(saved, grad_mix, visible, heads_here)
    grad_pre = (grad_act * sig_p * (1.0 + pre * (1.0 - sig_p))).astype(jnp.bfloat16)
    local = inputs.shape[1]
    offset = lax.axis_index("mp") * local
    normed_term = lax.dot_general(
        grad_pre, proj_in, (((1,), (1,)), ((), ())), preferred_element_type=jnp.float32
    ).astype(jnp.bfloat16)
    term_scaled = normed_term.astype(jnp.float32) * input_norm_gain[None, :]
    sums = jnp.stack([jnp.sum(term_scaled, axis=1), jnp.sum(term_scaled * standardized_input, axis=1)])
    partial_out = lax.dot_general(
        mixed, full_dy, (((0,), (0,)), ((), ())), preferred_element_type=jnp.float32
    )
    grad_proj_out = lax.psum_scatter(
        partial_out.astype(jnp.bfloat16), "dp", scatter_dimension=1, tiled=True
    ).astype(jnp.float32)
    partial_in = lax.dot_general(
        normalized_rows, grad_pre, (((0,), (0,)), ((), ())), preferred_element_type=jnp.float32
    )
    grad_proj_in = lax.psum_scatter(
        partial_in.astype(jnp.bfloat16), "dp", scatter_dimension=0, tiled=True
    ).astype(jnp.float32)
    sums = lax.psum(sums, "mp")
    grad_normed = lax.psum_scatter(
        normed_term, "mp", scatter_dimension=1, tiled=True
    ).astype(jnp.float32)
    means = sums / standardized_input.shape[1]
    here = lambda array: lax.dynamic_slice_in_dim(array, offset, local, 1)
    grad_here = here(full_dy).astype(jnp.float32) + inverse_deviation * (
        grad_normed * here(input_norm_gain[None, :])
        - means[0][:, None]
        - here(standardized_input) * means[1][:, None]
    )
    input_gradient = grad_here.astype(jnp.bfloat16)
    return (input_gradient, grad_proj_in, grad_proj_out)


def solution(mesh):
    return jax.shard_map(
        on_device,
        mesh=mesh,
        in_specs=(
            P("dp", "mp"),
            P("dp", "mp"),
            P("dp", None),
            P("dp"),
            P(),
            P(None, "mp"),
            P("mp", None),
        ),
        out_specs=(P("dp", "mp"), P("dp", "mp"), P("mp", "dp")),
        check_vma=False,
    )
```

```python
import jax
import jax.numpy as jnp
from jax import lax
from jax.experimental import pallas as pl
from jax.experimental.pallas import tpu as pltpu
from jax.sharding import PartitionSpec as P

DV = 128
DQK = 64
BLOCK = 128


epsilon = 1e-05
head_floor = 1.0


def swapped(block, axis, apart):
    count = lax.axis_size(axis)
    route = []
    for low in range(count):
        high = low | 1 << apart
        if high != low and high < count:
            route += [(low, high), (high, low)]
    return lax.ppermute(block, axis, route)


def gathered(block):
    return lax.all_gather(block, "mp", axis=1, tiled=True)


def forward_heads(acts, visible, heads_here):
    span = 2 * DV + 2 * DQK
    rows = acts.shape[0]
    parts = acts.reshape(rows, heads_here, span)
    u_vals = parts[:, :, :DV]
    v_vals = parts[:, :, DV : 2 * DV]
    q_vals = parts[:, :, 2 * DV : 2 * DV + DQK]
    k_vals = parts[:, :, 2 * DV + DQK :]
    scores = jnp.einsum("qhd,khd->hqk", q_vals, k_vals, preferred_element_type=jnp.float32)
    sig_s = jax.nn.sigmoid(scores)
    attend = (scores * sig_s * visible[None]).astype(jnp.bfloat16)
    slope = sig_s * (1.0 + scores * (1.0 - sig_s))
    outvals = jnp.einsum("hqk,khd->qhd", attend, v_vals, preferred_element_type=jnp.float32)
    mean_shifted = outvals - jnp.mean(outvals, axis=-1, keepdims=True)
    head_inv = lax.rsqrt(jnp.mean(mean_shifted * mean_shifted, axis=-1, keepdims=True) + head_floor)
    onorm = mean_shifted * head_inv
    mixed = (onorm * u_vals).astype(jnp.bfloat16).reshape(rows, heads_here * DV)
    saved = (u_vals, v_vals, q_vals, k_vals, attend, slope, onorm, head_inv)
    return (mixed, saved)


def backward_heads(saved, grad_mix, visible, heads_here):
    u_vals, v_vals, q_vals, k_vals, attend, slope, onorm, head_inv = saved
    rows = grad_mix.shape[0]
    grad_mixr = grad_mix.reshape(rows, heads_here, DV)
    grad_u = grad_mixr * onorm
    gon = grad_mixr * u_vals
    grad_o = (
        head_inv
        * (
            gon
            - jnp.mean(gon, axis=-1, keepdims=True)
            - onorm * jnp.mean(gon * onorm, axis=-1, keepdims=True)
        )
    ).astype(jnp.bfloat16)
    grad_att = jnp.einsum("qhd,khd->hqk", grad_o, v_vals, preferred_element_type=jnp.float32)
    grad_v = jnp.einsum("hqk,qhd->khd", attend, grad_o, preferred_element_type=jnp.float32)
    grad_scores = (grad_att * visible[None] * slope).astype(jnp.bfloat16)
    grad_q = jnp.einsum("hqk,khd->qhd", grad_scores, k_vals, preferred_element_type=jnp.float32)
    grad_k = jnp.einsum("hqk,qhd->khd", grad_scores, q_vals, preferred_element_type=jnp.float32)
    grad_act = jnp.concatenate([grad_u, grad_v, grad_q, grad_k], axis=-1)
    return grad_act.reshape(rows, heads_here * (2 * DV + 2 * DQK))


MESH = pl.DeviceIdType.MESH
SPAN = 2 * DV + 2 * DQK
PIECE = 512
STRIP = 32
LOW, FULL = jnp.bfloat16, jnp.float32


def dot(a, b, i, j):
    return lax.dot_general(a, b, (((i,), (j,)), ((), ())), preferred_element_type=FULL)


def fused_kernel(
    x_hbm, g_hbm, moved_hbm, seg_hbm, gain_hbm, win_hbm, wout_hbm,
    gin_hbm, gout_hbm, grad_hbm,
    x2, own_g, land_z, dy2, w_in, w_out, norm_t, dy_t, rhs, mixed, slope_p, u_all, v_all, q_all, k_all,
    att0, att1, att2, att3, slo0, slo1, slo2, slo3, onorm_ref, hinv_ref, gm_ref, gv_acc, gk_acc,
    mean_ref, inv_ref, land_t, send_t, own_t, land_s, send_s, side_t, mixed_y,
    send_c, recv_c, send_g, recv_g, send_y, keep_y, recv_y, send_z, from_low, from_high,
    pair_ref, moved_ref, seg_ref, gain_ref, gin_ref, gout_ref, grad_ref,
    sem_local, sem_zs, sem_zr, sem_xs, sem_xr, sem_ds, sem_dr, sem_ts, sem_tr, sem_ms, sem_mr,
    sem_os, sem_or, sem_cs, sem_cr, sem_gs, sem_gr, sem_ys, sem_yr, sem_fs, sem_low, sem_high,
    sem_out,
):
    heads = u_all.shape[0]
    half = x_hbm.shape[1]
    wide = heads * SPAN
    attends = (att0, att1, att2, att3)
    slopes = (slo0, slo1, slo2, slo3)
    d = lax.axis_index("dp")
    x = lax.axis_index("mp")
    z = d // 4
    y = (d // 2) % 2
    c = d % 2
    upper = z // 2
    inner = (z + upper) % 2
    core_peer = d + 1 - 2 * c
    y_peer = d + 2 - 4 * y
    partner = (d + 8) % 16

    barrier = pltpu.get_barrier_semaphore()

    def greet(where):
        pl.semaphore_signal(barrier, inc=1, device_id=where, device_id_type=MESH)

    greet({"dp": partner})
    greet({"mp": 1 - x})
    greet({"dp": core_peer})
    greet({"dp": y_peer})

    @pl.when(z > 0)
    def _():
        greet({"dp": d - 4})

    @pl.when(z < 3)
    def _():
        greet({"dp": d + 4})

    def local(i, src, dst):
        return pltpu.make_async_copy(src, dst, sem_local.at[i])

    local_x = local(0, x_hbm, x2.at[x])
    local_win = local(1, win_hbm, w_in)
    local_g = local(2, g_hbm, own_g)
    local_wout = local(3, wout_hbm, w_out)
    local_gain = local(4, gain_hbm, gain_ref)
    local_seg = local(5, seg_hbm, seg_ref)
    local_moved = local(6, moved_hbm, moved_ref)
    local_x.start()
    local_gain.start()
    local_win.start()
    local_seg.start()
    local_moved.start()
    local_g.start()
    local_wout.start()

    pl.semaphore_wait(barrier, 4 + (z + 3) // 4 + (6 - z) // 4)

    def remote(src, dst, send_sem, recv_sem, where):
        return pltpu.make_async_remote_copy(
            src_ref=src, dst_ref=dst, send_sem=send_sem, recv_sem=recv_sem,
            device_id=where, device_id_type=MESH,
        )

    def rows_of(j):
        return pl.ds(pl.multiple_of(j * BLOCK, BLOCK), BLOCK)

    def short(i):
        return pl.ds(pl.multiple_of(i * STRIP, STRIP), STRIP)

    def swap(i):
        return remote(
            g_hbm.at[short(i)], land_z.at[short(i)], sem_zs.at[i], sem_zr.at[i], {"dp": partner}
        )

    def share_x(j):
        return remote(
            x_hbm.at[rows_of(j)], x2.at[x, rows_of(j)], sem_xs.at[j], sem_xr.at[j], {"mp": 1 - x}
        )

    def share_dy(i):
        return remote(
            dy2.at[x, short(i)], dy2.at[x, short(i)], sem_ds.at[i], sem_dr.at[i], {"mp": 1 - x}
        )

    def cross_t(i):
        return remote(send_t.at[i], land_t.at[i], sem_ts.at[i], sem_tr.at[i], {"mp": 1 - x})

    def share_mixed(j):
        return remote(
            mixed.at[rows_of(j)], mixed_y.at[rows_of(j)], sem_ms.at[j], sem_mr.at[j],
            {"dp": y_peer},
        )

    def share_turned(q, j):
        there = pl.ds(pl.multiple_of((2 * q + 1 - y) * 256, 256), 256)
        landing = pl.ds(pl.multiple_of(q * 256, 256), 256)
        return remote(
            dy_t.at[j, there], side_t.at[j, landing],
            sem_os.at[q, j], sem_or.at[q, j], {"dp": y_peer},
        )

    cross_s = remote(send_s, land_s, sem_ts.at[4], sem_tr.at[4], {"mp": 1 - x})

    def begin_swap(i, carry):
        swap(15 - i).start()
        return carry

    def begin_share(j, carry):
        share_x(j).start()
        return carry

    lax.fori_loop(0, 16, begin_swap, 0)
    lax.fori_loop(0, 4, begin_share, 0)

    def arrive(j):
        rows = rows_of(j)
        share_x(j).wait_recv()
        first = x2[0, rows, :].astype(FULL)
        second = x2[1, rows, :].astype(FULL)
        total = jnp.sum(first, axis=1, keepdims=True) + jnp.sum(second, axis=1, keepdims=True)
        mean = total * (1.0 / (2 * half))
        first = first - mean
        second = second - mean
        square = jnp.sum(first * first, axis=1, keepdims=True) + jnp.sum(
            second * second, axis=1, keepdims=True
        )
        inverse = lax.rsqrt(square * (1.0 / (2 * half)) + epsilon)
        mean_ref[rows, :] = mean
        inv_ref[rows, :] = inverse
        n0 = (first * inverse * gain_ref[:, :half]).astype(LOW)
        n1 = (second * inverse * gain_ref[:, half:]).astype(LOW)
        norm_t[:half, rows] = n0.T
        norm_t[half:, rows] = n1.T
        for h in range(heads):
            cols = slice(h * SPAN, (h + 1) * SPAN)
            pre = dot(n0, w_in[:half, cols], 1, 0) + dot(n1, w_in[half:, cols], 1, 0)
            sig = jax.nn.sigmoid(pre)
            act = (pre * sig).astype(LOW)
            slope_p[rows, cols] = sig * (1.0 + pre * (1.0 - sig))
            u_all[h, rows, :] = act[:, :DV]
            v_all[h, rows, :] = act[:, DV : 2 * DV]
            q_all[h, rows, :] = act[:, 2 * DV : 2 * DV + DQK]
            k_all[h, rows, :] = act[:, 2 * DV + DQK :]

    def forward(j):
        rows = slice(j * BLOCK, (j + 1) * BLOCK)
        w = (j + 1) * BLOCK
        seg = seg_ref[:, :w].astype(FULL)
        mine = jnp.broadcast_to(seg[:, j * BLOCK :], (BLOCK, BLOCK)).T
        row = lax.broadcasted_iota(jnp.int32, (BLOCK, w), 0) + j * BLOCK
        col = lax.broadcasted_iota(jnp.int32, (BLOCK, w), 1)
        same = jnp.concatenate([mine] * (j + 1), axis=1) == seg
        visible = jnp.where(same & (col <= row), 1.0, 0.0)

        def head(h, carry):
            scores = dot(q_all[h, rows, :], k_all[h, :w, :], 1, 1)
            sig = jax.nn.sigmoid(scores)
            attend = (scores * sig * visible).astype(LOW)
            attends[j][h] = attend
            slopes[j][h] = sig * (1.0 + scores * (1.0 - sig)) * visible
            outvals = dot(attend, v_all[h, :w, :], 1, 0)
            shifted = outvals - jnp.mean(outvals, axis=1, keepdims=True)
            inverse = lax.rsqrt(jnp.mean(shifted * shifted, axis=1, keepdims=True) + head_floor)
            onorm = shifted * inverse
            hinv_ref[h, rows, :] = inverse
            onorm_ref[rows, h * DV : (h + 1) * DV] = onorm
            mixed[rows, h * DV : (h + 1) * DV] = (onorm * u_all[h, rows, :].astype(FULL)).astype(LOW)
            return carry

        for h in range(heads):
            head(h, 0)
        share_mixed(j).start()

    def side_of(side):
        return pl.ds(pl.multiple_of(side * half, half), half)

    def turn(j, side):
        rows = slice(j * BLOCK, (j + 1) * BLOCK)
        dy_t[j, side_of(side), :] = dy2[side, rows, :].T
        share_turned(2 * side, j).start()
        share_turned(2 * side + 1, j).start()

    def relay(i):
        rows = slice(i * STRIP, (i + 1) * STRIP)
        swap(i).wait_recv()
        flags = jnp.full((STRIP, half), moved_ref[0, i // 4], jnp.int32)
        dy2[x, rows, :] = jnp.where(
            flags == 1, land_z[rows, :].astype(FULL), own_g[rows, :].astype(FULL)
        ).astype(LOW)
        share_dy(i).start()
        if i % 4 == 0:
            turn(i // 4, x)

    def backward(j):
        rows = slice(j * BLOCK, (j + 1) * BLOCK)
        w = (j + 1) * BLOCK
        for i in range(4):
            share_dy(4 * j + i).wait_recv()
        turn(j, 1 - x)
        d0, d1 = dy2[0, rows, :], dy2[1, rows, :]
        gm_ref[...] = dot(d0, w_out[:, :half], 1, 1) + dot(d1, w_out[:, half:], 1, 1)

        def head(h, carry):
            mix_at = slice(h * DV, (h + 1) * DV)
            u_at = slice(h * SPAN, h * SPAN + DV)
            v_at = slice(h * SPAN + DV, h * SPAN + 2 * DV)
            qk_at = slice(h * SPAN + 2 * DV, (h + 1) * SPAN)
            onorm = onorm_ref[rows, mix_at]
            mix = gm_ref[:, mix_at]
            gon = mix * u_all[h, rows, :].astype(FULL)
            grad_o = (
                hinv_ref[h, rows, :]
                * (
                    gon
                    - jnp.mean(gon, axis=1, keepdims=True)
                    - onorm * jnp.mean(gon * onorm, axis=1, keepdims=True)
                )
            ).astype(LOW)
            rhs[rows, u_at] = (mix * onorm * slope_p[rows, u_at]).astype(LOW)
            grad_s = (dot(grad_o, v_all[h, :w, :], 1, 1) * slopes[j][h]).astype(LOW)
            grad_v = dot(attends[j][h], grad_o, 0, 0)
            grad_k = dot(grad_s, q_all[h, rows, :], 0, 0)
            if j < 3:
                grad_v = grad_v + gv_acc[h, :w, :]
                grad_k = grad_k + gk_acc[h, :w, :]
            if j > 0:
                gv_acc[h, : j * BLOCK, :] = grad_v[: j * BLOCK]
                gk_acc[h, : j * BLOCK, :] = grad_k[: j * BLOCK]
            rhs[rows, v_at] = (grad_v[j * BLOCK :] * slope_p[rows, v_at]).astype(LOW)
            grad_qk = jnp.concatenate(
                [dot(grad_s, k_all[h, :w, :], 1, 0), grad_k[j * BLOCK :]], axis=1
            )
            rhs[rows, qk_at] = (grad_qk * slope_p[rows, qk_at]).astype(LOW)
            return carry

        for h in range(heads):
            head(h, 0)

    tile = 256

    def tile_of(side, i):
        return pl.ds(pl.multiple_of(side * half + i * tile, tile), tile)

    def inside(i):
        return pl.ds(pl.multiple_of(i * tile, tile), tile)

    def standard(side, i):
        return (x2[side, :, inside(i)].astype(FULL) - mean_ref[...]) * inv_ref[...]

    def term(side, i):
        part = dot(rhs[...], w_in[tile_of(side, i), :], 1, 1).astype(LOW)
        scaled = part.astype(FULL) * gain_ref[:, tile_of(side, i)]
        first = jnp.sum(scaled, axis=1, keepdims=True)
        second = jnp.sum(scaled * standard(side, i), axis=1, keepdims=True)
        lane = lax.broadcasted_iota(jnp.int32, send_s.shape, 1)
        return part, jnp.where(lane == 0, first, second)

    def term_away(i, carry):
        part, sums = term(1 - x, i)
        send_t[i] = part
        cross_t(i).start()
        send_s[...] = sums + send_s[...]
        return carry

    def term_kept(i, carry):
        part, sums = term(x, i)
        own_t[i] = part
        send_s[...] = sums + send_s[...]
        return carry

    def store_grad(i):
        return pltpu.make_async_copy(
            grad_ref.at[i], grad_hbm.at[:, inside(i)], sem_out.at[i]
        )

    def gradient(i, carry):
        cross_t(i).wait_recv()
        means = (send_s[...] + land_s[...]) * (1.0 / (2 * half))
        normed_grad = own_t[i].astype(FULL) + land_t[i].astype(FULL)
        grad_ref[i] = (
            dy2[x, :, inside(i)].astype(FULL)
            + inv_ref[...]
            * (
                normed_grad * gain_ref[:, tile_of(x, i)]
                - means[:, 0:1]
                - standard(x, i) * means[:, 1:2]
            )
        ).astype(LOW)
        store_grad(i).start()
        cross_t(i).wait_send()
        return carry

    def target(k):
        v = (3 - k) + (k // 2) * inner * (2 * k - 5)
        return (1 - upper) * v + upper * (3 - v)

    def product(k, side, p):
        pair = pl.ds(pl.multiple_of((target(k) * 2 + side) * 256, 256), 256)
        both = dot(norm_t[pair, :], rhs[:, pl.ds(pl.multiple_of(p * PIECE, PIECE), PIECE)], 1, 0)
        pair_ref[p] = both

    def to_core(slot, p):
        return remote(
            send_c.at[slot, p], recv_c.at[slot, p], sem_cs.at[slot, p], sem_cr.at[slot, p],
            {"dp": core_peer},
        )

    def to_y(k, p):
        return remote(
            send_y.at[k, p], recv_y.at[k, p], sem_ys.at[k, p], sem_yr.at[k, p], {"dp": y_peer}
        )

    def up(k, t, p):
        return remote(
            send_z.at[k, p], from_low.at[t, p], sem_fs.at[k, p], sem_low.at[t, p], {"dp": d + 4}
        )

    def down(k, t, p):
        return remote(
            send_z.at[k, p], from_high.at[t, p], sem_fs.at[k, p], sem_high.at[t, p], {"dp": d - 4}
        )

    def away(k):
        def issue(p, carry):
            product(k, 1 - y, p)
            send_c[k, p] = pair_ref[p, rows_of(1 - c), :].astype(LOW)
            to_core(k, p).start()
            return carry

        def finish(p, carry):
            mine = pair_ref[p, rows_of(c), :]
            to_core(k, p).wait_recv()
            send_y[k, p] = (mine + recv_c[k, p].astype(FULL)).astype(LOW)
            to_y(k, p).start()
            return carry

        lax.fori_loop(0, 3, issue, 0)
        lax.fori_loop(0, 3, finish, 0)

    def keep(k):
        def issue(p, carry):
            product(k, y, p)
            send_c[k + 4, p] = pair_ref[p, rows_of(1 - c), :].astype(LOW)
            to_core(k + 4, p).start()
            return carry

        def finish(p, carry):
            mine = pair_ref[p, rows_of(c), :]
            to_core(k + 4, p).wait_recv()
            keep_y[k, p] = (mine + recv_c[k + 4, p].astype(FULL)).astype(LOW)
            return carry

        lax.fori_loop(0, 3, issue, 0)
        lax.fori_loop(0, 3, finish, 0)

    def out_product(k, core):
        chunk = target(k) * 4 + y * 2 + core
        other = target(k) * 2 + core
        mine = jnp.concatenate([dy_t[j, rows_of(chunk), :] for j in range(4)], axis=1)
        theirs = jnp.concatenate([side_t[j, rows_of(other), :] for j in range(4)], axis=1)
        return dot(mine, mixed[...], 1, 0) + dot(theirs, mixed_y[...], 1, 0)

    def out_core(k):
        return remote(
            send_g.at[k], recv_g.at[k], sem_gs.at[k], sem_gr.at[k], {"dp": core_peer}
        )

    def out_issue(k, carry):
        send_g[k] = out_product(k, 1 - c).astype(LOW)
        out_core(k).start()
        return carry

    def out_finish(k, carry):
        mine = out_product(k, c)
        out_core(k).wait_recv()
        keep_y[k, 3] = (mine + recv_g[k].astype(FULL)).astype(LOW)
        return carry

    def here(k, p, with_y):
        if with_y:
            to_y(k, p).wait_recv()
            return keep_y[k, p].astype(FULL) + recv_y[k, p].astype(FULL)
        return keep_y[k, p].astype(FULL)

    def end(k, p, with_y=True):
        @pl.when((z == 0) | (z == 3))
        def _():
            t = target(k)
            send_z[k, p] = here(k, p, with_y).astype(LOW)

            @pl.when(t > z)
            def _():
                up(k, t, p).start()

            @pl.when(t < z)
            def _():
                down(k, t, p).start()

    def mid(k, p, with_y=True):
        @pl.when((z == 1) | (z == 2))
        def _():
            t = target(k)
            part = here(k, p, with_y)

            @pl.when(t > z)
            def _():
                pltpu.make_async_copy(from_low.at[t, p], from_low.at[t, p], sem_low.at[t, p]).wait()
                send_z[k, p] = (part + from_low[t, p].astype(FULL)).astype(LOW)
                up(k, t, p).start()

            @pl.when(t < z)
            def _():
                pltpu.make_async_copy(from_high.at[t, p], from_high.at[t, p], sem_high.at[t, p]).wait()
                send_z[k, p] = (part + from_high[t, p].astype(FULL)).astype(LOW)
                down(k, t, p).start()

    def ends(k):
        def piece(p, carry):
            end(k, p)
            return carry

        lax.fori_loop(0, 3, piece, 0)

    def mids(k):
        def piece(p, carry):
            mid(k, p)
            return carry

        lax.fori_loop(0, 3, piece, 0)

    send_s[...] = jnp.zeros_like(send_s)
    local_x.wait()
    local_gain.wait()
    local_win.wait()
    arrive(0)
    local_g.wait()
    local_moved.wait()
    local_seg.wait()
    relay(15)
    forward(0)
    relay(14)
    arrive(1)
    relay(13)
    forward(1)
    relay(12)
    arrive(2)
    relay(11)
    forward(2)
    relay(10)
    arrive(3)
    relay(9)
    forward(3)
    relay(8)
    local_wout.wait()
    backward(3)
    relay(7)
    backward(2)
    relay(6)
    relay(5)
    relay(4)
    relay(3)
    backward(1)
    relay(2)
    relay(1)
    relay(0)
    backward(0)

    away(0)

    def mixed_here(j, carry):
        share_mixed(j).wait_recv()
        return carry

    def operands_here(i, carry):
        share_turned(i // 4, i % 4).wait_recv()
        return carry

    lax.fori_loop(0, 4, mixed_here, 0)
    lax.fori_loop(0, 16, operands_here, 0)
    lax.fori_loop(0, 4, out_issue, 0)
    lax.fori_loop(0, 4, out_finish, 0)
    for k in range(3):
        end(k, 3, False)
    keep(0)
    away(1)
    lax.fori_loop(0, 4, term_away, 0)
    ends(0)
    mid(0, 3, False)
    mid(1, 3, False)
    keep(1)
    away(2)
    mid(2, 3, False)
    keep(2)
    away(3)
    keep(3)
    ends(1)
    mid(0, 0)
    lax.fori_loop(0, 4, term_kept, 0)
    cross_s.start()
    mid(0, 1)
    mid(0, 2)

    def interior(p, carry):
        mid(1, p)
        mid(2, p)
        return carry

    lax.fori_loop(0, 3, interior, 0)
    ends(2)
    cross_s.wait()
    lax.fori_loop(0, 4, gradient, 0)

    total = gm_ref

    def gather_total(p, with_y):
        if with_y:
            to_y(3, p).wait_recv()
            total[...] = keep_y[3, p].astype(FULL) + recv_y[3, p].astype(FULL)
        else:
            total[...] = keep_y[3, p].astype(FULL)

        @pl.when(z > 0)
        def _():
            pltpu.make_async_copy(from_low.at[z, p], from_low.at[z, p], sem_low.at[z, p]).wait()
            total[...] += from_low[z, p].astype(FULL)

        @pl.when(z < 3)
        def _():
            pltpu.make_async_copy(from_high.at[z, p], from_high.at[z, p], sem_high.at[z, p]).wait()
            total[...] += from_high[z, p].astype(FULL)

    def store_in(p):
        cols = pl.ds(p * PIECE, PIECE)
        return pltpu.make_async_copy(gin_ref.at[:, cols], gin_hbm.at[:, cols], sem_out.at[4 + p])

    store_out = pltpu.make_async_copy(gout_ref, gout_hbm, sem_out.at[7])

    gather_total(3, False)
    gout_ref[...] = total[...].T
    store_out.start()
    for p in range(3):
        gather_total(p, True)
        gin_ref[:, p * PIECE : (p + 1) * PIECE] = total[...]
        store_in(p).start()

    def drain_swap(i, carry):
        swap(i).wait_send()
        share_dy(i).wait_send()
        return carry

    lax.fori_loop(0, 16, drain_swap, 0)

    def drain_share(j, carry):
        share_x(j).wait_send()
        out_core(j).wait_send()
        share_mixed(j).wait_send()
        store_grad(j).wait()
        for q in range(4):
            share_turned(q, j).wait_send()
        return carry

    lax.fori_loop(0, 4, drain_share, 0)

    def drain_core(i, carry):
        to_core(i // 3, i % 3).wait_send()
        return carry

    lax.fori_loop(0, 24, drain_core, 0)

    def drain_far(i, carry):
        k, p = i // 4, i % 4
        t = target(k)

        @pl.when(p < 3)
        def _():
            to_y(k, p).wait_send()

        @pl.when(t > z)
        def _():
            up(k, t, p).wait_send()

        @pl.when(t < z)
        def _():
            down(k, t, p).wait_send()

        return carry

    lax.fori_loop(0, 16, drain_far, 0)
    for p in range(3):
        store_in(p).wait()
    store_out.wait()


def finish_kernel(grad, gin, gout, grad_out, gin_out, gout_out, b_grad, b_gin, b_gout, sems):
    steps = []
    for source, staged, result, parts in (
        (grad, b_grad, grad_out, 4), (gin, b_gin, gin_out, 2), (gout, b_gout, gout_out, 1),
    ):
        size = source.shape[0] // parts
        for i in range(parts):
            at = pl.ds(i * size, size)
            n = len(steps)
            steps.append((
                pltpu.make_async_copy(source.at[at], staged.at[at], sems.at[0, n]),
                pltpu.make_async_copy(staged.at[at], result.at[at], sems.at[1, n]),
            ))
    for fetch, _ in steps:
        fetch.start()
    for fetch, store in steps:
        fetch.wait()
        store.start()
    for _, store in steps:
        store.wait()


def finished(*arrays):
    anywhere = pl.BlockSpec(memory_space=pl.ANY)
    return pl.pallas_call(
        finish_kernel,
        out_shape=tuple(jax.ShapeDtypeStruct(a.shape, a.dtype) for a in arrays),
        in_specs=[anywhere] * len(arrays),
        out_specs=[anywhere] * len(arrays),
        scratch_shapes=[pltpu.VMEM(a.shape, a.dtype) for a in arrays]
        + [pltpu.SemaphoreType.DMA((2, 7))],
    )(*arrays)


def fused(inputs, grad_moved, moved, segments, gain, proj_in, proj_out):
    rows, half = inputs.shape
    wide, narrow = proj_in.shape[1], proj_out.shape[0]
    heads = wide // SPAN
    vmem, dma = pltpu.VMEM, pltpu.SemaphoreType.DMA
    anywhere = pl.BlockSpec(memory_space=pl.ANY)
    pieces = vmem((4, 4, 128, PIECE), LOW)
    thirds = vmem((4, 3, 128, PIECE), LOW)
    widths = [(j + 1) * BLOCK for j in range(rows // BLOCK)]
    gin, gout, grad = pl.pallas_call(
        fused_kernel,
        out_shape=(
            jax.ShapeDtypeStruct((128, wide), FULL),
            jax.ShapeDtypeStruct((narrow, 128), FULL),
            jax.ShapeDtypeStruct((rows, half), LOW),
        ),
        in_specs=[anywhere] * 7,
        out_specs=[anywhere] * 3,
        scratch_shapes=[
            vmem((2, rows, half), LOW),
            vmem((rows, half), LOW),
            vmem((rows, half), LOW),
            vmem((2, rows, half), LOW),
            vmem(proj_in.shape, LOW),
            vmem(proj_out.shape, LOW),
            vmem((2 * half, rows), LOW),
            vmem((4, 2 * half, BLOCK), LOW),
            vmem((rows, wide), LOW),
            vmem((rows, narrow), LOW),
            vmem((rows, wide), FULL),
            vmem((heads, rows, DV), LOW),
            vmem((heads, rows, DV), LOW),
            vmem((heads, rows, DQK), LOW),
            vmem((heads, rows, DQK), LOW),
        ]
        + [vmem((heads, BLOCK, w), LOW) for w in widths]
        + [vmem((heads, BLOCK, w), FULL) for w in widths]
        + [
            vmem((rows, narrow), FULL),
            vmem((heads, rows, 1), FULL),
            vmem((BLOCK, narrow), FULL),
            vmem((heads, rows - BLOCK, DV), FULL),
            vmem((heads, rows - BLOCK, DQK), FULL),
            vmem((rows, 1), FULL),
            vmem((rows, 1), FULL),
            vmem((4, rows, half // 4), LOW),
            vmem((4, rows, half // 4), LOW),
            vmem((4, rows, half // 4), LOW),
            vmem((rows, 128), FULL),
            vmem((rows, 128), FULL),
            vmem((4, half, BLOCK), LOW),
            vmem((rows, narrow), LOW),
            vmem((8, 3, 128, PIECE), LOW),
            vmem((8, 3, 128, PIECE), LOW),
            vmem((4, 128, PIECE), LOW),
            vmem((4, 128, PIECE), LOW),
            thirds, pieces, thirds, pieces, pieces, pieces,
            vmem((3, 256, PIECE), FULL),
            pltpu.SMEM(moved.shape, jnp.int32),
            vmem((1, rows), jnp.int32),
            vmem((1, 2 * half), FULL),
            vmem((128, wide), FULL),
            vmem((narrow, 128), FULL),
            vmem((4, rows, half // 4), LOW),
            dma((7,)), dma((16,)), dma((16,)), dma((4,)), dma((4,)), dma((16,)), dma((16,)),
            dma((5,)), dma((5,)), dma((4,)), dma((4,)), dma((4, 4)), dma((4, 4)), dma((8, 3)), dma((8, 3)),
            dma((4,)), dma((4,)), dma((4, 3)), dma((4, 3)), dma((4, 4)), dma((4, 4)), dma((4, 4)),
            dma((8,)),
        ],
        compiler_params=pltpu.CompilerParams(
            collective_id=0, has_side_effects=True, vmem_limit_bytes=62 * 1024 * 1024
        ),
    )(inputs, grad_moved, moved, segments[None, :], gain[None, :], proj_in, proj_out)
    return finished(grad, gin, gout)


def on_device(inputs, grad_moved, moved, segments, input_norm_gain, proj_in, proj_out):
    rows = inputs.shape[0]
    span = 2 * DV + 2 * DQK
    heads_here = proj_in.shape[1] // span
    if lax.axis_size("mp") == 2 and lax.axis_size("dp") == 16:
        return fused(inputs, grad_moved, moved, segments, input_norm_gain, proj_in, proj_out)
    top_bit = lax.axis_size("dp").bit_length() - 2
    blocks = rows // BLOCK
    mine = [grad_moved[j * BLOCK : (j + 1) * BLOCK] for j in range(blocks)]
    theirs = [swapped(block, "dp", top_bit) for block in mine]
    full_x = gathered(inputs)
    full_dy = jnp.concatenate(
        [gathered(jnp.where(moved[0, j] == 1, theirs[j], mine[j])) for j in range(blocks)], axis=0
    )
    xfull = full_x.astype(jnp.float32)
    mean_shifted = xfull - jnp.mean(xfull, axis=1, keepdims=True)
    inverse_deviation = lax.rsqrt(
        jnp.mean(mean_shifted * mean_shifted, axis=1, keepdims=True) + epsilon
    )
    standardized_input = mean_shifted * inverse_deviation
    normalized_rows = (standardized_input * input_norm_gain[None, :]).astype(jnp.bfloat16)
    pre = jnp.dot(normalized_rows, proj_in, preferred_element_type=jnp.float32)
    sig_p = jax.nn.sigmoid(pre)
    acts = (pre * sig_p).astype(jnp.bfloat16)
    grad_mix = lax.dot_general(
        full_dy, proj_out, (((1,), (1,)), ((), ())), preferred_element_type=jnp.float32
    )
    order = jnp.arange(rows, dtype=jnp.int32)
    visible = (
        (segments[:, None] == segments[None, :]) & (order[None, :] <= order[:, None])
    ).astype(jnp.float32)
    mixed, saved = forward_heads(acts, visible, heads_here)
    grad_act = backward_heads(saved, grad_mix, visible, heads_here)
    grad_pre = (grad_act * sig_p * (1.0 + pre * (1.0 - sig_p))).astype(jnp.bfloat16)
    local = inputs.shape[1]
    offset = lax.axis_index("mp") * local
    normed_term = lax.dot_general(
        grad_pre, proj_in, (((1,), (1,)), ((), ())), preferred_element_type=jnp.float32
    ).astype(jnp.bfloat16)
    term_scaled = normed_term.astype(jnp.float32) * input_norm_gain[None, :]
    sums = jnp.stack([jnp.sum(term_scaled, axis=1), jnp.sum(term_scaled * standardized_input, axis=1)])
    partial_out = lax.dot_general(
        mixed, full_dy, (((0,), (0,)), ((), ())), preferred_element_type=jnp.float32
    )
    grad_proj_out = lax.psum_scatter(
        partial_out.astype(jnp.bfloat16), "dp", scatter_dimension=1, tiled=True
    ).astype(jnp.float32)
    partial_in = lax.dot_general(
        normalized_rows, grad_pre, (((0,), (0,)), ((), ())), preferred_element_type=jnp.float32
    )
    grad_proj_in = lax.psum_scatter(
        partial_in.astype(jnp.bfloat16), "dp", scatter_dimension=0, tiled=True
    ).astype(jnp.float32)
    sums = lax.psum(sums, "mp")
    grad_normed = lax.psum_scatter(
        normed_term, "mp", scatter_dimension=1, tiled=True
    ).astype(jnp.float32)
    means = sums / standardized_input.shape[1]
    here = lambda array: lax.dynamic_slice_in_dim(array, offset, local, 1)
    grad_here = here(full_dy).astype(jnp.float32) + inverse_deviation * (
        grad_normed * here(input_norm_gain[None, :])
        - means[0][:, None]
        - here(standardized_input) * means[1][:, None]
    )
    input_gradient = grad_here.astype(jnp.bfloat16)
    return (input_gradient, grad_proj_in, grad_proj_out)


def solution(mesh):
    return jax.shard_map(
        on_device,
        mesh=mesh,
        in_specs=(
            P("dp", "mp"),
            P("dp", "mp"),
            P("dp", None),
            P("dp"),
            P(),
            P(None, "mp"),
            P("mp", None),
        ),
        out_specs=(P("dp", "mp"), P("dp", "mp"), P("mp", "dp")),
        check_vma=False,
    )
```

```python
import jax
import jax.numpy as jnp
from jax import lax
from jax.experimental import pallas as pl
from jax.experimental.pallas import tpu as pltpu
from jax.sharding import PartitionSpec as P

DV = 128
DQK = 64
BLOCK = 128


epsilon = 1e-05
head_floor = 1.0


def swapped(block, axis, apart):
    count = lax.axis_size(axis)
    route = []
    for low in range(count):
        high = low | 1 << apart
        if high != low and high < count:
            route += [(low, high), (high, low)]
    return lax.ppermute(block, axis, route)


def gathered(block):
    return lax.all_gather(block, "mp", axis=1, tiled=True)


def forward_heads(acts, visible, heads_here):
    span = 2 * DV + 2 * DQK
    rows = acts.shape[0]
    parts = acts.reshape(rows, heads_here, span)
    u_vals = parts[:, :, :DV]
    v_vals = parts[:, :, DV : 2 * DV]
    q_vals = parts[:, :, 2 * DV : 2 * DV + DQK]
    k_vals = parts[:, :, 2 * DV + DQK :]
    scores = jnp.einsum("qhd,khd->hqk", q_vals, k_vals, preferred_element_type=jnp.float32)
    sig_s = jax.nn.sigmoid(scores)
    attend = (scores * sig_s * visible[None]).astype(jnp.bfloat16)
    slope = sig_s * (1.0 + scores * (1.0 - sig_s))
    outvals = jnp.einsum("hqk,khd->qhd", attend, v_vals, preferred_element_type=jnp.float32)
    mean_shifted = outvals - jnp.mean(outvals, axis=-1, keepdims=True)
    head_inv = lax.rsqrt(jnp.mean(mean_shifted * mean_shifted, axis=-1, keepdims=True) + head_floor)
    onorm = mean_shifted * head_inv
    mixed = (onorm * u_vals).astype(jnp.bfloat16).reshape(rows, heads_here * DV)
    saved = (u_vals, v_vals, q_vals, k_vals, attend, slope, onorm, head_inv)
    return (mixed, saved)


def backward_heads(saved, grad_mix, visible, heads_here):
    u_vals, v_vals, q_vals, k_vals, attend, slope, onorm, head_inv = saved
    rows = grad_mix.shape[0]
    grad_mixr = grad_mix.reshape(rows, heads_here, DV)
    grad_u = grad_mixr * onorm
    gon = grad_mixr * u_vals
    grad_o = (
        head_inv
        * (
            gon
            - jnp.mean(gon, axis=-1, keepdims=True)
            - onorm * jnp.mean(gon * onorm, axis=-1, keepdims=True)
        )
    ).astype(jnp.bfloat16)
    grad_att = jnp.einsum("qhd,khd->hqk", grad_o, v_vals, preferred_element_type=jnp.float32)
    grad_v = jnp.einsum("hqk,qhd->khd", attend, grad_o, preferred_element_type=jnp.float32)
    grad_scores = (grad_att * visible[None] * slope).astype(jnp.bfloat16)
    grad_q = jnp.einsum("hqk,khd->qhd", grad_scores, k_vals, preferred_element_type=jnp.float32)
    grad_k = jnp.einsum("hqk,qhd->khd", grad_scores, q_vals, preferred_element_type=jnp.float32)
    grad_act = jnp.concatenate([grad_u, grad_v, grad_q, grad_k], axis=-1)
    return grad_act.reshape(rows, heads_here * (2 * DV + 2 * DQK))


MESH = pl.DeviceIdType.MESH
SPAN = 2 * DV + 2 * DQK
PIECE = 512
STRIP = 32
LOW, FULL = jnp.bfloat16, jnp.float32


def dot(a, b, i, j):
    return lax.dot_general(a, b, (((i,), (j,)), ((), ())), preferred_element_type=FULL)


def fused_kernel(
    x_hbm, g_hbm, moved_hbm, seg_hbm, gain_hbm, win_hbm, wout_hbm,
    gin_hbm, gout_hbm, grad_hbm,
    x2, own_g, land_z, dy2, w_in, w_out, norm_t, dy_t, rhs, mixed, slope_p, u_all, v_all, q_all, k_all,
    att0, att1, att2, att3, slo0, slo1, slo2, slo3, onorm_ref, hinv_ref, gm_ref, gv_acc, gk_acc,
    mean_ref, inv_ref, land_t, send_t, own_t, land_s, send_s, side_t, mixed_y,
    send_c, recv_c, send_g, recv_g, send_y, keep_y, recv_y, send_z, from_low, from_high,
    pair_ref, moved_ref, seg_ref, gain_ref, gin_ref, gout_ref, grad_ref,
    sem_local, sem_zs, sem_zr, sem_xs, sem_xr, sem_ds, sem_dr, sem_ts, sem_tr, sem_ms, sem_mr,
    sem_os, sem_or, sem_cs, sem_cr, sem_gs, sem_gr, sem_ys, sem_yr, sem_fs, sem_low, sem_high,
    sem_out,
):
    heads = u_all.shape[0]
    half = x_hbm.shape[1]
    wide = heads * SPAN
    attends = (att0, att1, att2, att3)
    slopes = (slo0, slo1, slo2, slo3)
    d = lax.axis_index("dp")
    x = lax.axis_index("mp")
    z = d // 4
    y = (d // 2) % 2
    c = d % 2
    upper = z // 2
    inner = (z + upper) % 2
    core_peer = d + 1 - 2 * c
    y_peer = d + 2 - 4 * y
    partner = (d + 8) % 16

    barrier = pltpu.get_barrier_semaphore()

    def greet(where):
        pl.semaphore_signal(barrier, inc=1, device_id=where, device_id_type=MESH)

    greet({"dp": partner})
    greet({"mp": 1 - x})
    greet({"dp": core_peer})
    greet({"dp": y_peer})

    @pl.when(z > 0)
    def _():
        greet({"dp": d - 4})

    @pl.when(z < 3)
    def _():
        greet({"dp": d + 4})

    def local(i, src, dst):
        return pltpu.make_async_copy(src, dst, sem_local.at[i])

    local_x = local(0, x_hbm, x2.at[x])
    local_win = local(1, win_hbm, w_in)
    local_g = local(2, g_hbm, own_g)
    local_wout = local(3, wout_hbm, w_out)
    local_gain = local(4, gain_hbm, gain_ref)
    local_seg = local(5, seg_hbm, seg_ref)
    local_moved = local(6, moved_hbm, moved_ref)
    local_x.start()
    local_gain.start()
    local_win.start()
    local_seg.start()
    local_moved.start()
    local_g.start()
    local_wout.start()

    pl.semaphore_wait(barrier, 4 + (z + 3) // 4 + (6 - z) // 4)

    def remote(src, dst, send_sem, recv_sem, where):
        return pltpu.make_async_remote_copy(
            src_ref=src, dst_ref=dst, send_sem=send_sem, recv_sem=recv_sem,
            device_id=where, device_id_type=MESH,
        )

    def rows_of(j):
        return pl.ds(pl.multiple_of(j * BLOCK, BLOCK), BLOCK)

    def short(i):
        return pl.ds(pl.multiple_of(i * STRIP, STRIP), STRIP)

    def swap(i):
        return remote(
            g_hbm.at[short(i)], land_z.at[short(i)], sem_zs.at[i], sem_zr.at[i], {"dp": partner}
        )

    def share_x(j):
        return remote(
            x_hbm.at[rows_of(j)], x2.at[x, rows_of(j)], sem_xs.at[j], sem_xr.at[j], {"mp": 1 - x}
        )

    def share_dy(i):
        return remote(
            dy2.at[x, short(i)], dy2.at[x, short(i)], sem_ds.at[i], sem_dr.at[i], {"mp": 1 - x}
        )

    def cross_t(i):
        return remote(send_t.at[i], land_t.at[i], sem_ts.at[i], sem_tr.at[i], {"mp": 1 - x})

    def share_mixed(j):
        return remote(
            mixed.at[rows_of(j)], mixed_y.at[rows_of(j)], sem_ms.at[j], sem_mr.at[j],
            {"dp": y_peer},
        )

    def share_turned(side, j):
        at = pl.ds(pl.multiple_of(side * 512, 512), 512)
        return remote(
            dy_t.at[j, 1 - y, at], side_t.at[j, at], sem_os.at[side, j], sem_or.at[side, j],
            {"dp": y_peer},
        )

    cross_s = remote(send_s, land_s, sem_ts.at[4], sem_tr.at[4], {"mp": 1 - x})

    def begin_swap(i, carry):
        swap(15 - i).start()
        return carry

    def begin_share(j, carry):
        share_x(j).start()
        return carry

    lax.fori_loop(0, 16, begin_swap, 0)
    lax.fori_loop(0, 4, begin_share, 0)

    def arrive(j):
        rows = rows_of(j)
        share_x(j).wait_recv()
        first = x2[0, rows, :].astype(FULL)
        second = x2[1, rows, :].astype(FULL)
        total = jnp.sum(first, axis=1, keepdims=True) + jnp.sum(second, axis=1, keepdims=True)
        mean = total * (1.0 / (2 * half))
        first = first - mean
        second = second - mean
        square = jnp.sum(first * first, axis=1, keepdims=True) + jnp.sum(
            second * second, axis=1, keepdims=True
        )
        inverse = lax.rsqrt(square * (1.0 / (2 * half)) + epsilon)
        mean_ref[rows, :] = mean
        inv_ref[rows, :] = inverse
        n0 = (first * inverse * gain_ref[:, :half]).astype(LOW)
        n1 = (second * inverse * gain_ref[:, half:]).astype(LOW)
        norm_t[:half, rows] = n0.T
        norm_t[half:, rows] = n1.T
        for h in range(heads):
            cols = slice(h * SPAN, (h + 1) * SPAN)
            pre = dot(n0, w_in[:half, cols], 1, 0) + dot(n1, w_in[half:, cols], 1, 0)
            sig = jax.nn.sigmoid(pre)
            act = (pre * sig).astype(LOW)
            slope_p[rows, cols] = sig * (1.0 + pre * (1.0 - sig))
            u_all[h, rows, :] = act[:, :DV]
            v_all[h, rows, :] = act[:, DV : 2 * DV]
            q_all[h, rows, :] = act[:, 2 * DV : 2 * DV + DQK]
            k_all[h, rows, :] = act[:, 2 * DV + DQK :]

    def forward(j):
        rows = slice(j * BLOCK, (j + 1) * BLOCK)
        w = (j + 1) * BLOCK
        seg = seg_ref[:, :w].astype(FULL)
        mine = jnp.broadcast_to(seg[:, j * BLOCK :], (BLOCK, BLOCK)).T
        row = lax.broadcasted_iota(jnp.int32, (BLOCK, w), 0) + j * BLOCK
        col = lax.broadcasted_iota(jnp.int32, (BLOCK, w), 1)
        same = jnp.concatenate([mine] * (j + 1), axis=1) == seg
        visible = jnp.where(same & (col <= row), 1.0, 0.0)

        def head(h, carry):
            scores = dot(q_all[h, rows, :], k_all[h, :w, :], 1, 1)
            sig = jax.nn.sigmoid(scores)
            attend = (scores * sig * visible).astype(LOW)
            attends[j][h] = attend
            slopes[j][h] = sig * (1.0 + scores * (1.0 - sig)) * visible
            outvals = dot(attend, v_all[h, :w, :], 1, 0)
            shifted = outvals - jnp.mean(outvals, axis=1, keepdims=True)
            inverse = lax.rsqrt(jnp.mean(shifted * shifted, axis=1, keepdims=True) + head_floor)
            onorm = shifted * inverse
            hinv_ref[h, rows, :] = inverse
            onorm_ref[rows, h * DV : (h + 1) * DV] = onorm
            mixed[rows, h * DV : (h + 1) * DV] = (onorm * u_all[h, rows, :].astype(FULL)).astype(LOW)
            return carry

        for h in range(heads):
            head(h, 0)
        share_mixed(j).start()

    def side_of(side):
        return pl.ds(pl.multiple_of(side * half, half), half)

    def turn(j, side):
        rows = slice(j * BLOCK, (j + 1) * BLOCK)
        turned = dy2[side, rows, :].T
        for g in range(4):
            at = pl.ds(pl.multiple_of(side * 512 + g // 2 * 256, 256), 256)
            dy_t[j, g % 2, at, :] = turned[g * 256 : (g + 1) * 256]
        share_turned(side, j).start()

    def relay(i):
        rows = slice(i * STRIP, (i + 1) * STRIP)
        swap(i).wait_recv()
        flags = jnp.full((STRIP, half), moved_ref[0, i // 4], jnp.int32)
        dy2[x, rows, :] = jnp.where(
            flags == 1, land_z[rows, :].astype(FULL), own_g[rows, :].astype(FULL)
        ).astype(LOW)
        share_dy(i).start()
        if i % 4 == 0:
            turn(i // 4, x)

    def backward(j):
        rows = slice(j * BLOCK, (j + 1) * BLOCK)
        w = (j + 1) * BLOCK
        for i in range(4):
            share_dy(4 * j + i).wait_recv()
        turn(j, 1 - x)
        d0, d1 = dy2[0, rows, :], dy2[1, rows, :]
        gm_ref[...] = dot(d0, w_out[:, :half], 1, 1) + dot(d1, w_out[:, half:], 1, 1)

        def head(h, carry):
            mix_at = slice(h * DV, (h + 1) * DV)
            u_at = slice(h * SPAN, h * SPAN + DV)
            v_at = slice(h * SPAN + DV, h * SPAN + 2 * DV)
            qk_at = slice(h * SPAN + 2 * DV, (h + 1) * SPAN)
            onorm = onorm_ref[rows, mix_at]
            mix = gm_ref[:, mix_at]
            gon = mix * u_all[h, rows, :].astype(FULL)
            grad_o = (
                hinv_ref[h, rows, :]
                * (
                    gon
                    - jnp.mean(gon, axis=1, keepdims=True)
                    - onorm * jnp.mean(gon * onorm, axis=1, keepdims=True)
                )
            ).astype(LOW)
            rhs[rows, u_at] = (mix * onorm * slope_p[rows, u_at]).astype(LOW)
            grad_s = (dot(grad_o, v_all[h, :w, :], 1, 1) * slopes[j][h]).astype(LOW)
            grad_v = dot(attends[j][h], grad_o, 0, 0)
            grad_k = dot(grad_s, q_all[h, rows, :], 0, 0)
            if j < 3:
                grad_v = grad_v + gv_acc[h, :w, :]
                grad_k = grad_k + gk_acc[h, :w, :]
            if j > 0:
                gv_acc[h, : j * BLOCK, :] = grad_v[: j * BLOCK]
                gk_acc[h, : j * BLOCK, :] = grad_k[: j * BLOCK]
            rhs[rows, v_at] = (grad_v[j * BLOCK :] * slope_p[rows, v_at]).astype(LOW)
            grad_qk = jnp.concatenate(
                [dot(grad_s, k_all[h, :w, :], 1, 0), grad_k[j * BLOCK :]], axis=1
            )
            rhs[rows, qk_at] = (grad_qk * slope_p[rows, qk_at]).astype(LOW)
            return carry

        for h in range(heads):
            head(h, 0)

    tile = 256

    def tile_of(side, i):
        return pl.ds(pl.multiple_of(side * half + i * tile, tile), tile)

    def inside(i):
        return pl.ds(pl.multiple_of(i * tile, tile), tile)

    def standard(side, i):
        return (x2[side, :, inside(i)].astype(FULL) - mean_ref[...]) * inv_ref[...]

    def term(side, i):
        part = dot(rhs[...], w_in[tile_of(side, i), :], 1, 1).astype(LOW)
        scaled = part.astype(FULL) * gain_ref[:, tile_of(side, i)]
        first = jnp.sum(scaled, axis=1, keepdims=True)
        second = jnp.sum(scaled * standard(side, i), axis=1, keepdims=True)
        lane = lax.broadcasted_iota(jnp.int32, send_s.shape, 1)
        return part, jnp.where(lane == 0, first, second)

    def term_away(i, carry):
        part, sums = term(1 - x, i)
        send_t[i] = part
        cross_t(i).start()
        send_s[...] = sums + send_s[...]
        return carry

    def term_kept(i, carry):
        part, sums = term(x, i)
        own_t[i] = part
        send_s[...] = sums + send_s[...]
        return carry

    def store_grad(i):
        return pltpu.make_async_copy(
            grad_ref.at[i], grad_hbm.at[:, inside(i)], sem_out.at[i]
        )

    def gradient(i, carry):
        cross_t(i).wait_recv()
        means = (send_s[...] + land_s[...]) * (1.0 / (2 * half))
        normed_grad = own_t[i].astype(FULL) + land_t[i].astype(FULL)
        grad_ref[i] = (
            dy2[x, :, inside(i)].astype(FULL)
            + inv_ref[...]
            * (
                normed_grad * gain_ref[:, tile_of(x, i)]
                - means[:, 0:1]
                - standard(x, i) * means[:, 1:2]
            )
        ).astype(LOW)
        store_grad(i).start()
        cross_t(i).wait_send()
        return carry

    def target(k):
        v = (3 - k) + (k // 2) * inner * (2 * k - 5)
        return (1 - upper) * v + upper * (3 - v)

    def product(k, side, p):
        pair = pl.ds(pl.multiple_of((target(k) * 2 + side) * 256, 256), 256)
        both = dot(norm_t[pair, :], rhs[:, pl.ds(pl.multiple_of(p * PIECE, PIECE), PIECE)], 1, 0)
        pair_ref[p] = both

    def to_core(slot, p):
        return remote(
            send_c.at[slot, p], recv_c.at[slot, p], sem_cs.at[slot, p], sem_cr.at[slot, p],
            {"dp": core_peer},
        )

    def to_y(k, p):
        return remote(
            send_y.at[k, p], recv_y.at[k, p], sem_ys.at[k, p], sem_yr.at[k, p], {"dp": y_peer}
        )

    def up(k, t, p):
        return remote(
            send_z.at[k, p], from_low.at[t, p], sem_fs.at[k, p], sem_low.at[t, p], {"dp": d + 4}
        )

    def down(k, t, p):
        return remote(
            send_z.at[k, p], from_high.at[t, p], sem_fs.at[k, p], sem_high.at[t, p], {"dp": d - 4}
        )

    def away(k):
        def issue(p, carry):
            product(k, 1 - y, p)
            send_c[k, p] = pair_ref[p, rows_of(1 - c), :].astype(LOW)
            to_core(k, p).start()
            return carry

        def finish(p, carry):
            mine = pair_ref[p, rows_of(c), :]
            to_core(k, p).wait_recv()
            send_y[k, p] = (mine + recv_c[k, p].astype(FULL)).astype(LOW)
            to_y(k, p).start()
            return carry

        lax.fori_loop(0, 3, issue, 0)
        lax.fori_loop(0, 3, finish, 0)

    def keep(k):
        def issue(p, carry):
            product(k, y, p)
            send_c[k + 4, p] = pair_ref[p, rows_of(1 - c), :].astype(LOW)
            to_core(k + 4, p).start()
            return carry

        def finish(p, carry):
            mine = pair_ref[p, rows_of(c), :]
            to_core(k + 4, p).wait_recv()
            keep_y[k, p] = (mine + recv_c[k + 4, p].astype(FULL)).astype(LOW)
            return carry

        lax.fori_loop(0, 3, issue, 0)
        lax.fori_loop(0, 3, finish, 0)

    def out_product(k, core):
        rows = rows_of(target(k) * 2 + core)
        mine = jnp.concatenate([dy_t[j, y, rows, :] for j in range(4)], axis=1)
        theirs = jnp.concatenate([side_t[j, rows, :] for j in range(4)], axis=1)
        return dot(mine, mixed[...], 1, 0) + dot(theirs, mixed_y[...], 1, 0)

    def out_core(k):
        return remote(
            send_g.at[k], recv_g.at[k], sem_gs.at[k], sem_gr.at[k], {"dp": core_peer}
        )

    def out_issue(k, carry):
        send_g[k] = out_product(k, 1 - c).astype(LOW)
        out_core(k).start()
        return carry

    def out_finish(k, carry):
        mine = out_product(k, c)
        out_core(k).wait_recv()
        keep_y[k, 3] = (mine + recv_g[k].astype(FULL)).astype(LOW)
        return carry

    def here(k, p, with_y):
        if with_y:
            to_y(k, p).wait_recv()
            return keep_y[k, p].astype(FULL) + recv_y[k, p].astype(FULL)
        return keep_y[k, p].astype(FULL)

    def end(k, p, with_y=True):
        @pl.when((z == 0) | (z == 3))
        def _():
            t = target(k)
            send_z[k, p] = here(k, p, with_y).astype(LOW)

            @pl.when(t > z)
            def _():
                up(k, t, p).start()

            @pl.when(t < z)
            def _():
                down(k, t, p).start()

    def mid(k, p, with_y=True):
        @pl.when((z == 1) | (z == 2))
        def _():
            t = target(k)
            part = here(k, p, with_y)

            @pl.when(t > z)
            def _():
                pltpu.make_async_copy(from_low.at[t, p], from_low.at[t, p], sem_low.at[t, p]).wait()
                send_z[k, p] = (part + from_low[t, p].astype(FULL)).astype(LOW)
                up(k, t, p).start()

            @pl.when(t < z)
            def _():
                pltpu.make_async_copy(from_high.at[t, p], from_high.at[t, p], sem_high.at[t, p]).wait()
                send_z[k, p] = (part + from_high[t, p].astype(FULL)).astype(LOW)
                down(k, t, p).start()

    def ends(k):
        def piece(p, carry):
            end(k, p)
            return carry

        lax.fori_loop(0, 3, piece, 0)

    def mids(k):
        def piece(p, carry):
            mid(k, p)
            return carry

        lax.fori_loop(0, 3, piece, 0)

    send_s[...] = jnp.zeros_like(send_s)
    local_x.wait()
    local_gain.wait()
    local_win.wait()
    arrive(0)
    local_g.wait()
    local_moved.wait()
    local_seg.wait()
    relay(15)
    forward(0)
    relay(14)
    arrive(1)
    relay(13)
    forward(1)
    relay(12)
    arrive(2)
    relay(11)
    forward(2)
    relay(10)
    arrive(3)
    relay(9)
    forward(3)
    relay(8)
    local_wout.wait()
    backward(3)
    relay(7)
    backward(2)
    relay(6)
    relay(5)
    relay(4)
    relay(3)
    backward(1)
    relay(2)
    relay(1)
    relay(0)
    backward(0)

    away(0)

    def mixed_here(j, carry):
        share_mixed(j).wait_recv()
        return carry

    def operands_here(i, carry):
        share_turned(i // 4, i % 4).wait_recv()
        return carry

    keep(0)
    lax.fori_loop(0, 2, term_away, 0)
    away(1)
    lax.fori_loop(2, 4, term_away, 0)
    lax.fori_loop(0, 4, mixed_here, 0)
    lax.fori_loop(0, 8, operands_here, 0)
    lax.fori_loop(0, 4, out_issue, 0)
    lax.fori_loop(0, 4, out_finish, 0)
    for k in range(3):
        end(k, 3, False)
    keep(1)
    ends(0)
    away(2)
    mid(0, 3, False)
    mid(1, 3, False)
    keep(2)
    mid(2, 3, False)
    away(3)
    keep(3)
    ends(1)
    mid(0, 0)
    lax.fori_loop(0, 4, term_kept, 0)
    cross_s.start()
    mid(0, 1)
    mid(0, 2)

    def interior(p, carry):
        mid(1, p)
        mid(2, p)
        return carry

    lax.fori_loop(0, 3, interior, 0)
    ends(2)
    cross_s.wait()
    lax.fori_loop(0, 4, gradient, 0)

    total = gm_ref

    def gather_total(p, with_y):
        if with_y:
            to_y(3, p).wait_recv()
            total[...] = keep_y[3, p].astype(FULL) + recv_y[3, p].astype(FULL)
        else:
            total[...] = keep_y[3, p].astype(FULL)

        @pl.when(z > 0)
        def _():
            pltpu.make_async_copy(from_low.at[z, p], from_low.at[z, p], sem_low.at[z, p]).wait()
            total[...] += from_low[z, p].astype(FULL)

        @pl.when(z < 3)
        def _():
            pltpu.make_async_copy(from_high.at[z, p], from_high.at[z, p], sem_high.at[z, p]).wait()
            total[...] += from_high[z, p].astype(FULL)

    def store_in(p):
        cols = pl.ds(p * PIECE, PIECE)
        return pltpu.make_async_copy(gin_ref.at[:, cols], gin_hbm.at[:, cols], sem_out.at[4 + p])

    store_out = pltpu.make_async_copy(gout_ref, gout_hbm, sem_out.at[7])

    gather_total(3, False)
    gout_ref[...] = total[...].T
    store_out.start()
    for p in range(3):
        gather_total(p, True)
        gin_ref[:, p * PIECE : (p + 1) * PIECE] = total[...]
        store_in(p).start()

    def drain_swap(i, carry):
        swap(i).wait_send()
        share_dy(i).wait_send()
        return carry

    lax.fori_loop(0, 16, drain_swap, 0)

    def drain_share(j, carry):
        share_x(j).wait_send()
        out_core(j).wait_send()
        share_mixed(j).wait_send()
        store_grad(j).wait()
        for side in range(2):
            share_turned(side, j).wait_send()
        return carry

    lax.fori_loop(0, 4, drain_share, 0)

    def drain_core(i, carry):
        to_core(i // 3, i % 3).wait_send()
        return carry

    lax.fori_loop(0, 24, drain_core, 0)

    def drain_far(i, carry):
        k, p = i // 4, i % 4
        t = target(k)

        @pl.when(p < 3)
        def _():
            to_y(k, p).wait_send()

        @pl.when(t > z)
        def _():
            up(k, t, p).wait_send()

        @pl.when(t < z)
        def _():
            down(k, t, p).wait_send()

        return carry

    lax.fori_loop(0, 16, drain_far, 0)
    for p in range(3):
        store_in(p).wait()
    store_out.wait()


def finish_kernel(grad, gin, gout, grad_out, gin_out, gout_out, b_grad, b_gin, b_gout, sems):
    steps = []
    for source, staged, result, parts in (
        (grad, b_grad, grad_out, 4), (gin, b_gin, gin_out, 2), (gout, b_gout, gout_out, 1),
    ):
        size = source.shape[0] // parts
        for i in range(parts):
            at = pl.ds(i * size, size)
            n = len(steps)
            steps.append((
                pltpu.make_async_copy(source.at[at], staged.at[at], sems.at[0, n]),
                pltpu.make_async_copy(staged.at[at], result.at[at], sems.at[1, n]),
            ))
    for fetch, _ in steps:
        fetch.start()
    for fetch, store in steps:
        fetch.wait()
        store.start()
    for _, store in steps:
        store.wait()


def finished(*arrays):
    anywhere = pl.BlockSpec(memory_space=pl.ANY)
    return pl.pallas_call(
        finish_kernel,
        out_shape=tuple(jax.ShapeDtypeStruct(a.shape, a.dtype) for a in arrays),
        in_specs=[anywhere] * len(arrays),
        out_specs=[anywhere] * len(arrays),
        scratch_shapes=[pltpu.VMEM(a.shape, a.dtype) for a in arrays]
        + [pltpu.SemaphoreType.DMA((2, 7))],
    )(*arrays)


def fused(inputs, grad_moved, moved, segments, gain, proj_in, proj_out):
    rows, half = inputs.shape
    wide, narrow = proj_in.shape[1], proj_out.shape[0]
    heads = wide // SPAN
    vmem, dma = pltpu.VMEM, pltpu.SemaphoreType.DMA
    anywhere = pl.BlockSpec(memory_space=pl.ANY)
    pieces = vmem((4, 4, 128, PIECE), LOW)
    thirds = vmem((4, 3, 128, PIECE), LOW)
    widths = [(j + 1) * BLOCK for j in range(rows // BLOCK)]
    gin, gout, grad = pl.pallas_call(
        fused_kernel,
        out_shape=(
            jax.ShapeDtypeStruct((128, wide), FULL),
            jax.ShapeDtypeStruct((narrow, 128), FULL),
            jax.ShapeDtypeStruct((rows, half), LOW),
        ),
        in_specs=[anywhere] * 7,
        out_specs=[anywhere] * 3,
        scratch_shapes=[
            vmem((2, rows, half), LOW),
            vmem((rows, half), LOW),
            vmem((rows, half), LOW),
            vmem((2, rows, half), LOW),
            vmem(proj_in.shape, LOW),
            vmem(proj_out.shape, LOW),
            vmem((2 * half, rows), LOW),
            vmem((4, 2, half, BLOCK), LOW),
            vmem((rows, wide), LOW),
            vmem((rows, narrow), LOW),
            vmem((rows, wide), FULL),
            vmem((heads, rows, DV), LOW),
            vmem((heads, rows, DV), LOW),
            vmem((heads, rows, DQK), LOW),
            vmem((heads, rows, DQK), LOW),
        ]
        + [vmem((heads, BLOCK, w), LOW) for w in widths]
        + [vmem((heads, BLOCK, w), FULL) for w in widths]
        + [
            vmem((rows, narrow), FULL),
            vmem((heads, rows, 1), FULL),
            vmem((BLOCK, narrow), FULL),
            vmem((heads, rows - BLOCK, DV), FULL),
            vmem((heads, rows - BLOCK, DQK), FULL),
            vmem((rows, 1), FULL),
            vmem((rows, 1), FULL),
            vmem((4, rows, half // 4), LOW),
            vmem((4, rows, half // 4), LOW),
            vmem((4, rows, half // 4), LOW),
            vmem((rows, 128), FULL),
            vmem((rows, 128), FULL),
            vmem((4, half, BLOCK), LOW),
            vmem((rows, narrow), LOW),
            vmem((8, 3, 128, PIECE), LOW),
            vmem((8, 3, 128, PIECE), LOW),
            vmem((4, 128, PIECE), LOW),
            vmem((4, 128, PIECE), LOW),
            thirds, pieces, thirds, pieces, pieces, pieces,
            vmem((3, 256, PIECE), FULL),
            pltpu.SMEM(moved.shape, jnp.int32),
            vmem((1, rows), jnp.int32),
            vmem((1, 2 * half), FULL),
            vmem((128, wide), FULL),
            vmem((narrow, 128), FULL),
            vmem((4, rows, half // 4), LOW),
            dma((7,)), dma((16,)), dma((16,)), dma((4,)), dma((4,)), dma((16,)), dma((16,)),
            dma((5,)), dma((5,)), dma((4,)), dma((4,)), dma((2, 4)), dma((2, 4)), dma((8, 3)), dma((8, 3)),
            dma((4,)), dma((4,)), dma((4, 3)), dma((4, 3)), dma((4, 4)), dma((4, 4)), dma((4, 4)),
            dma((8,)),
        ],
        compiler_params=pltpu.CompilerParams(
            collective_id=0, has_side_effects=True, vmem_limit_bytes=62 * 1024 * 1024
        ),
    )(inputs, grad_moved, moved, segments[None, :], gain[None, :], proj_in, proj_out)
    return finished(grad, gin, gout)


def on_device(inputs, grad_moved, moved, segments, input_norm_gain, proj_in, proj_out):
    rows = inputs.shape[0]
    span = 2 * DV + 2 * DQK
    heads_here = proj_in.shape[1] // span
    if lax.axis_size("mp") == 2 and lax.axis_size("dp") == 16:
        return fused(inputs, grad_moved, moved, segments, input_norm_gain, proj_in, proj_out)
    top_bit = lax.axis_size("dp").bit_length() - 2
    blocks = rows // BLOCK
    mine = [grad_moved[j * BLOCK : (j + 1) * BLOCK] for j in range(blocks)]
    theirs = [swapped(block, "dp", top_bit) for block in mine]
    full_x = gathered(inputs)
    full_dy = jnp.concatenate(
        [gathered(jnp.where(moved[0, j] == 1, theirs[j], mine[j])) for j in range(blocks)], axis=0
    )
    xfull = full_x.astype(jnp.float32)
    mean_shifted = xfull - jnp.mean(xfull, axis=1, keepdims=True)
    inverse_deviation = lax.rsqrt(
        jnp.mean(mean_shifted * mean_shifted, axis=1, keepdims=True) + epsilon
    )
    standardized_input = mean_shifted * inverse_deviation
    normalized_rows = (standardized_input * input_norm_gain[None, :]).astype(jnp.bfloat16)
    pre = jnp.dot(normalized_rows, proj_in, preferred_element_type=jnp.float32)
    sig_p = jax.nn.sigmoid(pre)
    acts = (pre * sig_p).astype(jnp.bfloat16)
    grad_mix = lax.dot_general(
        full_dy, proj_out, (((1,), (1,)), ((), ())), preferred_element_type=jnp.float32
    )
    order = jnp.arange(rows, dtype=jnp.int32)
    visible = (
        (segments[:, None] == segments[None, :]) & (order[None, :] <= order[:, None])
    ).astype(jnp.float32)
    mixed, saved = forward_heads(acts, visible, heads_here)
    grad_act = backward_heads(saved, grad_mix, visible, heads_here)
    grad_pre = (grad_act * sig_p * (1.0 + pre * (1.0 - sig_p))).astype(jnp.bfloat16)
    local = inputs.shape[1]
    offset = lax.axis_index("mp") * local
    normed_term = lax.dot_general(
        grad_pre, proj_in, (((1,), (1,)), ((), ())), preferred_element_type=jnp.float32
    ).astype(jnp.bfloat16)
    term_scaled = normed_term.astype(jnp.float32) * input_norm_gain[None, :]
    sums = jnp.stack([jnp.sum(term_scaled, axis=1), jnp.sum(term_scaled * standardized_input, axis=1)])
    partial_out = lax.dot_general(
        mixed, full_dy, (((0,), (0,)), ((), ())), preferred_element_type=jnp.float32
    )
    grad_proj_out = lax.psum_scatter(
        partial_out.astype(jnp.bfloat16), "dp", scatter_dimension=1, tiled=True
    ).astype(jnp.float32)
    partial_in = lax.dot_general(
        normalized_rows, grad_pre, (((0,), (0,)), ((), ())), preferred_element_type=jnp.float32
    )
    grad_proj_in = lax.psum_scatter(
        partial_in.astype(jnp.bfloat16), "dp", scatter_dimension=0, tiled=True
    ).astype(jnp.float32)
    sums = lax.psum(sums, "mp")
    grad_normed = lax.psum_scatter(
        normed_term, "mp", scatter_dimension=1, tiled=True
    ).astype(jnp.float32)
    means = sums / standardized_input.shape[1]
    here = lambda array: lax.dynamic_slice_in_dim(array, offset, local, 1)
    grad_here = here(full_dy).astype(jnp.float32) + inverse_deviation * (
        grad_normed * here(input_norm_gain[None, :])
        - means[0][:, None]
        - here(standardized_input) * means[1][:, None]
    )
    input_gradient = grad_here.astype(jnp.bfloat16)
    return (input_gradient, grad_proj_in, grad_proj_out)


def solution(mesh):
    return jax.shard_map(
        on_device,
        mesh=mesh,
        in_specs=(
            P("dp", "mp"),
            P("dp", "mp"),
            P("dp", None),
            P("dp"),
            P(),
            P(None, "mp"),
            P("mp", None),
        ),
        out_specs=(P("dp", "mp"), P("dp", "mp"), P("mp", "dp")),
        check_vma=False,
    )
```

```python
import jax
import jax.numpy as jnp
from jax import lax
from jax.experimental import pallas as pl
from jax.experimental.pallas import tpu as pltpu
from jax.sharding import PartitionSpec as P

DV = 128
DQK = 64
BLOCK = 128


epsilon = 1e-05
head_floor = 1.0


def swapped(block, axis, apart):
    count = lax.axis_size(axis)
    route = []
    for low in range(count):
        high = low | 1 << apart
        if high != low and high < count:
            route += [(low, high), (high, low)]
    return lax.ppermute(block, axis, route)


def gathered(block):
    return lax.all_gather(block, "mp", axis=1, tiled=True)


def forward_heads(acts, visible, heads_here):
    span = 2 * DV + 2 * DQK
    rows = acts.shape[0]
    parts = acts.reshape(rows, heads_here, span)
    u_vals = parts[:, :, :DV]
    v_vals = parts[:, :, DV : 2 * DV]
    q_vals = parts[:, :, 2 * DV : 2 * DV + DQK]
    k_vals = parts[:, :, 2 * DV + DQK :]
    scores = jnp.einsum("qhd,khd->hqk", q_vals, k_vals, preferred_element_type=jnp.float32)
    sig_s = jax.nn.sigmoid(scores)
    attend = (scores * sig_s * visible[None]).astype(jnp.bfloat16)
    slope = sig_s * (1.0 + scores * (1.0 - sig_s))
    outvals = jnp.einsum("hqk,khd->qhd", attend, v_vals, preferred_element_type=jnp.float32)
    mean_shifted = outvals - jnp.mean(outvals, axis=-1, keepdims=True)
    head_inv = lax.rsqrt(jnp.mean(mean_shifted * mean_shifted, axis=-1, keepdims=True) + head_floor)
    onorm = mean_shifted * head_inv
    mixed = (onorm * u_vals).astype(jnp.bfloat16).reshape(rows, heads_here * DV)
    saved = (u_vals, v_vals, q_vals, k_vals, attend, slope, onorm, head_inv)
    return (mixed, saved)


def backward_heads(saved, grad_mix, visible, heads_here):
    u_vals, v_vals, q_vals, k_vals, attend, slope, onorm, head_inv = saved
    rows = grad_mix.shape[0]
    grad_mixr = grad_mix.reshape(rows, heads_here, DV)
    grad_u = grad_mixr * onorm
    gon = grad_mixr * u_vals
    grad_o = (
        head_inv
        * (
            gon
            - jnp.mean(gon, axis=-1, keepdims=True)
            - onorm * jnp.mean(gon * onorm, axis=-1, keepdims=True)
        )
    ).astype(jnp.bfloat16)
    grad_att = jnp.einsum("qhd,khd->hqk", grad_o, v_vals, preferred_element_type=jnp.float32)
    grad_v = jnp.einsum("hqk,qhd->khd", attend, grad_o, preferred_element_type=jnp.float32)
    grad_scores = (grad_att * visible[None] * slope).astype(jnp.bfloat16)
    grad_q = jnp.einsum("hqk,khd->qhd", grad_scores, k_vals, preferred_element_type=jnp.float32)
    grad_k = jnp.einsum("hqk,qhd->khd", grad_scores, q_vals, preferred_element_type=jnp.float32)
    grad_act = jnp.concatenate([grad_u, grad_v, grad_q, grad_k], axis=-1)
    return grad_act.reshape(rows, heads_here * (2 * DV + 2 * DQK))


MESH = pl.DeviceIdType.MESH
SPAN = 2 * DV + 2 * DQK
PIECE = 512
STRIP = 32
LOW, FULL = jnp.bfloat16, jnp.float32


def dot(a, b, i, j):
    return lax.dot_general(a, b, (((i,), (j,)), ((), ())), preferred_element_type=FULL)


def fused_kernel(
    x_hbm, g_hbm, moved_hbm, seg_hbm, gain_hbm, win_hbm, wout_hbm,
    gin_hbm, gout_hbm, grad_hbm,
    x2, own_g, land_z, dy2, w_in, w_out, norm_t, dy_t, rhs, mixed, slope_p, u_all, v_all, q_all, k_all,
    att0, att1, att2, att3, slo0, slo1, slo2, slo3, onorm_ref, hinv_ref, gm_ref, gv_acc, gk_acc,
    mean_ref, inv_ref, land_t, send_t, own_t, land_s, send_s, side_t, mixed_y,
    send_c, recv_c, send_g, recv_g, send_y, keep_y, recv_y, send_z, from_low, from_high,
    send_n, land_n, pair_ref, moved_ref, seg_ref, gain_ref, gin_ref, gout_ref, grad_ref,
    sem_local, sem_zs, sem_zr, sem_xs, sem_xr, sem_ds, sem_dr, sem_ts, sem_tr, sem_ms, sem_mr,
    sem_os, sem_or, sem_cs, sem_cr, sem_gs, sem_gr, sem_ys, sem_yr, sem_fs, sem_low, sem_high,
    sem_out,
):
    heads = u_all.shape[0]
    half = x_hbm.shape[1]
    wide = heads * SPAN
    attends = (att0, att1, att2, att3)
    slopes = (slo0, slo1, slo2, slo3)
    d = lax.axis_index("dp")
    x = lax.axis_index("mp")
    z = d // 4
    y = (d // 2) % 2
    c = d % 2
    upper = z // 2
    inner = (z + upper) % 2
    core_peer = d + 1 - 2 * c
    y_peer = d + 2 - 4 * y
    partner = (d + 8) % 16

    barrier = pltpu.get_barrier_semaphore()

    def greet(where):
        pl.semaphore_signal(barrier, inc=1, device_id=where, device_id_type=MESH)

    greet({"dp": partner})
    greet({"mp": 1 - x})
    greet({"dp": core_peer})
    greet({"dp": y_peer})

    @pl.when(z > 0)
    def _():
        greet({"dp": d - 4})

    @pl.when(z < 3)
    def _():
        greet({"dp": d + 4})

    def local(i, src, dst):
        return pltpu.make_async_copy(src, dst, sem_local.at[i])

    local_x = local(0, x_hbm, x2.at[x])
    local_win = local(1, win_hbm, w_in)
    local_g = local(2, g_hbm, own_g)
    local_wout = local(3, wout_hbm, w_out)
    local_gain = local(4, gain_hbm, gain_ref)
    local_seg = local(5, seg_hbm, seg_ref)
    local_moved = local(6, moved_hbm, moved_ref)
    local_x.start()
    local_gain.start()
    local_win.start()
    local_seg.start()
    local_moved.start()
    local_g.start()
    local_wout.start()

    pl.semaphore_wait(barrier, 4 + (z + 3) // 4 + (6 - z) // 4)

    def remote(src, dst, send_sem, recv_sem, where):
        return pltpu.make_async_remote_copy(
            src_ref=src, dst_ref=dst, send_sem=send_sem, recv_sem=recv_sem,
            device_id=where, device_id_type=MESH,
        )

    def rows_of(j):
        return pl.ds(pl.multiple_of(j * BLOCK, BLOCK), BLOCK)

    def short(i):
        return pl.ds(pl.multiple_of(i * STRIP, STRIP), STRIP)

    def swap(i):
        return remote(
            g_hbm.at[short(i)], land_z.at[short(i)], sem_zs.at[i], sem_zr.at[i], {"dp": partner}
        )

    def share_x(j):
        return remote(
            x_hbm.at[rows_of(j)], x2.at[x, rows_of(j)], sem_xs.at[j], sem_xr.at[j], {"mp": 1 - x}
        )

    def share_dy(i):
        return remote(
            dy2.at[x, short(i)], dy2.at[x, short(i)], sem_ds.at[i], sem_dr.at[i], {"mp": 1 - x}
        )

    def cross_t(i):
        return remote(send_t.at[i], land_t.at[i], sem_ts.at[i], sem_tr.at[i], {"mp": 1 - x})

    def share_mixed(j):
        return remote(
            mixed.at[rows_of(j)], mixed_y.at[rows_of(j)], sem_ms.at[j], sem_mr.at[j],
            {"dp": y_peer},
        )

    def share_turned(side, j):
        at = pl.ds(pl.multiple_of(side * 512, 512), 512)
        return remote(
            dy_t.at[j, 1 - y, at], side_t.at[j, at], sem_os.at[side, j], sem_or.at[side, j],
            {"dp": y_peer},
        )

    cross_s = remote(send_n, land_n, sem_ts.at[4], sem_tr.at[4], {"mp": 1 - x})

    def begin_swap(i, carry):
        swap(15 - i).start()
        return carry

    def begin_share(j, carry):
        share_x(j).start()
        return carry

    lax.fori_loop(0, 16, begin_swap, 0)
    lax.fori_loop(0, 4, begin_share, 0)

    def arrive(j):
        rows = rows_of(j)
        share_x(j).wait_recv()
        first = x2[0, rows, :].astype(FULL)
        second = x2[1, rows, :].astype(FULL)
        total = jnp.sum(first, axis=1, keepdims=True) + jnp.sum(second, axis=1, keepdims=True)
        mean = total * (1.0 / (2 * half))
        first = first - mean
        second = second - mean
        square = jnp.sum(first * first, axis=1, keepdims=True) + jnp.sum(
            second * second, axis=1, keepdims=True
        )
        inverse = lax.rsqrt(square * (1.0 / (2 * half)) + epsilon)
        mean_ref[rows, :] = mean
        inv_ref[rows, :] = inverse
        n0 = (first * inverse * gain_ref[:, :half]).astype(LOW)
        n1 = (second * inverse * gain_ref[:, half:]).astype(LOW)
        norm_t[:half, rows] = n0.T
        norm_t[half:, rows] = n1.T
        for h in range(heads):
            cols = slice(h * SPAN, (h + 1) * SPAN)
            pre = dot(n0, w_in[:half, cols], 1, 0) + dot(n1, w_in[half:, cols], 1, 0)
            sig = jax.nn.sigmoid(pre)
            act = (pre * sig).astype(LOW)
            slope_p[rows, cols] = sig * (1.0 + pre * (1.0 - sig))
            u_all[h, rows, :] = act[:, :DV]
            v_all[h, rows, :] = act[:, DV : 2 * DV]
            q_all[h, rows, :] = act[:, 2 * DV : 2 * DV + DQK]
            k_all[h, rows, :] = act[:, 2 * DV + DQK :]

    def forward(j):
        rows = slice(j * BLOCK, (j + 1) * BLOCK)
        w = (j + 1) * BLOCK
        seg = seg_ref[:, :w].astype(FULL)
        mine = jnp.broadcast_to(seg[:, j * BLOCK :], (BLOCK, BLOCK)).T
        row = lax.broadcasted_iota(jnp.int32, (BLOCK, w), 0) + j * BLOCK
        col = lax.broadcasted_iota(jnp.int32, (BLOCK, w), 1)
        same = jnp.concatenate([mine] * (j + 1), axis=1) == seg
        visible = jnp.where(same & (col <= row), 1.0, 0.0)

        def head(h, carry):
            scores = dot(q_all[h, rows, :], k_all[h, :w, :], 1, 1)
            sig = jax.nn.sigmoid(scores)
            attend = (scores * sig * visible).astype(LOW)
            attends[j][h] = attend
            slopes[j][h] = sig * (1.0 + scores * (1.0 - sig)) * visible
            outvals = dot(attend, v_all[h, :w, :], 1, 0)
            shifted = outvals - jnp.mean(outvals, axis=1, keepdims=True)
            inverse = lax.rsqrt(jnp.mean(shifted * shifted, axis=1, keepdims=True) + head_floor)
            onorm = shifted * inverse
            hinv_ref[h, rows, :] = inverse
            onorm_ref[rows, h * DV : (h + 1) * DV] = onorm
            mixed[rows, h * DV : (h + 1) * DV] = (onorm * u_all[h, rows, :].astype(FULL)).astype(LOW)
            return carry

        for h in range(heads):
            head(h, 0)
        share_mixed(j).start()

    def side_of(side):
        return pl.ds(pl.multiple_of(side * half, half), half)

    def turn(j, side):
        rows = slice(j * BLOCK, (j + 1) * BLOCK)
        turned = dy2[side, rows, :].T
        for g in range(4):
            at = pl.ds(pl.multiple_of(side * 512 + g // 2 * 256, 256), 256)
            dy_t[j, g % 2, at, :] = turned[g * 256 : (g + 1) * 256]
        share_turned(side, j).start()

    def relay(i):
        rows = slice(i * STRIP, (i + 1) * STRIP)
        swap(i).wait_recv()
        flags = jnp.full((STRIP, half), moved_ref[0, i // 4], jnp.int32)
        dy2[x, rows, :] = jnp.where(
            flags == 1, land_z[rows, :].astype(FULL), own_g[rows, :].astype(FULL)
        ).astype(LOW)
        share_dy(i).start()
        if i % 4 == 0:
            turn(i // 4, x)

    def backward(j):
        rows = slice(j * BLOCK, (j + 1) * BLOCK)
        w = (j + 1) * BLOCK
        for i in range(4):
            share_dy(4 * j + i).wait_recv()
        turn(j, 1 - x)
        d0, d1 = dy2[0, rows, :], dy2[1, rows, :]
        gm_ref[...] = dot(d0, w_out[:, :half], 1, 1) + dot(d1, w_out[:, half:], 1, 1)

        def head(h, carry):
            mix_at = slice(h * DV, (h + 1) * DV)
            u_at = slice(h * SPAN, h * SPAN + DV)
            v_at = slice(h * SPAN + DV, h * SPAN + 2 * DV)
            qk_at = slice(h * SPAN + 2 * DV, (h + 1) * SPAN)
            onorm = onorm_ref[rows, mix_at]
            mix = gm_ref[:, mix_at]
            gon = mix * u_all[h, rows, :].astype(FULL)
            grad_o = (
                hinv_ref[h, rows, :]
                * (
                    gon
                    - jnp.mean(gon, axis=1, keepdims=True)
                    - onorm * jnp.mean(gon * onorm, axis=1, keepdims=True)
                )
            ).astype(LOW)
            rhs[rows, u_at] = (mix * onorm * slope_p[rows, u_at]).astype(LOW)
            grad_s = (dot(grad_o, v_all[h, :w, :], 1, 1) * slopes[j][h]).astype(LOW)
            grad_v = dot(attends[j][h], grad_o, 0, 0)
            grad_k = dot(grad_s, q_all[h, rows, :], 0, 0)
            if j < 3:
                grad_v = grad_v + gv_acc[h, :w, :]
                grad_k = grad_k + gk_acc[h, :w, :]
            if j > 0:
                gv_acc[h, : j * BLOCK, :] = grad_v[: j * BLOCK]
                gk_acc[h, : j * BLOCK, :] = grad_k[: j * BLOCK]
            rhs[rows, v_at] = (grad_v[j * BLOCK :] * slope_p[rows, v_at]).astype(LOW)
            grad_qk = jnp.concatenate(
                [dot(grad_s, k_all[h, :w, :], 1, 0), grad_k[j * BLOCK :]], axis=1
            )
            rhs[rows, qk_at] = (grad_qk * slope_p[rows, qk_at]).astype(LOW)
            return carry

        for h in range(heads):
            head(h, 0)

    tile = 256

    def tile_of(side, i):
        return pl.ds(pl.multiple_of(side * half + i * tile, tile), tile)

    def inside(i):
        return pl.ds(pl.multiple_of(i * tile, tile), tile)

    def standard(side, i):
        return (x2[side, :, inside(i)].astype(FULL) - mean_ref[...]) * inv_ref[...]

    def term(side, i):
        part = dot(rhs[...], w_in[tile_of(side, i), :], 1, 1).astype(LOW)
        scaled = part.astype(FULL) * gain_ref[:, tile_of(side, i)]
        first = jnp.sum(scaled, axis=1, keepdims=True)
        second = jnp.sum(scaled * standard(side, i), axis=1, keepdims=True)
        lane = lax.broadcasted_iota(jnp.int32, send_s.shape, 1)
        return part, jnp.where(lane == 0, first, second)

    def term_away(i, carry):
        part, sums = term(1 - x, i)
        send_t[i] = part
        cross_t(i).start()
        send_s[...] = sums + send_s[...]
        return carry

    def term_kept(i, carry):
        part, sums = term(x, i)
        own_t[i] = part
        send_s[...] = sums + send_s[...]
        return carry

    def store_grad(i):
        return pltpu.make_async_copy(
            grad_ref.at[i], grad_hbm.at[:, inside(i)], sem_out.at[i]
        )

    def gradient(i, carry):
        cross_t(i).wait_recv()
        means = (send_s[...] + land_s[...]) * (1.0 / (2 * half))
        normed_grad = own_t[i].astype(FULL) + land_t[i].astype(FULL)
        grad_ref[i] = (
            dy2[x, :, inside(i)].astype(FULL)
            + inv_ref[...]
            * (
                normed_grad * gain_ref[:, tile_of(x, i)]
                - means[:, 0:1]
                - standard(x, i) * means[:, 1:2]
            )
        ).astype(LOW)
        store_grad(i).start()
        cross_t(i).wait_send()
        return carry

    def target(k):
        v = (3 - k) + (k // 2) * inner * (2 * k - 5)
        return (1 - upper) * v + upper * (3 - v)

    def product(k, side, p):
        pair = pl.ds(pl.multiple_of((target(k) * 2 + side) * 256, 256), 256)
        both = dot(norm_t[pair, :], rhs[:, pl.ds(pl.multiple_of(p * PIECE, PIECE), PIECE)], 1, 0)
        pair_ref[p] = both

    def to_core(slot, p):
        return remote(
            send_c.at[slot, p], recv_c.at[slot, p], sem_cs.at[slot, p], sem_cr.at[slot, p],
            {"dp": core_peer},
        )

    def to_y(k, p):
        return remote(
            send_y.at[k, p], recv_y.at[k, p], sem_ys.at[k, p], sem_yr.at[k, p], {"dp": y_peer}
        )

    def up(k, t, p):
        return remote(
            send_z.at[k, p], from_low.at[t, p], sem_fs.at[k, p], sem_low.at[t, p], {"dp": d + 4}
        )

    def down(k, t, p):
        return remote(
            send_z.at[k, p], from_high.at[t, p], sem_fs.at[k, p], sem_high.at[t, p], {"dp": d - 4}
        )

    def away(k):
        def issue(p, carry):
            product(k, 1 - y, p)
            send_c[k, p] = pair_ref[p, rows_of(1 - c), :].astype(LOW)
            to_core(k, p).start()
            return carry

        def finish(p, carry):
            mine = pair_ref[p, rows_of(c), :]
            to_core(k, p).wait_recv()
            send_y[k, p] = (mine + recv_c[k, p].astype(FULL)).astype(LOW)
            to_y(k, p).start()
            return carry

        lax.fori_loop(0, 3, issue, 0)
        lax.fori_loop(0, 3, finish, 0)

    def keep(k):
        def issue(p, carry):
            product(k, y, p)
            send_c[k + 4, p] = pair_ref[p, rows_of(1 - c), :].astype(LOW)
            to_core(k + 4, p).start()
            return carry

        def finish(p, carry):
            mine = pair_ref[p, rows_of(c), :]
            to_core(k + 4, p).wait_recv()
            keep_y[k, p] = (mine + recv_c[k + 4, p].astype(FULL)).astype(LOW)
            return carry

        lax.fori_loop(0, 3, issue, 0)
        lax.fori_loop(0, 3, finish, 0)

    def out_product(k, core):
        rows = rows_of(target(k) * 2 + core)
        mine = jnp.concatenate([dy_t[j, y, rows, :] for j in range(4)], axis=1)
        theirs = jnp.concatenate([side_t[j, rows, :] for j in range(4)], axis=1)
        return dot(mine, mixed[...], 1, 0) + dot(theirs, mixed_y[...], 1, 0)

    def out_core(k):
        return remote(
            send_g.at[k], recv_g.at[k], sem_gs.at[k], sem_gr.at[k], {"dp": core_peer}
        )

    def out_issue(k, carry):
        send_g[k] = out_product(k, 1 - c).astype(LOW)
        out_core(k).start()
        return carry

    def out_finish(k, carry):
        mine = out_product(k, c)
        out_core(k).wait_recv()
        keep_y[k, 3] = (mine + recv_g[k].astype(FULL)).astype(LOW)
        return carry

    def here(k, p, with_y):
        if with_y:
            to_y(k, p).wait_recv()
            return keep_y[k, p].astype(FULL) + recv_y[k, p].astype(FULL)
        return keep_y[k, p].astype(FULL)

    def end(k, p, with_y=True):
        @pl.when((z == 0) | (z == 3))
        def _():
            t = target(k)
            send_z[k, p] = here(k, p, with_y).astype(LOW)

            @pl.when(t > z)
            def _():
                up(k, t, p).start()

            @pl.when(t < z)
            def _():
                down(k, t, p).start()

    def mid(k, p, with_y=True):
        @pl.when((z == 1) | (z == 2))
        def _():
            t = target(k)
            part = here(k, p, with_y)

            @pl.when(t > z)
            def _():
                pltpu.make_async_copy(from_low.at[t, p], from_low.at[t, p], sem_low.at[t, p]).wait()
                send_z[k, p] = (part + from_low[t, p].astype(FULL)).astype(LOW)
                up(k, t, p).start()

            @pl.when(t < z)
            def _():
                pltpu.make_async_copy(from_high.at[t, p], from_high.at[t, p], sem_high.at[t, p]).wait()
                send_z[k, p] = (part + from_high[t, p].astype(FULL)).astype(LOW)
                down(k, t, p).start()

    def ends(k):
        def piece(p, carry):
            end(k, p)
            return carry

        lax.fori_loop(0, 3, piece, 0)

    def mids(k):
        def piece(p, carry):
            mid(k, p)
            return carry

        lax.fori_loop(0, 3, piece, 0)

    send_s[...] = jnp.zeros_like(send_s)
    local_x.wait()
    local_gain.wait()
    local_win.wait()
    arrive(0)
    local_g.wait()
    local_moved.wait()
    local_seg.wait()
    relay(15)
    forward(0)
    relay(14)
    arrive(1)
    relay(13)
    forward(1)
    relay(12)
    arrive(2)
    relay(11)
    forward(2)
    relay(10)
    arrive(3)
    relay(9)
    forward(3)
    relay(8)
    local_wout.wait()
    backward(3)
    relay(7)
    backward(2)
    relay(6)
    relay(5)
    relay(4)
    relay(3)
    backward(1)
    relay(2)
    relay(1)
    relay(0)
    backward(0)

    away(0)

    def mixed_here(j, carry):
        share_mixed(j).wait_recv()
        return carry

    def operands_here(i, carry):
        share_turned(i // 4, i % 4).wait_recv()
        return carry

    keep(0)
    lax.fori_loop(0, 2, term_away, 0)
    away(1)
    lax.fori_loop(2, 4, term_away, 0)
    lax.fori_loop(0, 4, mixed_here, 0)
    lax.fori_loop(0, 8, operands_here, 0)
    lax.fori_loop(0, 4, out_issue, 0)
    lax.fori_loop(0, 4, out_finish, 0)
    for k in range(3):
        end(k, 3, False)
    keep(1)
    ends(0)
    away(2)
    mid(0, 3, False)
    mid(1, 3, False)
    keep(2)
    mid(2, 3, False)
    away(3)
    keep(3)
    ends(1)
    mid(0, 0)
    lax.fori_loop(0, 4, term_kept, 0)
    send_n[...] = send_s[...].T[:8]
    cross_s.start()
    mid(0, 1)
    mid(0, 2)

    def interior(p, carry):
        mid(1, p)
        mid(2, p)
        return carry

    lax.fori_loop(0, 3, interior, 0)
    ends(2)
    cross_s.wait()
    land_s[...] = jnp.concatenate([land_n[...]] * 16, axis=0).T
    lax.fori_loop(0, 4, gradient, 0)

    total = gm_ref

    def gather_total(p, with_y):
        if with_y:
            to_y(3, p).wait_recv()
            total[...] = keep_y[3, p].astype(FULL) + recv_y[3, p].astype(FULL)
        else:
            total[...] = keep_y[3, p].astype(FULL)

        @pl.when(z > 0)
        def _():
            pltpu.make_async_copy(from_low.at[z, p], from_low.at[z, p], sem_low.at[z, p]).wait()
            total[...] += from_low[z, p].astype(FULL)

        @pl.when(z < 3)
        def _():
            pltpu.make_async_copy(from_high.at[z, p], from_high.at[z, p], sem_high.at[z, p]).wait()
            total[...] += from_high[z, p].astype(FULL)

    def store_in(p):
        cols = pl.ds(p * PIECE, PIECE)
        return pltpu.make_async_copy(gin_ref.at[:, cols], gin_hbm.at[:, cols], sem_out.at[4 + p])

    store_out = pltpu.make_async_copy(gout_ref, gout_hbm, sem_out.at[7])

    gather_total(3, False)
    gout_ref[...] = total[...].T
    store_out.start()
    for p in range(3):
        gather_total(p, True)
        gin_ref[:, p * PIECE : (p + 1) * PIECE] = total[...]
        store_in(p).start()

    def drain_swap(i, carry):
        swap(i).wait_send()
        share_dy(i).wait_send()
        return carry

    lax.fori_loop(0, 16, drain_swap, 0)

    def drain_share(j, carry):
        share_x(j).wait_send()
        out_core(j).wait_send()
        share_mixed(j).wait_send()
        store_grad(j).wait()
        for side in range(2):
            share_turned(side, j).wait_send()
        return carry

    lax.fori_loop(0, 4, drain_share, 0)

    def drain_core(i, carry):
        to_core(i // 3, i % 3).wait_send()
        return carry

    lax.fori_loop(0, 24, drain_core, 0)

    def drain_far(i, carry):
        k, p = i // 4, i % 4
        t = target(k)

        @pl.when(p < 3)
        def _():
            to_y(k, p).wait_send()

        @pl.when(t > z)
        def _():
            up(k, t, p).wait_send()

        @pl.when(t < z)
        def _():
            down(k, t, p).wait_send()

        return carry

    lax.fori_loop(0, 16, drain_far, 0)
    for p in range(3):
        store_in(p).wait()
    store_out.wait()


def finish_kernel(grad, gin, gout, grad_out, gin_out, gout_out, b_grad, b_gin, b_gout, sems):
    steps = []
    for source, staged, result, parts in (
        (grad, b_grad, grad_out, 4), (gin, b_gin, gin_out, 2), (gout, b_gout, gout_out, 1),
    ):
        size = source.shape[0] // parts
        for i in range(parts):
            at = pl.ds(i * size, size)
            n = len(steps)
            steps.append((
                pltpu.make_async_copy(source.at[at], staged.at[at], sems.at[0, n]),
                pltpu.make_async_copy(staged.at[at], result.at[at], sems.at[1, n]),
            ))
    for fetch, _ in steps:
        fetch.start()
    for fetch, store in steps:
        fetch.wait()
        store.start()
    for _, store in steps:
        store.wait()


def finished(*arrays):
    anywhere = pl.BlockSpec(memory_space=pl.ANY)
    return pl.pallas_call(
        finish_kernel,
        out_shape=tuple(jax.ShapeDtypeStruct(a.shape, a.dtype) for a in arrays),
        in_specs=[anywhere] * len(arrays),
        out_specs=[anywhere] * len(arrays),
        scratch_shapes=[pltpu.VMEM(a.shape, a.dtype) for a in arrays]
        + [pltpu.SemaphoreType.DMA((2, 7))],
    )(*arrays)


def fused(inputs, grad_moved, moved, segments, gain, proj_in, proj_out):
    rows, half = inputs.shape
    wide, narrow = proj_in.shape[1], proj_out.shape[0]
    heads = wide // SPAN
    vmem, dma = pltpu.VMEM, pltpu.SemaphoreType.DMA
    anywhere = pl.BlockSpec(memory_space=pl.ANY)
    pieces = vmem((4, 4, 128, PIECE), LOW)
    thirds = vmem((4, 3, 128, PIECE), LOW)
    widths = [(j + 1) * BLOCK for j in range(rows // BLOCK)]
    gin, gout, grad = pl.pallas_call(
        fused_kernel,
        out_shape=(
            jax.ShapeDtypeStruct((128, wide), FULL),
            jax.ShapeDtypeStruct((narrow, 128), FULL),
            jax.ShapeDtypeStruct((rows, half), LOW),
        ),
        in_specs=[anywhere] * 7,
        out_specs=[anywhere] * 3,
        scratch_shapes=[
            vmem((2, rows, half), LOW),
            vmem((rows, half), LOW),
            vmem((rows, half), LOW),
            vmem((2, rows, half), LOW),
            vmem(proj_in.shape, LOW),
            vmem(proj_out.shape, LOW),
            vmem((2 * half, rows), LOW),
            vmem((4, 2, half, BLOCK), LOW),
            vmem((rows, wide), LOW),
            vmem((rows, narrow), LOW),
            vmem((rows, wide), FULL),
            vmem((heads, rows, DV), LOW),
            vmem((heads, rows, DV), LOW),
            vmem((heads, rows, DQK), LOW),
            vmem((heads, rows, DQK), LOW),
        ]
        + [vmem((heads, BLOCK, w), LOW) for w in widths]
        + [vmem((heads, BLOCK, w), FULL) for w in widths]
        + [
            vmem((rows, narrow), FULL),
            vmem((heads, rows, 1), FULL),
            vmem((BLOCK, narrow), FULL),
            vmem((heads, rows - BLOCK, DV), FULL),
            vmem((heads, rows - BLOCK, DQK), FULL),
            vmem((rows, 1), FULL),
            vmem((rows, 1), FULL),
            vmem((4, rows, half // 4), LOW),
            vmem((4, rows, half // 4), LOW),
            vmem((4, rows, half // 4), LOW),
            vmem((rows, 128), FULL),
            vmem((rows, 128), FULL),
            vmem((4, half, BLOCK), LOW),
            vmem((rows, narrow), LOW),
            vmem((8, 3, 128, PIECE), LOW),
            vmem((8, 3, 128, PIECE), LOW),
            vmem((4, 128, PIECE), LOW),
            vmem((4, 128, PIECE), LOW),
            thirds, pieces, thirds, pieces, pieces, pieces,
            vmem((8, rows), FULL),
            vmem((8, rows), FULL),
            vmem((3, 256, PIECE), FULL),
            pltpu.SMEM(moved.shape, jnp.int32),
            vmem((1, rows), jnp.int32),
            vmem((1, 2 * half), FULL),
            vmem((128, wide), FULL),
            vmem((narrow, 128), FULL),
            vmem((4, rows, half // 4), LOW),
            dma((7,)), dma((16,)), dma((16,)), dma((4,)), dma((4,)), dma((16,)), dma((16,)),
            dma((5,)), dma((5,)), dma((4,)), dma((4,)), dma((2, 4)), dma((2, 4)), dma((8, 3)), dma((8, 3)),
            dma((4,)), dma((4,)), dma((4, 3)), dma((4, 3)), dma((4, 4)), dma((4, 4)), dma((4, 4)),
            dma((8,)),
        ],
        compiler_params=pltpu.CompilerParams(
            collective_id=0, has_side_effects=True, vmem_limit_bytes=62 * 1024 * 1024
        ),
    )(inputs, grad_moved, moved, segments[None, :], gain[None, :], proj_in, proj_out)
    return finished(grad, gin, gout)


def on_device(inputs, grad_moved, moved, segments, input_norm_gain, proj_in, proj_out):
    rows = inputs.shape[0]
    span = 2 * DV + 2 * DQK
    heads_here = proj_in.shape[1] // span
    if lax.axis_size("mp") == 2 and lax.axis_size("dp") == 16:
        return fused(inputs, grad_moved, moved, segments, input_norm_gain, proj_in, proj_out)
    top_bit = lax.axis_size("dp").bit_length() - 2
    blocks = rows // BLOCK
    mine = [grad_moved[j * BLOCK : (j + 1) * BLOCK] for j in range(blocks)]
    theirs = [swapped(block, "dp", top_bit) for block in mine]
    full_x = gathered(inputs)
    full_dy = jnp.concatenate(
        [gathered(jnp.where(moved[0, j] == 1, theirs[j], mine[j])) for j in range(blocks)], axis=0
    )
    xfull = full_x.astype(jnp.float32)
    mean_shifted = xfull - jnp.mean(xfull, axis=1, keepdims=True)
    inverse_deviation = lax.rsqrt(
        jnp.mean(mean_shifted * mean_shifted, axis=1, keepdims=True) + epsilon
    )
    standardized_input = mean_shifted * inverse_deviation
    normalized_rows = (standardized_input * input_norm_gain[None, :]).astype(jnp.bfloat16)
    pre = jnp.dot(normalized_rows, proj_in, preferred_element_type=jnp.float32)
    sig_p = jax.nn.sigmoid(pre)
    acts = (pre * sig_p).astype(jnp.bfloat16)
    grad_mix = lax.dot_general(
        full_dy, proj_out, (((1,), (1,)), ((), ())), preferred_element_type=jnp.float32
    )
    order = jnp.arange(rows, dtype=jnp.int32)
    visible = (
        (segments[:, None] == segments[None, :]) & (order[None, :] <= order[:, None])
    ).astype(jnp.float32)
    mixed, saved = forward_heads(acts, visible, heads_here)
    grad_act = backward_heads(saved, grad_mix, visible, heads_here)
    grad_pre = (grad_act * sig_p * (1.0 + pre * (1.0 - sig_p))).astype(jnp.bfloat16)
    local = inputs.shape[1]
    offset = lax.axis_index("mp") * local
    normed_term = lax.dot_general(
        grad_pre, proj_in, (((1,), (1,)), ((), ())), preferred_element_type=jnp.float32
    ).astype(jnp.bfloat16)
    term_scaled = normed_term.astype(jnp.float32) * input_norm_gain[None, :]
    sums = jnp.stack([jnp.sum(term_scaled, axis=1), jnp.sum(term_scaled * standardized_input, axis=1)])
    partial_out = lax.dot_general(
        mixed, full_dy, (((0,), (0,)), ((), ())), preferred_element_type=jnp.float32
    )
    grad_proj_out = lax.psum_scatter(
        partial_out.astype(jnp.bfloat16), "dp", scatter_dimension=1, tiled=True
    ).astype(jnp.float32)
    partial_in = lax.dot_general(
        normalized_rows, grad_pre, (((0,), (0,)), ((), ())), preferred_element_type=jnp.float32
    )
    grad_proj_in = lax.psum_scatter(
        partial_in.astype(jnp.bfloat16), "dp", scatter_dimension=0, tiled=True
    ).astype(jnp.float32)
    sums = lax.psum(sums, "mp")
    grad_normed = lax.psum_scatter(
        normed_term, "mp", scatter_dimension=1, tiled=True
    ).astype(jnp.float32)
    means = sums / standardized_input.shape[1]
    here = lambda array: lax.dynamic_slice_in_dim(array, offset, local, 1)
    grad_here = here(full_dy).astype(jnp.float32) + inverse_deviation * (
        grad_normed * here(input_norm_gain[None, :])
        - means[0][:, None]
        - here(standardized_input) * means[1][:, None]
    )
    input_gradient = grad_here.astype(jnp.bfloat16)
    return (input_gradient, grad_proj_in, grad_proj_out)


def solution(mesh):
    return jax.shard_map(
        on_device,
        mesh=mesh,
        in_specs=(
            P("dp", "mp"),
            P("dp", "mp"),
            P("dp", None),
            P("dp"),
            P(),
            P(None, "mp"),
            P("mp", None),
        ),
        out_specs=(P("dp", "mp"), P("dp", "mp"), P("mp", "dp")),
        check_vma=False,
    )
```
